32 devices in a mesh: rep: 4 (over y, core), shard: 8 (over z, x).
Axes of the slice: x: 2, y: 2, z: 4, core: 2. Of those that a mesh axis runs over, the one named last changes fastest.
Arguments:
- hidden: bfloat16 [6144, 1280], P(('rep', 'shard')), may hold values from -6 to 6
- out_grad: bfloat16 [6144, 1280], P(('rep', 'shard')), may hold values from -6 to 6
- clip_lengths: int32 [4], P('rep'), may hold values from 768 to 1536, as said below
- adapter_index: int32 [4], P('rep'), may hold values from 0 to 7
- w_query: bfloat16 [1280, 1280], P('shard'), may hold values from -0.15625 to 0.15625
- w_key: bfloat16 [1280, 1280], P('shard'), may hold values from -0.15625 to 0.15625
- w_value: bfloat16 [1280, 1280], P('shard'), may hold values from -0.15625 to 0.15625
- w_output: bfloat16 [1280, 1280], P('shard'), may hold values from -3 to 3
- w_up: bfloat16 [1280, 5120], P('shard'), may hold values from -0.15625 to 0.15625
- w_down: bfloat16 [5120, 1280], P('shard'), may hold values from -0.078125 to 0.078125
- a_query: bfloat16 [8, 1280, 16], P(None, 'shard'), may hold values from -0.15625 to 0.15625
- b_query: bfloat16 [8, 16, 1280], P(None, None, 'shard'), may hold values from -0.75 to 0.75
- a_key: bfloat16 [8, 1280, 16], P(None, 'shard'), may hold values from -0.15625 to 0.15625
- b_key: bfloat16 [8, 16, 1280], P(None, None, 'shard'), may hold values from -0.75 to 0.75
- a_value: bfloat16 [8, 1280, 16], P(None, 'shard'), may hold values from -0.15625 to 0.15625
- b_value: bfloat16 [8, 16, 1280], P(None, None, 'shard'), may hold values from -0.75 to 0.75
- a_output: bfloat16 [8, 1280, 16], P(None, 'shard'), may hold values from -3 to 3
- b_output: bfloat16 [8, 16, 1280], P(None, None, 'shard'), may hold values from -0.75 to 0.75
- a_up: bfloat16 [8, 1280, 16], P(None, 'shard'), may hold values from -0.15625 to 0.15625
- b_up: bfloat16 [8, 16, 5120], P(None, None, 'shard'), may hold values from -0.75 to 0.75
- a_down: bfloat16 [8, 5120, 16], P(None, 'shard'), may hold values from -0.078125 to 0.078125
- b_down: bfloat16 [8, 16, 1280], P(None, None, 'shard'), may hold values from -0.75 to 0.75
Outputs:
- layer_out: bfloat16 [6144, 1280], P(('rep', 'shard'))
- input_grad: bfloat16 [6144, 1280], P(('rep', 'shard'))
- grad_a_query: float32 [8, 1280, 16], P(None, 'shard')
- grad_b_query: float32 [8, 16, 1280], P(None, None, 'shard')
- grad_a_key: float32 [8, 1280, 16], P(None, 'shard')
- grad_b_key: float32 [8, 16, 1280], P(None, None, 'shard')
- grad_a_value: float32 [8, 1280, 16], P(None, 'shard')
- grad_b_value: float32 [8, 16, 1280], P(None, None, 'shard')
- grad_a_output: float32 [8, 1280, 16], P(None, 'shard')
- grad_b_output: float32 [8, 16, 1280], P(None, None, 'shard')
- grad_a_up: float32 [8, 1280, 16], P(None, 'shard')
- grad_b_up: float32 [8, 16, 5120], P(None, None, 'shard')
- grad_a_down: float32 [8, 5120, 16], P(None, 'shard')
- grad_b_down: float32 [8, 16, 1280], P(None, None, 'shard')
The draws below stay inside these ranges and needn't reach their ends.
Inputs may be any that keep to these rules, and one draw needn't show every extreme that they name: `clip_lengths`: slots of a clip at positions of its length or more are padding; some clip has length exactly 1536.
All inputs are finite; a program needn't handle non-finite values.
Results may differ from the reference program's by a relative error of at most 0.02.
Values may be sent and summed in bfloat16 or wider, within the bound.
No kernel may reach another device: no remote copies, remote signals or barrier semaphores. Data moves between devices by JAX's collectives and lax.ppermute only.
A program may use at most 256 MiB of HBM per device.

```python
import jax
import jax.numpy as jnp
from jax import lax

D = 1280
FF = 5120
HEADS = 16
HEAD = 80
RANK = 16
SETS = 8
LEN = 1536
CLIPS = 4
TOKENS = 6144


def draw_clip_lengths(key, part):
    key_values, key_pick = jax.random.split(key)
    values = jax.random.randint(key_values, (CLIPS,), LEN // 2, LEN + 1)
    chosen = jax.random.randint(key_pick, (), 0, CLIPS)
    return jnp.where(jnp.arange(CLIPS) == chosen, LEN, values).astype(jnp.int32)


def touch_ends(drawn, key, low, largest):
    extent = drawn.shape
    place = [jax.random.randint(jax.random.fold_in(key, axis), (), 0, extent[axis]) for axis in range(len(extent))]
    drawn = drawn.at[tuple(place)].set(low)
    longest = extent.index(max(extent))
    place[longest] = (place[longest] + 1) % extent[longest]
    return drawn.at[tuple(place)].set(largest)


def steps_of(key, dims, pieces, least, high):
    def one(dim, blocks):
        steps = jax.random.uniform(jax.random.fold_in(jax.random.fold_in(key, 6), dim), (blocks,), jnp.float32, least / len(pieces), high / len(pieces))
        return jnp.repeat(jnp.exp(steps), dims[dim] // blocks).reshape((-1,) + (1,) * (len(dims) - dim - 1))

    gain = one(*pieces[0])
    for cut in pieces[1:]:
        gain = gain * one(*cut)
    return gain


def gaussian(key, shape, width, limit, cuts=(), kind=jnp.bfloat16):
    values = width * jax.random.normal(key, shape, jnp.float32)
    if cuts:
        values = values * steps_of(key, shape, cuts, -0.22, 0.18)
    return jnp.clip(values, -limit, limit).astype(kind)


def setup_inputs(seed: int = 0) -> dict:
    key_of = jax.random.split(jax.random.key(seed), 23)
    hidden = gaussian(key_of[0], (TOKENS, D), 1.0, 6.0, ((0, 32),))
    out_grad = gaussian(key_of[1], (TOKENS, D), 1.0, 6.0, ((0, 32),))
    clip_lengths = draw_clip_lengths(jax.random.fold_in(key_of[22], 71), 0)
    adapter_index = touch_ends(jax.random.randint(key_of[3], (CLIPS,), 0, SETS), jax.random.fold_in(key_of[3], 1), 0, SETS - 1).astype(jnp.int32)
    w_query = gaussian(key_of[4], (D, D), D ** -0.5, 0.15625, ((0, 8),))
    w_key = gaussian(key_of[5], (D, D), D ** -0.5, 0.15625, ((0, 8),))
    w_value = gaussian(key_of[6], (D, D), D ** -0.5, 0.15625, ((0, 8),))
    w_output = gaussian(key_of[7], (D, D), (max(1, D * 5 // LEN)) ** -0.5, 3.0, ((0, 8),))
    w_up = gaussian(key_of[8], (D, FF), D ** -0.5, 0.15625, ((0, 8),))
    w_down = gaussian(key_of[9], (FF, D), FF ** -0.5, 0.078125, ((0, 8),))
    a_query = gaussian(key_of[10], (SETS, D, RANK), D ** -0.5, 0.15625, ((1, 8),))
    b_query = gaussian(key_of[11], (SETS, RANK, D), (4 * RANK) ** -0.5, 0.75, ((2, 8),))
    a_key = gaussian(key_of[12], (SETS, D, RANK), D ** -0.5, 0.15625, ((1, 8),))
    b_key = gaussian(key_of[13], (SETS, RANK, D), (4 * RANK) ** -0.5, 0.75, ((2, 8),))
    a_value = gaussian(key_of[14], (SETS, D, RANK), D ** -0.5, 0.15625, ((1, 8),))
    b_value = gaussian(key_of[15], (SETS, RANK, D), (4 * RANK) ** -0.5, 0.75, ((2, 8),))
    a_output = gaussian(key_of[16], (SETS, D, RANK), (max(1, D * 5 // LEN)) ** -0.5, 3.0, ((1, 8),))
    b_output = gaussian(key_of[17], (SETS, RANK, D), (4 * RANK) ** -0.5, 0.75, ((2, 8),))
    a_up = gaussian(key_of[18], (SETS, D, RANK), D ** -0.5, 0.15625, ((1, 8),))
    b_up = gaussian(key_of[19], (SETS, RANK, FF), (4 * RANK) ** -0.5, 0.75, ((2, 8),))
    a_down = gaussian(key_of[20], (SETS, FF, RANK), FF ** -0.5, 0.078125, ((1, 8),))
    b_down = gaussian(key_of[21], (SETS, RANK, D), (4 * RANK) ** -0.5, 0.75, ((2, 8),))
    return {"hidden": hidden, "out_grad": out_grad, "clip_lengths": clip_lengths, "adapter_index": adapter_index, "w_query": w_query, "w_key": w_key, "w_value": w_value, "w_output": w_output, "w_up": w_up, "w_down": w_down, "a_query": a_query, "b_query": b_query, "a_key": a_key, "b_key": b_key, "a_value": a_value, "b_value": b_value, "a_output": a_output, "b_output": b_output, "a_up": a_up, "b_up": b_up, "a_down": a_down, "b_down": b_down}


HIGHEST_PRECISION = lax.Precision.HIGHEST
EPSILON = 1e-05
NEGATIVE = -1e+30

@jax.custom_vjp
def low(v):
    return lax.optimization_barrier(v.astype(jnp.bfloat16)).astype(jnp.float32)

@jax.custom_vjp
def low_back(v):
    return v

def low_keep(v):
    return (low(v), None)

def low_pass(kept, grad):
    return (grad,)

def back_keep(v):
    return (v, None)

def back_low(kept, grad):
    return (low(grad),)
low.defvjp(low_keep, low_pass)
low_back.defvjp(back_keep, back_low)

def matmul(left, right):
    return jnp.dot(left, right, precision=HIGHEST_PRECISION, preferred_element_type=jnp.float32)

def norm_rows(values):
    center = values - lax.optimization_barrier(jnp.mean(values, axis=-1, keepdims=True))
    spread = lax.optimization_barrier(jnp.mean(center * center, axis=-1, keepdims=True))
    return center * lax.rsqrt(spread + EPSILON)

def project(inputs, weight, enter, leave):
    inner = low(low_back(matmul(inputs, enter)))
    return matmul(inputs, weight) + matmul(inner, leave)

def clip_forward(frozen, clip_rows, picked, length):
    w_query, w_key, w_value, w_output, w_up, w_down = frozen
    enter_q, leave_q, enter_k, leave_k, enter_v, leave_v, enter_o, leave_o, enter_u, leave_u, enter_d, leave_d = picked
    score_scale = HEAD ** (-0.5)
    first = low(norm_rows(clip_rows))
    queries = low(low_back(project(first, w_query, enter_q, leave_q)))
    key_rows = low(low_back(project(first, w_key, enter_k, leave_k)))
    values = low(low_back(project(first, w_value, enter_v, leave_v)))
    key_valid = jnp.arange(LEN) < length

    def one_head(head_parts):
        head_query, head_key, head_value = head_parts
        scores = low_back(matmul(head_query, head_key.T) * score_scale)
        scores = jnp.where(key_valid[None, :], scores, NEGATIVE)
        weights = jax.nn.softmax(scores, axis=-1)
        return matmul(low(weights), head_value)

    def to_heads(matrix):
        return matrix.reshape(LEN, HEADS, HEAD).transpose(1, 0, 2)
    context = lax.map(jax.checkpoint(one_head), (to_heads(queries), to_heads(key_rows), to_heads(values)))
    context = low(low_back(context.transpose(1, 0, 2).reshape(LEN, D)))
    middle = clip_rows + low_back(project(context, w_output, enter_o, leave_o))
    second = low(norm_rows(middle))
    pre_act = low_back(project(second, w_up, enter_u, leave_u))
    activated = low(jax.nn.gelu(pre_act, approximate=False))
    return middle + low_back(project(activated, w_down, enter_d, leave_d))

def reference(hidden, out_grad, clip_lengths, adapter_index, w_query, w_key, w_value, w_output, w_up, w_down, a_query, b_query, a_key, b_key, a_value, b_value, a_output, b_output, a_up, b_up, a_down, b_down):
    frozen = tuple((weight.astype(jnp.float32) for weight in (w_query, w_key, w_value, w_output, w_up, w_down)))
    adapters = tuple((tables.astype(jnp.float32) for tables in (a_query, b_query, a_key, b_key, a_value, b_value, a_output, b_output, a_up, b_up, a_down, b_down)))
    inputs = hidden.astype(jnp.float32).reshape(CLIPS, LEN, D)

    def whole_layer(layer_inputs, layer_adapters):

        def clip_step(carried, item):
            clip_rows, length, chosen = item
            picked = tuple((tables[chosen] for tables in layer_adapters))
            return (carried, clip_forward(frozen, clip_rows, picked, length))
        unused, outputs = lax.scan(jax.checkpoint(clip_step), None, (layer_inputs, clip_lengths, adapter_index))
        return outputs
    outputs, pullback = jax.vjp(whole_layer, inputs, adapters)
    grad_inputs, grads = pullback(out_grad.astype(jnp.float32).reshape(CLIPS, LEN, D))
    return (outputs.reshape(TOKENS, D).astype(jnp.bfloat16), grad_inputs.reshape(TOKENS, D).astype(jnp.bfloat16), grads[0], grads[1], grads[2], grads[3], grads[4], grads[5], grads[6], grads[7], grads[8], grads[9], grads[10], grads[11])
```

```python
from functools import partial

import jax
import jax.numpy as jnp
from jax import lax
from jax.experimental import pallas as pl
from jax.experimental.pallas import tpu as pltpu
from jax.sharding import PartitionSpec as P

D = 1280
FF = 5120
HEADS = 16
HEAD = 80
LANES = 128
RANK = 16
SETS = 8
GROUP = 4

EPSILON = 1e-05
NEGATIVE = -1e30
LOG2E = 1.4426950408889634
SCALE = HEAD ** (-0.5)
ONE_LANE = HEAD
MASK_LANE = HEAD + 1

BF = jnp.bfloat16
F32 = jnp.float32


def dot(left, right):
    return jnp.dot(left, right, preferred_element_type=F32)


def dot_nt(left, right):
    return lax.dot_general(left, right, (((1,), (1,)), ((), ())), preferred_element_type=F32)


def dot_tn(left, right):
    return lax.dot_general(left, right, (((0,), (0,)), ((), ())), preferred_element_type=F32)


def norm_parts(values):
    center = values - jnp.mean(values, axis=-1, keepdims=True)
    spread = jnp.mean(center * center, axis=-1, keepdims=True)
    inverse = lax.rsqrt(spread + EPSILON)
    return center * inverse, inverse


def norm_back(grad, normal, inverse):
    average = jnp.mean(grad, axis=-1, keepdims=True)
    along = jnp.mean(grad * normal, axis=-1, keepdims=True)
    return inverse * (grad - average - normal * along)


def forward_kernel(q_ref, k_ref, v_ref, ctx_ref, lse_ref):
    scores = dot_nt(q_ref[...], k_ref[...])
    factor = SCALE * LOG2E
    highest = jnp.max(scores, axis=1, keepdims=True)
    weights = jnp.exp2((scores - highest) * factor).astype(BF)
    portion = dot(weights, v_ref[...])
    total = portion[:, ONE_LANE : ONE_LANE + 1]
    ctx_ref[...] = (portion / total).astype(BF)
    lse_ref[0] = highest * factor + jnp.log2(total)


def attend(qkv, heads_here, block):
    seq_len = qkv.shape[0]
    lanes = heads_here * LANES
    return pl.pallas_call(
        forward_kernel,
        grid=(heads_here, seq_len // block),
        in_specs=[
            pl.BlockSpec((block, LANES), lambda h, i: (i, h)),
            pl.BlockSpec((seq_len, LANES), lambda h, i: (0, heads_here + h)),
            pl.BlockSpec((seq_len, LANES), lambda h, i: (0, 2 * heads_here + h)),
        ],
        out_specs=[
            pl.BlockSpec((block, LANES), lambda h, i: (i, h)),
            pl.BlockSpec((1, block, 1), lambda h, i: (h, i, 0)),
        ],
        out_shape=[
            jax.ShapeDtypeStruct((seq_len, lanes), BF),
            jax.ShapeDtypeStruct((heads_here, seq_len, 1), F32),
        ],
        compiler_params=pltpu.CompilerParams(vmem_limit_bytes=48 << 20),
        cost_estimate=pl.CostEstimate(
            flops=4 * lanes * seq_len * seq_len,
            transcendentals=heads_here * seq_len * seq_len,
            bytes_accessed=8 * seq_len * lanes,
        ),
        name="attention_forward",
    )(qkv, qkv, qkv)


def backward_kernel(q_ref, k_ref, v_ref, do_ref, lse_ref, delta_ref, dq_ref, dk_ref, dv_ref, dq_acc):
    step = pl.program_id(1)
    queries = q_ref[...]
    keys = k_ref[...]
    douts = do_ref[...]
    scores = dot_nt(keys, queries)
    weights = jnp.exp2(scores * (SCALE * LOG2E) - lse_ref[0])
    grad_weights = dot_nt(v_ref[...], douts)
    grad_scores = (weights * (grad_weights - delta_ref[0])).astype(BF)
    dv_ref[...] = dot(weights.astype(BF), douts).astype(BF)
    dk_ref[...] = (dot(grad_scores, queries) * SCALE).astype(BF)
    part = dot_tn(grad_scores, keys)

    @pl.when(step == 0)
    def _():
        dq_acc[...] = part

    @pl.when(step > 0)
    def _():
        dq_acc[...] += part

    @pl.when(step == pl.num_programs(1) - 1)
    def _():
        dq_ref[...] = (dq_acc[...] * SCALE).astype(BF)


def attend_back(qkv, douts, lse, delta, heads_here, block):
    seq_len = qkv.shape[0]
    lanes = heads_here * LANES
    full = jax.ShapeDtypeStruct((seq_len, lanes), BF)
    return pl.pallas_call(
        backward_kernel,
        grid=(heads_here, seq_len // block),
        in_specs=[
            pl.BlockSpec((seq_len, LANES), lambda h, i: (0, h)),
            pl.BlockSpec((block, LANES), lambda h, i: (i, heads_here + h)),
            pl.BlockSpec((block, LANES), lambda h, i: (i, 2 * heads_here + h)),
            pl.BlockSpec((seq_len, LANES), lambda h, i: (0, h)),
            pl.BlockSpec((1, 1, seq_len), lambda h, i: (h, 0, 0)),
            pl.BlockSpec((1, 1, seq_len), lambda h, i: (h, 0, 0)),
        ],
        out_specs=[
            pl.BlockSpec((seq_len, LANES), lambda h, i: (0, h)),
            pl.BlockSpec((block, LANES), lambda h, i: (i, h)),
            pl.BlockSpec((block, LANES), lambda h, i: (i, h)),
        ],
        out_shape=[full, full, full],
        scratch_shapes=[pltpu.VMEM((seq_len, LANES), F32)],
        compiler_params=pltpu.CompilerParams(vmem_limit_bytes=48 << 20),
        cost_estimate=pl.CostEstimate(
            flops=10 * lanes * seq_len * seq_len,
            transcendentals=heads_here * seq_len * seq_len,
            bytes_accessed=16 * seq_len * lanes,
        ),
        name="attention_backward",
    )(qkv, qkv, qkv, douts, lse, delta)


def body(
    hidden,
    out_grad,
    clip_lengths,
    adapter_index,
    w_query,
    w_key,
    w_value,
    w_output,
    w_up,
    w_down,
    a_query,
    b_query,
    a_key,
    b_key,
    a_value,
    b_value,
    a_output,
    b_output,
    a_up,
    b_up,
    a_down,
    b_down,
):
    shards = lax.axis_size("shard")
    reps = lax.axis_size("rep")
    rows = hidden.shape[0]
    seq_len = rows * shards
    wide = D // shards
    heads_here = HEADS // shards
    lanes_here = heads_here * LANES
    ff_wide = FF // shards
    quarter = ff_wide // GROUP
    shard = lax.axis_index("shard")
    rep = lax.axis_index("rep")
    part = rep % GROUP
    length = clip_lengths[0]
    chosen = adapter_index[0]

    def mate(value, flip):
        return lax.ppermute(value, "rep", [(i, i ^ flip) for i in range(reps)])

    def pick(tables):
        return lax.dynamic_index_in_dim(tables, chosen, 0, keepdims=False)

    sets = [adapter_index] + [mate(adapter_index, flip) for flip in range(1, GROUP)]

    hidden_all = lax.all_gather(hidden, "shard", axis=0, tiled=True)
    stacked = jnp.stack((w_query, w_key, w_value), axis=1).reshape(wide, 3, shards, wide)
    qkv_cols = lax.all_to_all(
        jnp.transpose(stacked, (2, 0, 1, 3)), "shard", split_axis=0, concat_axis=0, tiled=True
    )
    qkv_cols = qkv_cols.reshape(D, 3 * heads_here, HEAD)
    qkv_cols = jnp.pad(qkv_cols, ((0, 0), (0, 0), (0, LANES - HEAD))).reshape(D, 3 * lanes_here)

    enter_pack = jnp.concatenate([pick(t) for t in (a_query, a_key, a_value, a_output, a_up)], axis=1)
    enters = lax.all_gather(enter_pack, "shard", axis=0, tiled=True)
    leave_pack = jnp.concatenate([pick(t) for t in (b_query, b_key, b_value, b_output, b_down)], axis=0)
    leaves = lax.all_gather(leave_pack, "shard", axis=1, tiled=True)
    enter_qkv = enters[:, : 3 * RANK]
    enter_o = enters[:, 3 * RANK : 4 * RANK]
    enter_u = enters[:, 4 * RANK :]
    leave_q, leave_k, leave_v, leave_o, leave_d = [leaves[i * RANK : (i + 1) * RANK] for i in range(5)]

    up_cols = lax.dynamic_index_in_dim(
        w_up.reshape(wide, shards, GROUP, quarter), part, 2, keepdims=False
    ).reshape(wide, shards * quarter)
    up_weight = lax.all_gather(up_cols, "shard", axis=0, tiled=True)
    down_rows = lax.dynamic_slice_in_dim(w_down, part * quarter, quarter, 0)
    down_weight = lax.all_gather(down_rows, "shard", axis=0, tiled=True)
    enter_d_rows = lax.dynamic_slice_in_dim(a_down, part * quarter, quarter, 1)
    leave_u_cols = lax.dynamic_slice_in_dim(b_up, part * quarter, quarter, 2)
    enter_d_pack = jnp.concatenate(
        [lax.dynamic_index_in_dim(enter_d_rows, s[0], 0, keepdims=False) for s in sets], axis=1
    )
    leave_u_pack = jnp.concatenate(
        [lax.dynamic_index_in_dim(leave_u_cols, s[0], 0, keepdims=False) for s in sets], axis=0
    )
    enter_d_all = lax.all_gather(enter_d_pack, "shard", axis=0, tiled=True)
    leave_u_all = lax.all_gather(leave_u_pack, "shard", axis=1, tiled=True)
    output_weight = lax.all_gather(w_output, "shard", axis=0, tiled=True)
    qkv_weight = lax.all_gather(
        jnp.concatenate((w_query, w_key, w_value), axis=1), "shard", axis=0, tiled=True
    )

    gi_down = dot_nt(out_grad, leave_d).astype(BF)

    def group_gather(value):
        other = mate(value, 2)
        return [value, mate(value, 1), other, mate(other, 1)]

    grads_out = group_gather(out_grad)
    gis_down = group_gather(gi_down)

    inputs_all = hidden_all.astype(F32)
    first_all = norm_parts(inputs_all)[0].astype(BF)
    inner_qkv = dot(first_all, enter_qkv).astype(BF)

    def head_lanes(matrix):
        cut = matrix.reshape(matrix.shape[0], heads_here, HEAD)
        return jnp.pad(cut, ((0, 0), (0, 0), (0, LANES - HEAD))).reshape(matrix.shape[0], lanes_here)

    zero = jnp.zeros((RANK, lanes_here), BF)
    leave_block = jnp.concatenate(
        [
            jnp.concatenate([head_lanes(pick(t)) if i == j else zero for j in range(3)], axis=1)
            for i, t in enumerate((b_query, b_key, b_value))
        ],
        axis=0,
    )
    lane = lax.broadcasted_iota(jnp.int32, (1, 3 * lanes_here), 1)
    kind = lane // lanes_here
    inside = lane % LANES
    ones = jnp.where((kind == 2) & (inside == ONE_LANE) | (kind == 0) & (inside == MASK_LANE), 1.0, 0.0)
    bias = jnp.where(jnp.arange(seq_len)[:, None] < length, 0.0, NEGATIVE)
    extra = ones + jnp.where((kind == 1) & (inside == MASK_LANE), bias, 0.0)
    qkv = (dot(first_all, qkv_cols) + dot(inner_qkv, leave_block) + extra).astype(BF)
    ctx_heads, lse = attend(qkv, heads_here, 256)

    def drop_lanes(matrix):
        return matrix.reshape(seq_len, heads_here, LANES)[:, :, :HEAD].reshape(shards, rows, wide)

    def to_tokens(matrix):
        moved = lax.all_to_all(drop_lanes(matrix), "shard", split_axis=0, concat_axis=0, tiled=True)
        return jnp.transpose(moved, (1, 0, 2)).reshape(rows, D)

    context = to_tokens(ctx_heads)

    inputs = hidden.astype(F32)
    first, first_inverse = norm_parts(inputs)
    inner_o = dot(context, enter_o).astype(BF)
    middle = inputs + dot(context, output_weight) + dot(inner_o, leave_o)
    second, second_inverse = norm_parts(middle)
    second_b = second.astype(BF)
    inner_u = dot(second_b, enter_u).astype(BF)

    seconds = group_gather(second_b)
    inners_u = group_gather(inner_u)
    leave_us = [leave_u_all[i * RANK : (i + 1) * RANK] for i in range(GROUP)]
    enter_ds = [enter_d_all[:, i * RANK : (i + 1) * RANK] for i in range(GROUP)]

    def join(pieces):
        return jnp.concatenate(pieces, axis=0)

    def cut(matrix):
        return [matrix[i * rows : (i + 1) * rows] for i in range(GROUP)]

    pre_act = dot(join(seconds), up_weight) + join([dot(i, l) for i, l in zip(inners_u, leave_us)])
    cumulative = 0.5 * (1.0 + lax.erf(pre_act * (0.5**0.5)))
    density = jnp.exp(-0.5 * pre_act * pre_act) * (0.5 / jnp.pi) ** 0.5
    activated = (pre_act * cumulative).astype(BF)
    acts = cut(activated)
    mlp_parts = cut(dot(activated, down_weight).astype(BF))
    down_parts = [dot(a, e).astype(BF) for a, e in zip(acts, enter_ds)]
    grad_act = dot_nt(join(grads_out), down_weight) + join(
        [dot_nt(g, e) for g, e in zip(gis_down, enter_ds)]
    )
    grad_pre = (grad_act * (cumulative + pre_act * density)).astype(BF)
    grad_pres = cut(grad_pre)
    h2_parts = cut(dot_nt(grad_pre, up_weight).astype(BF))
    gi_up_parts = [dot_nt(g, l).astype(BF) for g, l in zip(grad_pres, leave_us)]
    ga_down = [dot_tn(a, g) for a, g in zip(acts, gis_down)]
    gb_up = [dot_tn(g, i) for g, i in zip(grad_pres, inners_u)]

    def group_reduce(pieces):
        near = pieces[0].astype(F32) + mate(pieces[1], 1).astype(F32)
        far = (pieces[2].astype(F32) + mate(pieces[3], 1).astype(F32)).astype(BF)
        return near + mate(far, 2).astype(F32)

    inner_d = group_reduce(down_parts).astype(BF)
    mlp = group_reduce(mlp_parts) + dot(inner_d, leave_d)
    layer_out = (middle + mlp).astype(BF)
    gb_down = dot_tn(out_grad, inner_d)
    gi_up = group_reduce(gi_up_parts).astype(BF)
    grad_second = group_reduce(h2_parts) + dot_nt(gi_up, enter_u)
    ga_up = dot_tn(second_b, gi_up)
    grad_middle = out_grad.astype(F32) + norm_back(grad_second, second, second_inverse)
    grad_attn = grad_middle.astype(BF)
    gb_output = dot_tn(grad_attn, inner_o)
    gi_output = dot_nt(grad_attn, leave_o).astype(BF)
    ga_output = dot_tn(context, gi_output)
    grad_context = (dot_nt(grad_attn, output_weight) + dot_nt(gi_output, enter_o)).astype(BF)

    moved = jnp.transpose(grad_context.reshape(rows, shards, wide), (1, 0, 2))
    moved = lax.all_to_all(moved, "shard", split_axis=0, concat_axis=0, tiled=True)
    douts = head_lanes(moved.reshape(seq_len, wide))
    delta = jnp.sum(
        (douts.astype(F32) * ctx_heads.astype(F32)).reshape(seq_len, heads_here, LANES), axis=2
    )
    delta = jnp.transpose(delta)[:, None, :]
    grads = attend_back(qkv, douts, lse.reshape(heads_here, 1, seq_len), delta, heads_here, 256)
    gb_heads = [
        jnp.transpose(
            dot_tn(g, inner_qkv[:, i * RANK : (i + 1) * RANK]).reshape(heads_here, LANES, RANK)[:, :HEAD], (2, 0, 1)
        ).reshape(RANK, wide)
        for i, g in enumerate(grads)
    ]
    joined = jnp.concatenate([drop_lanes(g) for g in grads], axis=2)
    joined = lax.all_to_all(joined, "shard", split_axis=0, concat_axis=0, tiled=True)
    grad_qkv = jnp.transpose(joined.reshape(shards, rows, 3, wide), (1, 2, 0, 3)).reshape(rows, 3 * D)
    first_b = first.astype(BF)
    gis = [
        dot_nt(grad_qkv[:, i * D : (i + 1) * D], l).astype(BF)
        for i, l in enumerate((leave_q, leave_k, leave_v))
    ]
    gi_qkv = jnp.concatenate(gis, axis=1)
    ga_qkv = dot_tn(first_b, gi_qkv)
    grad_first = dot_nt(grad_qkv, qkv_weight) + dot_nt(gi_qkv, enter_qkv)
    input_grad = (grad_middle + norm_back(grad_first, first, first_inverse)).astype(BF)

    pieces = jnp.concatenate([ga_qkv, ga_output, ga_up, gb_output, gb_down] + ga_down + gb_up, axis=1)
    pieces = pieces.astype(BF).reshape(shards, wide, -1)
    pieces = lax.all_to_all(pieces, "shard", split_axis=0, concat_axis=0, tiled=True)
    pieces = jnp.sum(pieces.astype(F32), axis=0)
    heads_t = jnp.transpose(jnp.concatenate(gb_heads, axis=0))
    pieces = jnp.concatenate([pieces, heads_t], axis=1).astype(BF)
    gathered = lax.all_gather(pieces, "rep", axis=0, tiled=False).astype(F32)
    indices = lax.all_gather(adapter_index, "rep", axis=0, tiled=True)
    hot = (indices[:, None] == jnp.arange(SETS)[None, :]).astype(F32)

    def own(slot):
        return jnp.einsum(
            "cs,cir->sir", hot, gathered[:, :, slot * RANK : (slot + 1) * RANK], precision=lax.Precision.HIGHEST
        )

    def turned(matrix):
        return jnp.transpose(matrix, (0, 2, 1))

    def split(first_slot):
        outs = []
        for q in range(GROUP):
            total = 0.0
            for base in range(0, reps, GROUP):
                device = base + q
                for k in range(GROUP):
                    slot = first_slot + k
                    piece = gathered[device, :, slot * RANK : (slot + 1) * RANK]
                    total = total + hot[device ^ k][:, None, None] * piece[None]
            outs.append(total)
        return jnp.concatenate(outs, axis=1)

    return (
        layer_out,
        input_grad,
        own(0),
        turned(own(15)),
        own(1),
        turned(own(16)),
        own(2),
        turned(own(17)),
        own(3),
        turned(own(5)),
        own(4),
        turned(split(11)),
        split(7),
        turned(own(6)),
    )


def solution(mesh):
    rows = P("shard", None)
    enter = P(None, "shard", None)
    leave = P(None, None, "shard")
    tokens = P(("rep", "shard"), None)
    return jax.shard_map(
        body,
        mesh=mesh,
        in_specs=(tokens, tokens, P("rep"), P("rep")) + (rows,) * 6 + (enter, leave) * 6,
        out_specs=(tokens, tokens) + (enter, leave) * 6,
        check_vma=False,
    )
```

```python
import jax
import jax.numpy as jnp
from jax import lax
from jax.experimental import pallas as pl
from jax.experimental.pallas import tpu as pltpu
from jax.sharding import PartitionSpec as P

D = 1280
FF = 5120
HEADS = 16
HEAD = 80
LANES = 128
RANK = 16
SETS = 8
GROUP = 4
FOLD = 4
CHUNK = 256
TAIL = D + LANES
RATE = 1.15e9

EPSILON = 1e-05
NEGATIVE = -1e30
LOG2E = 1.4426950408889634
SCALE = HEAD ** (-0.5)
ONE_LANE = HEAD
MASK_LANE = HEAD + 1

BF = jnp.bfloat16
F32 = jnp.float32

QUARTER = D // GROUP
ENTER_QKV = 0
ENTER_O = 48
ENTER_U = 64
LEAVE_O = 80
LEAVE_D = 96
FIRST = 128
BESIDE = 512
BUNDLE = D + BESIDE

ENTER_D = 0
LEAVE_U = 64
LEAVE_QKV = 128
LATE = 256

SHARD, PART, LENGTH, CORE, RING = range(5)

VMEM = pl.BlockSpec(memory_space=pltpu.VMEM)
SMEM = pl.BlockSpec(memory_space=pltpu.SMEM)
ANY = pl.BlockSpec(memory_space=pl.ANY)


def dot(left, right):
    return jnp.dot(left, right, preferred_element_type=F32)


def dot_nt(left, right):
    return lax.dot_general(left, right, (((1,), (1,)), ((), ())), preferred_element_type=F32)


def dot_tn(left, right):
    return lax.dot_general(left, right, (((0,), (0,)), ((), ())), preferred_element_type=F32)


def norm_parts(values):
    center = values - jnp.mean(values, axis=-1, keepdims=True)
    spread = jnp.mean(center * center, axis=-1, keepdims=True)
    inverse = lax.rsqrt(spread + EPSILON)
    return center * inverse, inverse


def norm_back(grad, normal, inverse):
    average = jnp.mean(grad, axis=-1, keepdims=True)
    along = jnp.mean(grad * normal, axis=-1, keepdims=True)
    return inverse * (grad - average - normal * along)


def cost(micros):
    return pl.CostEstimate(flops=int(micros * RATE), transcendentals=0, bytes_accessed=0)


def call(kernel, name, outs, ins, specs, out_specs=None, scratch=(), micros=1.0, **rest):
    return pl.pallas_call(
        kernel,
        out_shape=outs,
        in_specs=specs,
        out_specs=[VMEM] * len(outs) if out_specs is None else out_specs,
        scratch_shapes=list(scratch),
        compiler_params=pltpu.CompilerParams(vmem_limit_bytes=56 << 20),
        cost_estimate=cost(micros),
        name=name,
        **rest,
    )(*ins)


def shape(*dims, dtype=BF):
    return jax.ShapeDtypeStruct(dims, dtype)


def padded(size):
    return -(-size // LANES) * LANES


def column_blocks(wq, wk, wv, shards):
    wide = D // shards
    pad = jnp.zeros((wide, padded(3 * wide) - 3 * wide), BF)
    for s in range(shards):
        at = slice(s * wide, (s + 1) * wide)
        yield s, jnp.concatenate([wq[:, at], wk[:, at], wv[:, at], pad], axis=1)


def pack_columns(meta, weights, after, shards):
    wide = D // shards
    slot = padded(3 * wide)
    count = shards // GROUP

    def kernel(meta, wq, wk, wv, after, cols, quarter):
        for s, block in column_blocks(wq, wk, wv, shards):
            cols[s] = jnp.where(meta[CORE] == 0, block[:, : slot // 2], block[:, slot // 2 :])

            @pl.when(meta[PART] == s // count)
            def _():
                quarter[:, s % count * slot : (s % count + 1) * slot] = block

    outs = [shape(shards, wide, slot // 2), shape(wide, count * slot)]
    return call(kernel, "pack_columns", outs, (meta, *weights, after), [SMEM] + [VMEM] * 3 + [ANY], micros=3)


def unit(size):
    row = lax.broadcasted_iota(jnp.int32, (size, size), 0)
    col = lax.broadcasted_iota(jnp.int32, (size, size), 1)
    return (row == col).astype(BF)


def pack_first(chosen, meta, hidden, w_output, narrow):
    rows = hidden.shape[0]
    wide = narrow[0].shape[2]

    def kernel(chosen, meta, hidden, w_output, *refs):
        out = refs[-1]
        eye = unit(wide)
        out[:, :D] = hidden[...]
        out[:, D:] = jnp.zeros((rows, BESIDE), BF)
        for i, ref in enumerate(refs[:-1]):
            out[:wide, D + i * RANK : D + (i + 1) * RANK] = dot_nt(eye, ref[...]).astype(BF)
        for p in range(GROUP):

            @pl.when(meta[PART] == p)
            def _():
                out[:wide, D + FIRST : D + FIRST + QUARTER] = w_output[:, p * QUARTER : (p + 1) * QUARTER]

    return pl.pallas_call(
        kernel,
        out_shape=shape(rows, BUNDLE),
        grid_spec=pltpu.PrefetchScalarGridSpec(
            num_scalar_prefetch=1,
            grid=(1,),
            in_specs=[SMEM, pl.BlockSpec((rows, D), lambda i, m: (0, 0)), pl.BlockSpec((wide, D), lambda i, m: (0, 0))]
            + [pl.BlockSpec((None, RANK, wide), lambda i, m: (m[0], 0, 0))] * len(narrow),
            out_specs=pl.BlockSpec((rows, BUNDLE), lambda i, m: (0, 0)),
        ),
        cost_estimate=cost(3),
        name="pack_first",
    )(chosen, meta, hidden, w_output, *narrow)


def feed_kernel(*refs, wide, shards):
    part = refs[GROUP][0]
    (w_up, w_down), maps, (out, rows_down, sem) = refs[GROUP + 1 : GROUP + 3], refs[GROUP + 3 : -4], refs[-3:]
    narrow, downs, ups = maps[:3], maps[3:7], maps[7:11]
    copy = pltpu.make_async_copy(w_down.at[part], rows_down, sem)
    copy.start()
    eye = unit(wide)
    beside = D
    for i, ref in enumerate(narrow):
        start = beside + LEAVE_QKV + i * RANK
        out[:, start : start + RANK] = dot_nt(eye, ref[...]).astype(BF)
    end = beside + LEAVE_QKV + 3 * RANK
    out[:, end:] = jnp.zeros((wide, D + LATE - end), BF)
    for p in range(GROUP):

        @pl.when(part == p)
        def _():
            at = slice(p * wide, (p + 1) * wide)
            for i, ref in enumerate(downs):
                start = beside + ENTER_D + i * RANK
                out[:, start : start + RANK] = dot_nt(eye, ref[:, at]).astype(BF)
            for i, ref in enumerate(ups):
                start = beside + LEAVE_U + i * RANK
                out[:, start : start + RANK] = dot_nt(eye, ref[:, at]).astype(BF)
            for s in range(shards):
                start = (s * GROUP + p) * wide
                out[:, s * wide : (s + 1) * wide] = w_up[:, start : start + wide]

    copy.wait()


def pack_feed(sets, part, w_up, w_down, narrow, a_down, b_up, after, shards):
    wide = D // shards
    ff_wide = GROUP * wide
    width = D + LATE

    def at(k):
        return lambda i, *m: (m[k][0], 0, 0)

    specs = (
        [pl.BlockSpec((wide, FF), lambda i, *m: (0, 0)), ANY]
        + [pl.BlockSpec((None, RANK, wide), at(0))] * 3
        + [pl.BlockSpec((None, RANK, ff_wide), at(k)) for k in range(GROUP)] * 2
        + [ANY]
    )

    def kernel(*refs):
        feed_kernel(*refs, wide=wide, shards=shards)

    return pl.pallas_call(
        kernel,
        out_shape=[shape(wide, width), shape(wide, D)],
        grid_spec=pltpu.PrefetchScalarGridSpec(
            num_scalar_prefetch=GROUP + 1,
            grid=(1,),
            in_specs=specs,
            out_specs=[pl.BlockSpec((wide, n), lambda i, *m: (0, 0)) for n in (width, D)],
            scratch_shapes=[pltpu.SemaphoreType.DMA],
        ),
        cost_estimate=cost(5),
        name="pack_feed",
    )(*sets, part, w_up, w_down.reshape(GROUP, wide, D), *narrow, *[a_down] * GROUP, *[b_up] * GROUP, after)


def ring_shard(place, shards):
    return jnp.where(place < shards // 2, 2 * place, 2 * (shards - 1 - place) + 1)


def ring_pieces(value, shards, between):
    places = [2 * i if i < shards // 2 else 2 * (shards - 1 - i) + 1 for i in range(shards)]
    onward = [(places[i], places[(i + 1) % shards]) for i in range(shards)]
    back = [(b, a) for a, b in onward]
    half = value.shape[0] // 2
    pieces = [(value, 0, 0)]
    below, above = value, value
    for k in range(1, shards // 2):
        below = lax.ppermute(below, "shard", onward)
        above = lax.ppermute(above, "shard", back)
        below, above = between(k, (below, above))
        pieces += [(below, -k, 0), (above, k, 0)]
    far = shards // 2
    pieces.append((lax.ppermute(below[:half], "shard", onward), far, 0))
    pieces.append((lax.ppermute(above[half:], "shard", back), far, half))
    return pieces


def piece_shard(meta, step, shards):
    return ring_shard((meta[RING] + step + shards) % shards, shards)


def place_pieces(meta, pieces, steps, target, sems):
    shards = target.shape[0]
    copies = []
    for i, (ref, (step, start)) in enumerate(zip(pieces, steps)):
        block = target.at[piece_shard(meta, step, shards), pl.ds(start, ref.shape[0])]
        copies.append(pltpu.make_async_copy(ref, block, sems.at[i]))
    for copy in copies:
        copy.start()
    for copy in copies:
        copy.wait()


def qkv_kernel(meta, w_mine, w_mate, *refs, shards, steps):
    count = len(steps)
    pieces, leaves = refs[:count], refs[count : count + 3]
    first_ref, qkv_ref, inner_ref, enter, quarter, hid, sems = refs[-7:]
    wide = D // shards
    heads_here = HEADS // shards
    slot = padded(3 * wide)
    side = meta[CORE]
    rows = hid.shape[1]
    place_pieces(meta, pieces, steps, hid, sems)
    for s in range(shards):
        enter[s * wide : (s + 1) * wide, :] = hid[s, :wide, D : D + FIRST]
        quarter[s * wide : (s + 1) * wide, :] = hid[s, :wide, D + FIRST : D + FIRST + QUARTER]
    lane = lax.broadcasted_iota(jnp.int32, (rows, LANES - HEAD), 1)
    spot = lax.broadcasted_iota(jnp.int32, (rows, LANES - HEAD), 0)

    def step(s, carry):
        at = pl.ds(pl.multiple_of(s * rows, 64), rows)
        first = norm_parts(hid[s, :, :D].astype(F32))[0].astype(BF)
        first_ref[at, :] = first
        inner = dot(first, enter[:, : 3 * RANK]).astype(BF)
        inner_ref[at, :] = inner
        y_mine = dot(first, w_mine[...].reshape(D, slot // 2))
        y_mate = dot(first, w_mate[...].reshape(D, slot // 2))
        lo = jnp.where(side == 0, y_mine, y_mate)
        hi = jnp.where(side == 0, y_mate, y_mine)
        y = jnp.concatenate([lo, hi], axis=1)
        hidden_key = jnp.where((spot + s * rows < meta[LENGTH]) | (lane != MASK_LANE - HEAD), 0.0, NEGATIVE)
        for kind in range(3):
            lanes = slice(kind * RANK, (kind + 1) * RANK)
            out = y[:, kind * wide : (kind + 1) * wide] + dot(inner[:, lanes], leaves[kind][...])
            if kind == 0:
                tail = jnp.where(lane == MASK_LANE - HEAD, 1.0, 0.0)
            elif kind == 1:
                tail = hidden_key
            else:
                tail = jnp.where(lane == ONE_LANE - HEAD, 1.0, 0.0)
            for h in range(heads_here):
                base = (kind * heads_here + h) * LANES
                head = jnp.concatenate([out[:, h * HEAD : (h + 1) * HEAD], tail], axis=1)
                qkv_ref[at, base : base + LANES] = head.astype(BF)
        return carry

    lax.fori_loop(0, shards, step, 0)


def project_qkv(meta, chosen, w_mine, w_mate, pieces, leaves):
    shards = len(pieces) - 1
    steps = [p[1:] for p in pieces]
    rows = pieces[0][0].shape[0]
    seq_len = rows * shards
    lanes = HEADS // shards * LANES
    wide = D // shards
    weight = pl.BlockSpec(w_mine.shape, lambda i, c: (0, 0, 0))
    outs = [
        shape(seq_len, D),
        shape(seq_len, 3 * lanes),
        shape(seq_len, 3 * RANK),
        shape(D, FIRST),
        shape(D, QUARTER),
    ]

    def kernel(chosen, *refs):
        qkv_kernel(*refs, shards=shards, steps=steps)

    return pl.pallas_call(
        kernel,
        out_shape=outs,
        grid_spec=pltpu.PrefetchScalarGridSpec(
            num_scalar_prefetch=1,
            grid=(1,),
            in_specs=[SMEM, weight, weight]
            + [ANY] * len(pieces)
            + [pl.BlockSpec((None, RANK, wide), lambda i, c: (c[0], 0, 0))] * 3,
            out_specs=[pl.BlockSpec(o.shape, lambda i, c: (0, 0)) for o in outs],
            scratch_shapes=[
                pltpu.VMEM((shards, rows, BUNDLE), BF),
                pltpu.SemaphoreType.DMA((len(pieces),)),
            ],
        ),
        compiler_params=pltpu.CompilerParams(vmem_limit_bytes=56 << 20),
        cost_estimate=cost(14),
        name="project_qkv",
    )(chosen, meta, w_mine, w_mate, *[p[0] for p in pieces], *leaves)


def forward_kernel(qkv_ref, *refs, heads_here, wide):
    packed_ref, ctx_ref, lse_ref = refs[-3:]
    rows = ctx_ref.shape[0]
    part = rows // FOLD
    at = pl.ds(pl.multiple_of(pl.program_id(0) * rows, 64), rows)
    factor = SCALE * LOG2E
    for h in range(heads_here):
        queries = qkv_ref[at, h * LANES : (h + 1) * LANES]
        keys = qkv_ref[:, (heads_here + h) * LANES : (heads_here + h + 1) * LANES]
        values = qkv_ref[:, (2 * heads_here + h) * LANES : (2 * heads_here + h + 1) * LANES]
        scores = dot_nt(queries, keys)
        highest = jnp.max(scores, axis=1, keepdims=True)
        weights = jnp.exp2((scores - highest) * factor).astype(BF)
        portion = dot(weights, values)
        total = portion[:, ONE_LANE : ONE_LANE + 1]
        context = (portion / total).astype(BF)
        ctx_ref[:, h * LANES : (h + 1) * LANES] = context
        lse_ref[h] = highest * factor + jnp.log2(total)
        for g in range(FOLD):
            start = g * wide + h * HEAD
            packed_ref[0, :, start : start + HEAD] = context[g * part : (g + 1) * part, :HEAD]


def attend(qkv, shards):
    seq_len = qkv.shape[0]
    rows = seq_len // shards
    heads_here = HEADS // shards
    lanes = heads_here * LANES
    wide = D // shards

    def kernel(*refs):
        forward_kernel(*refs, heads_here=heads_here, wide=wide)

    return call(
        kernel,
        "attention_forward",
        [
            shape(shards, rows // FOLD, FOLD * wide),
            shape(seq_len, lanes),
            shape(heads_here, seq_len, 1, dtype=F32),
        ],
        (qkv,),
        [pl.BlockSpec((seq_len, 3 * lanes), lambda d: (0, 0))],
        out_specs=[
            pl.BlockSpec((1, rows // FOLD, FOLD * wide), lambda d: (d, 0, 0)),
            pl.BlockSpec((rows, lanes), lambda d: (d, 0)),
            pl.BlockSpec((heads_here, rows, 1), lambda d: (0, d, 0)),
        ],
        micros=12,
        grid=(shards,),
    )


def backward_kernel(
    qkv_ref, moved_ref, ctx_ref, lse_ref, first, inner, leave_q, leave_k, leave_v, out_ref, heads_ref, douts, delta, acc,
    *, heads_here, wide, block
):
    shards = moved_ref.shape[0]
    seq_len = qkv_ref.shape[0]
    rows = seq_len // shards
    part = rows // FOLD
    slot = out_ref.shape[2]
    for d in range(shards):
        for g in range(FOLD):
            base = d * rows + g * part
            for h in range(heads_here):
                start = g * wide + h * HEAD
                piece = moved_ref[d, :, start : start + HEAD]
                douts[base : base + part, h * LANES : h * LANES + HEAD] = piece
    for h in range(heads_here):
        douts[:, h * LANES + HEAD : (h + 1) * LANES] = jnp.zeros((seq_len, LANES - HEAD), BF)
    ones = jnp.ones((8, LANES), F32)
    if slot > 3 * wide:
        out_ref[:, :, 3 * wide :] = jnp.zeros((shards, rows + RANK, slot - 3 * wide), BF)
    for h in range(heads_here):
        lanes = slice(h * LANES, (h + 1) * LANES)
        product = douts[:, lanes].astype(F32) * ctx_ref[:, lanes].astype(F32)
        delta[...] = lax.dot_general(
            ones, product, (((1,), (1,)), ((), ())), precision=lax.Precision.HIGHEST, preferred_element_type=F32
        )
        queries = qkv_ref[:, lanes]
        grads = douts[:, lanes]

        def step(i, carry):
            at = pl.ds(pl.multiple_of(i * block, block), block)
            keys = qkv_ref[at, (heads_here + h) * LANES : (heads_here + h + 1) * LANES]
            values = qkv_ref[at, (2 * heads_here + h) * LANES : (2 * heads_here + h + 1) * LANES]
            scores = dot_nt(keys, queries)
            weights = jnp.exp2(scores * (SCALE * LOG2E) - lse_ref[h])
            grad_weights = dot_nt(values, grads)
            grad_scores = (weights * (grad_weights - delta[0:1, :])).astype(BF)
            acc[2, at, :] = dot(weights.astype(BF), grads)
            acc[1, at, :] = dot(grad_scores, queries) * SCALE
            moved = dot_tn(grad_scores, keys)

            @pl.when(i == 0)
            def _():
                acc[0] = moved

            @pl.when(i > 0)
            def _():
                acc[0] += moved

            return carry

        lax.fori_loop(0, seq_len // block, step, 0)
        for kind in range(3):
            start = kind * wide + h * HEAD
            for d in range(shards):
                piece = acc[kind, d * rows : (d + 1) * rows, :HEAD]
                if kind == 0:
                    piece = piece * SCALE
                out_ref[d, :rows, start : start + HEAD] = piece.astype(BF)
    heads_ref[...] = jnp.zeros_like(heads_ref)
    parts = []
    for kind, leave in enumerate((leave_q, leave_k, leave_v)):
        grad = out_ref[:, :rows, kind * wide : (kind + 1) * wide].reshape(seq_len, wide)
        lanes = slice(kind * RANK, (kind + 1) * RANK)
        parts.append(dot_nt(grad, leave[...]))
        heads_ref[:, kind * wide : (kind + 1) * wide] = dot_tn(inner[:, lanes], grad).astype(BF)
    entered = dot_tn(jnp.concatenate(parts, axis=1).astype(BF), first[...]).astype(BF)
    for kind in range(3):
        for d in range(shards):
            piece = entered[kind * RANK : (kind + 1) * RANK, d * wide : (d + 1) * wide]
            out_ref[d, rows:, kind * wide : (kind + 1) * wide] = piece


def attend_back(chosen, qkv, moved, ctx, lse, first, inner, leaves, after, shards):
    seq_len = qkv.shape[0]
    rows = seq_len // shards
    heads_here = HEADS // shards
    lanes = heads_here * LANES
    wide = D // shards
    outs = [shape(shards, rows + RANK, padded(3 * wide)), shape(RANK, padded(3 * wide))]

    def kernel(chosen, *refs):
        backward_kernel(*refs[:9], *refs[10:], heads_here=heads_here, wide=wide, block=256)

    def whole(array):
        return pl.BlockSpec(array.shape, lambda i, c: (0,) * len(array.shape))

    return pl.pallas_call(
        kernel,
        out_shape=outs,
        grid_spec=pltpu.PrefetchScalarGridSpec(
            num_scalar_prefetch=1,
            grid=(1,),
            in_specs=[whole(x) for x in (qkv, moved, ctx, lse, first, inner)]
            + [pl.BlockSpec((None, RANK, wide), lambda i, c: (c[0], 0, 0))] * 3
            + [ANY],
            out_specs=[whole(o) for o in outs],
            scratch_shapes=[
                pltpu.VMEM((seq_len, lanes), BF),
                pltpu.VMEM((8, seq_len), F32),
                pltpu.VMEM((3, seq_len, LANES), F32),
            ],
        ),
        compiler_params=pltpu.CompilerParams(vmem_limit_bytes=56 << 20),
        cost_estimate=cost(24),
        name="attention_backward",
    )(chosen, qkv, moved, ctx, lse, first, inner, *leaves, after)


def by_part(part, values):
    ordered = []
    for b in range(GROUP):
        total = values[0]
        for k in range(1, GROUP):
            total = jnp.where((part ^ k) == b, values[k], total)
        ordered.append(total)
    return ordered


def output_kernel(meta, moved, w0, w1, w2, w3, adapters, hidden, out_grad, *refs):
    ctx_ref, middle_ref, cat_ref, inner_ref = refs[-4:]
    shards, part, lanes = moved.shape
    wide = lanes // FOLD
    for s in range(shards):
        for g in range(FOLD):
            ctx_ref[g * part : (g + 1) * part, s * wide : (s + 1) * wide] = moved[s, :, g * wide : (g + 1) * wide]
    context = ctx_ref[...]
    inner = dot(context, adapters[:, ENTER_O : ENTER_O + RANK]).astype(BF)
    inner_ref[...] = inner
    branch = jnp.concatenate(by_part(meta[PART], [dot(context, w[...]) for w in (w0, w1, w2, w3)]), axis=1)
    branch = branch + dot_nt(inner, adapters[:, LEAVE_O : LEAVE_O + RANK])
    middle = hidden[...].astype(F32) + branch
    middle_ref[...] = middle
    second = norm_parts(middle)[0].astype(BF)
    cat_ref[:, :D] = second
    inner_u = dot(second, adapters[:, ENTER_U : ENTER_U + RANK])
    gi_down = dot(out_grad[...], adapters[:, LEAVE_D : LEAVE_D + RANK])
    empty = jnp.zeros((second.shape[0], LANES - 2 * RANK), F32)
    cat_ref[:, D:] = jnp.concatenate([inner_u, gi_down, empty], axis=1).astype(BF)


def project_output(meta, moved, weights, adapters, hidden, out_grad):
    rows = hidden.shape[0]
    return call(
        output_kernel,
        "project_output",
        [shape(rows, D), shape(rows, D, dtype=F32), shape(rows, TAIL), shape(rows, RANK)],
        (meta, moved, *weights, adapters, hidden, out_grad),
        [SMEM] + [VMEM] * 8,
        micros=6,
    )


def feed_spec(index, width=D):
    return pl.BlockSpec((D, width), lambda i: (0, index))


def down_back(meta, pieces, grads):
    arrays = [p[0] for p in pieces]
    steps = [p[1:] for p in pieces]
    count = len(arrays)
    shards, wide = count - 1, arrays[0].shape[0]
    rows = grads[0].shape[0]

    def kernel(meta, *refs):
        given, (out, weight, joined, sems) = refs[count : count + GROUP], refs[count + GROUP :]
        for k in range(GROUP):
            joined[k * rows : (k + 1) * rows] = given[k][...]
        place_pieces(meta, refs[:count], steps, weight, sems)
        for n in range(D // CHUNK):
            at = slice(n * CHUNK, (n + 1) * CHUNK)
            out[:, at] = dot_nt(joined[...], weight[...].reshape(D, D)[at, :])

    return call(
        kernel,
        "down_backward",
        [shape(GROUP * rows, D, dtype=F32), shape(shards, wide, D)],
        (meta, *arrays, *grads),
        [SMEM] + [ANY] * count + [VMEM] * GROUP,
        scratch=[pltpu.VMEM((GROUP * rows, D), BF), pltpu.SemaphoreType.DMA((count,))],
        micros=7,
    )


def up_kernel(w_ref, grad_ref, adapters, *refs):
    cats, (act_ref, pre_ref, keep, send, joined) = refs[:GROUP], refs[GROUP:]
    rows = cats[0].shape[0]
    for k in range(GROUP):
        joined[k * rows : (k + 1) * rows] = cats[k][:, :D]

    def step(n, carry):
        lanes = pl.ds(pl.multiple_of(n * CHUNK, CHUNK), CHUNK)
        weight = w_ref[:, lanes]
        pre = dot(joined[...], weight)
        extra, extra_grad = [], []
        for k in range(GROUP):
            leave = adapters[lanes, LEAVE_U + k * RANK : LEAVE_U + (k + 1) * RANK]
            enter = adapters[lanes, ENTER_D + k * RANK : ENTER_D + (k + 1) * RANK]
            extra.append(dot_nt(cats[k][:, D : D + RANK], leave))
            extra_grad.append(dot_nt(cats[k][:, D + RANK : D + 2 * RANK], enter))
        pre = pre + jnp.concatenate(extra, axis=0)
        grad = grad_ref[:, lanes] + jnp.concatenate(extra_grad, axis=0)
        cumulative = 0.5 * (1.0 + lax.erf(pre * (0.5**0.5)))
        density = jnp.exp2(pre * pre * (-0.5 * LOG2E)) * 0.3989422804014327
        act_ref[:, lanes] = (pre * cumulative).astype(BF)
        pre_ref[:, lanes] = (grad * (cumulative + pre * density)).astype(BF)
        return carry

    lax.fori_loop(0, D // CHUNK, step, 0)
    weight = w_ref[...]
    for k in range(GROUP):
        target = send if k % 2 else keep
        at = slice(k * rows, (k + 1) * rows)
        target[k // 2, :, :D] = dot_nt(pre_ref[at], weight).astype(BF)
        gi = dot(pre_ref[at], adapters[:, LEAVE_U + k * RANK : LEAVE_U + (k + 1) * RANK])
        empty = jnp.zeros((rows, LANES - RANK), F32)
        target[k // 2, :, D:] = jnp.concatenate([gi, empty], axis=1).astype(BF)


def up_both(ff, grad, cats):
    rows = cats[0].shape[0]
    total = GROUP * rows
    bundle = shape(2, rows, TAIL)
    return call(
        up_kernel,
        "up_forward_backward",
        [shape(total, D), shape(total, D), bundle, bundle],
        (ff, grad, ff, *cats),
        [feed_spec(0), pl.BlockSpec((total, D), lambda i: (0, 0)), feed_spec(D // LATE, LATE)]
        + [pl.BlockSpec((rows, TAIL), lambda i: (0, 0))] * GROUP,
        out_specs=[pl.BlockSpec((total, D), lambda i: (0, 0))] * 2
        + [pl.BlockSpec((2, rows, TAIL), lambda i: (0, 0, 0))] * 2,
        scratch=[pltpu.VMEM((total, D), BF)],
        micros=15,
        grid=(1,),
    )


def down_kernel(w_ref, act_ref, pre_ref, adapters, *refs):
    tails, (keep, send, pieces) = refs[:GROUP], refs[GROUP:]
    rows = tails[0].shape[0]
    weight = w_ref[...].reshape(D, D)
    for k in range(GROUP):
        target = send if k % 2 else keep
        at = slice(k * rows, (k + 1) * rows)
        act = act_ref[at]
        target[k // 2, :, :D] = dot(act, weight).astype(BF)
        inner = dot(act, adapters[:, ENTER_D + k * RANK : ENTER_D + (k + 1) * RANK])
        empty = jnp.zeros((rows, LANES - RANK), F32)
        target[k // 2, :, D:] = jnp.concatenate([inner, empty], axis=1).astype(BF)
        pieces[k * RANK : (k + 1) * RANK] = dot_tn(tails[k][:, RANK : 2 * RANK], act).astype(BF)
        start = (GROUP + k) * RANK
        pieces[start : start + RANK] = dot_tn(tails[k][:, :RANK], pre_ref[at]).astype(BF)


def down_forward(weight, ff, act, pre, cats):
    rows = cats[0].shape[0]
    total = GROUP * rows
    bundle = shape(2, rows, TAIL)
    return call(
        down_kernel,
        "down_forward",
        [bundle, bundle, shape(2 * GROUP * RANK, D)],
        (weight, act, pre, ff, *cats),
        [
            pl.BlockSpec(weight.shape, lambda i: (0, 0, 0)),
            pl.BlockSpec((total, D), lambda i: (0, 0)),
            pl.BlockSpec((total, D), lambda i: (0, 0)),
            feed_spec(D // LATE, LATE),
        ]
        + [pl.BlockSpec((rows, LANES), lambda i: (0, D // LANES))] * GROUP,
        out_specs=[pl.BlockSpec((2, rows, TAIL), lambda i: (0, 0, 0))] * 2
        + [pl.BlockSpec((2 * GROUP * RANK, D), lambda i: (0, 0))],
        micros=9,
        grid=(1,),
    )


def middle_kernel(
    meta, keep, near, far, middle, out_grad, w0, w1, w2, w3, adapters, grad_ref, packed, attn_ref, gi_up_ref, gi_o_ref
):
    shards, part, lanes = packed.shape
    wide = lanes // FOLD
    total = keep[0].astype(F32) + near[0].astype(F32) + far[...].astype(F32)
    gi_up = total[:, D : D + RANK].astype(BF)
    gi_up_ref[...] = gi_up
    grad = total[:, :D] + dot_nt(gi_up, adapters[:, ENTER_U : ENTER_U + RANK])
    second, inverse = norm_parts(middle[...])
    grad_middle = out_grad[...].astype(F32) + norm_back(grad, second, inverse)
    grad_ref[...] = grad_middle
    attn = grad_middle.astype(BF)
    attn_ref[...] = attn
    gi_o = dot(attn, adapters[:, LEAVE_O : LEAVE_O + RANK]).astype(BF)
    gi_o_ref[...] = gi_o
    parts = [attn[:, b * QUARTER : (b + 1) * QUARTER] for b in range(GROUP)]
    context = 0.0
    for k, w in enumerate((w0, w1, w2, w3)):
        chosen = parts[0]
        for b in range(1, GROUP):
            chosen = jnp.where((meta[PART] ^ k) == b, parts[b], chosen)
        context = context + dot_nt(chosen, w[...])
    context = (context + dot_nt(gi_o, adapters[:, ENTER_O : ENTER_O + RANK])).astype(BF)
    for s in range(shards):
        for g in range(FOLD):
            packed[s, :, g * wide : (g + 1) * wide] = context[g * part : (g + 1) * part, s * wide : (s + 1) * wide]


def middle_back(meta, keep, near, far, middle, out_grad, weights, adapters, shards):
    rows = middle.shape[0]
    wide = D // shards
    return call(
        middle_kernel,
        "middle_backward",
        [
            shape(rows, D, dtype=F32),
            shape(shards, rows // FOLD, FOLD * wide),
            shape(rows, D),
            shape(rows, RANK),
            shape(rows, RANK),
        ],
        (meta, keep, near, far, middle, out_grad, *weights, adapters),
        [SMEM] + [VMEM] * 10,
        micros=7,
    )


def scatter_stack(stack, natural):
    shards, height, _ = natural.shape
    wide = D // shards
    if natural.shape[2] > 3 * wide:
        natural[:, :, 3 * wide :] = jnp.zeros((shards, height, natural.shape[2] - 3 * wide), BF)
    for d in range(shards):
        for m in range(3 * height // RANK):
            piece = stack[m * RANK : (m + 1) * RANK, d * wide : (d + 1) * wide]
            natural[d, m // 3 * RANK : (m // 3 + 1) * RANK, m % 3 * wide : (m % 3 + 1) * wide] = piece


def token_kernel(meta, keep, near, far, middle, out_grad, adapters, cat, gi_up, context, gi_o, attn, inner_o, *refs):
    pieces, layer_ref, natural, stack = refs
    total = keep[0].astype(F32) + near[0].astype(F32) + far[...].astype(F32)
    inner_d = total[:, D : D + RANK].astype(BF)
    mlp = total[:, :D] + dot_nt(inner_d, adapters[:, LEAVE_D : LEAVE_D + RANK])
    layer_ref[...] = (middle[...] + mlp).astype(BF)
    width = pieces.shape[0]
    stack[:width] = pieces[...]
    pairs = ((gi_o[...], context[...]), (gi_up[...], cat[:, :D]), (inner_o[...], attn[...]), (inner_d, out_grad[...]))
    for i, (left, right) in enumerate(pairs):
        stack[width + i * RANK : width + (i + 1) * RANK] = dot_tn(left, right).astype(BF)
    scatter_stack(stack, natural)


def token_grads(meta, *args, shards):
    block = (4 * RANK, padded(3 * D // shards))
    rows = args[3].shape[0]
    return call(
        token_kernel,
        "token_adapter_grads",
        [shape(rows, D), shape(shards, *block)],
        (meta, *args),
        [SMEM] + [VMEM] * len(args),
        scratch=[pltpu.VMEM((12 * RANK, D), BF)],
        micros=4,
    )


def sum_pieces(moved, heads):
    rows = moved.shape[1] - RANK

    def kernel(moved, heads, out):
        out[:RANK] = jnp.sum(moved[:, rows:, :].astype(F32), axis=0).astype(BF)
        out[RANK:] = heads[...]

    return call(kernel, "sum_adapter_grads", [shape(2 * RANK, heads.shape[1])], (moved, heads), [VMEM] * 2)[0]


def input_kernel(meta, moved, w0, w1, w2, w3, adapters, late, hidden, grad_ref, after, out_ref, *, wide):
    shards, slot = moved.shape[0], moved.shape[2]
    rows = hidden.shape[0]
    count = shards // GROUP
    gis = [0.0, 0.0, 0.0]
    for s in range(shards):
        block = moved[s, :rows]
        for kind in range(3):
            bt = late[s * wide : (s + 1) * wide, LEAVE_QKV + kind * RANK : LEAVE_QKV + (kind + 1) * RANK]
            gis[kind] = gis[kind] + dot(block[:, kind * wide : (kind + 1) * wide], bt)
    gi = jnp.concatenate(gis, axis=1).astype(BF)
    grad = dot_nt(gi, adapters[:, ENTER_QKV : ENTER_QKV + 3 * RANK])
    for k, w in enumerate((w0, w1, w2, w3)):
        for j in range(count):
            place = (meta[PART] ^ k) * count + j
            grad = grad + dot_nt(moved[place, :rows], w[:, j * slot : (j + 1) * slot])
    first, inverse = norm_parts(hidden[...].astype(F32))
    out_ref[...] = (grad_ref[...] + norm_back(grad, first, inverse)).astype(BF)


def input_back(meta, moved, weights, adapters, ff, hidden, grad_middle, after, shards):
    rows = hidden.shape[0]
    wide = D // shards

    def kernel(*refs):
        input_kernel(*refs, wide=wide)

    return call(
        kernel,
        "input_backward",
        [shape(rows, D)],
        (meta, moved, *weights, adapters, ff, hidden, grad_middle, after),
        [SMEM]
        + [pl.BlockSpec(x.shape, lambda i, n=x.ndim: (0,) * n) for x in (moved, *weights, adapters)]
        + [feed_spec(D // LATE, LATE)]
        + [pl.BlockSpec(x.shape, lambda i: (0, 0)) for x in (hidden, grad_middle)]
        + [ANY],
        out_specs=[pl.BlockSpec((rows, D), lambda i: (0, 0))],
        grid=(1,),
        micros=10,
    )[0]


def spread_tokens_kernel(part, *refs, reps, wide):
    sets, blocks, (ao, bo, au, bu, ad, bd) = refs[:reps], refs[reps : 2 * reps], refs[2 * reps :]
    this = pl.program_id(0)
    flags = [jnp.where(sets[k][0] == this, 1.0, 0.0) for k in range(reps)]

    def one(value, m):
        row, lane = m // 3 * RANK, m % 3 * wide
        return value[row : row + RANK, lane : lane + wide]

    own = 0.0
    quarters = [0.0] * GROUP
    for k in range(reps):
        block = blocks[k][...].astype(F32)
        own = own + flags[k] * block[2 * RANK :]
        for j in range(GROUP):
            pair = jnp.concatenate([one(block, j), one(block, GROUP + j)], axis=0)
            quarters[k % GROUP] = quarters[k % GROUP] + flags[k ^ j] * pair
    ordered = by_part(part[0], quarters)
    ad[0] = jnp.concatenate([q[:RANK] for q in ordered], axis=1)
    bu[0] = jnp.concatenate([q[RANK:] for q in ordered], axis=1)
    for i, ref in enumerate((ao, au, bo, bd)):
        ref[0] = one(own, 2 + i)


def spread_heads_kernel(*refs, reps, wide):
    sets, blocks, outs = refs[:reps], refs[reps : 2 * reps], refs[2 * reps + 1 :]
    this = pl.program_id(0)
    own = 0.0
    for k in range(reps):
        own = own + jnp.where(sets[k][0] == this, 1.0, 0.0) * blocks[k][...].astype(F32)
    for kind in range(3):
        lanes = slice(kind * wide, (kind + 1) * wide)
        outs[2 * kind][0] = own[:RANK, lanes]
        outs[2 * kind + 1][0] = own[RANK:, lanes]


def spread(kernel, name, ins, scalars, blocks, kinds, micros, rest=0):
    outs = call(
        kernel,
        name,
        [shape(SETS, *k, dtype=F32) for k in kinds],
        ins,
        [SMEM] * scalars + [pl.BlockSpec(b.shape, lambda e: (0, 0)) for b in blocks] + [ANY] * rest,
        out_specs=[pl.BlockSpec((1, *k), lambda e: (e, 0, 0)) for k in kinds],
        micros=micros,
        grid=(SETS,),
    )
    return [jnp.transpose(o, (0, 2, 1)) if i % 2 == 0 else o for i, o in enumerate(outs)]


def spread_tokens(part, sets, blocks, wide):
    reps = len(blocks)
    narrow, broad = (RANK, wide), (RANK, GROUP * wide)

    def kernel(*refs):
        spread_tokens_kernel(*refs, reps=reps, wide=wide)

    kinds = [narrow] * 3 + [broad, broad, narrow]
    return spread(kernel, "spread_token_grads", (part, *sets, *blocks), 1 + reps, blocks, kinds, 5)


def spread_heads(sets, blocks, after, wide):
    reps = len(blocks)

    def kernel(*refs):
        spread_heads_kernel(*refs, reps=reps, wide=wide)

    return spread(kernel, "spread_head_grads", (*sets, *blocks, after), reps, blocks, [(RANK, wide)] * 6, 4, rest=1)


def body(
    hidden,
    out_grad,
    clip_lengths,
    adapter_index,
    w_query,
    w_key,
    w_value,
    w_output,
    w_up,
    w_down,
    a_query,
    b_query,
    a_key,
    b_key,
    a_value,
    b_value,
    a_output,
    b_output,
    a_up,
    b_up,
    a_down,
    b_down,
):
    shards = lax.axis_size("shard")
    reps = lax.axis_size("rep")
    wide = D // shards
    shard = lax.axis_index("shard")
    rep = lax.axis_index("rep")
    part = rep % GROUP

    def mate(value, flip):
        return lax.ppermute(value, "rep", [(i, i ^ flip) for i in range(reps)])

    def across(value):
        return lax.all_to_all(value, "shard", split_axis=0, concat_axis=0, tiled=True)

    def turned(table):
        return jnp.transpose(table, (0, 2, 1))

    def group_gather(value):
        other = mate(value, 2)
        return [value, mate(value, 1), other, mate(other, 1)]

    place = jnp.where(shard % 2 == 0, shard // 2, shards - 1 - shard // 2)
    meta = jnp.stack([shard, part, clip_lengths[0], rep & 1, place]).astype(jnp.int32)
    part_only = part[None].astype(jnp.int32)
    sets = [adapter_index] + [mate(adapter_index, flip) for flip in range(1, reps)]
    enters = [turned(t) for t in (a_query, a_key, a_value)]
    leaves = [b_query, b_key, b_value]

    narrow = enters + [turned(a_output), turned(a_up), b_output, b_down]
    bundle = pack_first(adapter_index, meta, hidden, w_output, narrow)
    cols, halves = pack_columns(meta, (w_query, w_key, w_value), bundle, shards)
    feed, down_own = pack_feed(sets[:GROUP], part_only, w_up, w_down, leaves, turned(a_down), b_up, bundle, shards)
    cols = across(cols)
    held = {}

    def between(k, arrivals):
        if k == 1:
            return lax.optimization_barrier((*arrivals, halves, feed))[:2]
        if k == 2:
            below, above, held["cols"] = lax.optimization_barrier((*arrivals, cols))
            return below, above
        if k == shards // 2 - 1:
            below, above, held["feed"], held["down"] = lax.optimization_barrier((*arrivals, feed, down_own))
            return below, above
        return lax.optimization_barrier(arrivals)

    pieces = ring_pieces(bundle, shards, between)
    cols = held["cols"]
    cols_mate = mate(cols, 1)
    ff_moved = lax.all_gather(held["feed"], "shard", axis=0, tiled=True)
    grads_out = group_gather(out_grad)

    first, qkv, inner_qkv, adapters, out_quarter = project_qkv(meta, adapter_index, cols, cols_mate, pieces, leaves)
    stage = {}

    def down_between(k, arrivals):
        if k == 1:
            below, above, stage["qkv"] = lax.optimization_barrier((*arrivals, qkv))
            stage["out_weights"] = group_gather(out_quarter)
            packed, stage["ctx"], stage["lse"] = attend(stage["qkv"], shards)
            stage["packed"] = packed
            return below, above
        if k == 2:
            below, above, packed = lax.optimization_barrier((*arrivals, stage["packed"]))
            stage["moved"] = across(packed)
            return below, above
        if k == 3:
            below, above, stage["moved"], stage["ff"] = lax.optimization_barrier((*arrivals, stage["moved"], ff_moved))
            return below, above
        return lax.optimization_barrier(arrivals)

    down_pieces = ring_pieces(held["down"], shards, down_between)
    ff_all = stage["ff"]
    qkv, ctx, lse, out_weights = stage["qkv"], stage["ctx"], stage["lse"], stage["out_weights"]
    context, middle, cat, inner_o = project_output(
        meta, stage["moved"], out_weights, adapters, hidden, out_grad
    )
    halves, lse = lax.optimization_barrier((halves, lse))
    qkv_quarter = lax.all_gather(halves, "shard", axis=0, tiled=True)

    grad_act, down_weight = down_back(meta, down_pieces, grads_out)
    other = mate(cat, 2)
    other, grad_act = lax.optimization_barrier((other, grad_act))
    cats = [cat, mate(cat, 1), other, mate(other, 1)]
    act, pre, keep, give = up_both(ff_all, grad_act, cats)

    def near_sum(keep, give):
        near = mate(give, 1)
        return near, (keep[1].astype(F32) + near[1].astype(F32)).astype(BF)

    near, far = near_sum(keep, give)
    far = mate(far, 2)
    keep_d, give_d, pieces_d = down_forward(down_weight, ff_all, act, pre, cats)
    give_d, far = lax.optimization_barrier((give_d, far))
    near_d, far_d = near_sum(keep_d, give_d)
    far_d = mate(far_d, 2)
    grad_middle, dctx, attn, gi_up, gi_o = middle_back(
        meta, keep, near, far, middle, out_grad, out_weights, adapters, shards
    )
    dctx_moved = across(dctx)
    layer_out, token_pieces = token_grads(
        meta, keep_d, near_d, far_d, middle, out_grad, adapters, cat, gi_up, context, gi_o, attn, inner_o, pieces_d,
        shards=shards,
    )
    early = across(token_pieces)
    qkv_quarter, token_pieces = lax.optimization_barrier((qkv_quarter, token_pieces))
    qkv_weights = group_gather(qkv_quarter)
    lse_rows = lse.reshape(lse.shape[0], 1, lse.shape[1])
    dqkv, head_out = attend_back(
        adapter_index, qkv, dctx_moved, ctx, lse_rows, first, inner_qkv, leaves, token_pieces, shards
    )
    dqkv, early = lax.optimization_barrier((dqkv, early))
    dqkv_moved = across(dqkv)

    def over_reps(value):
        return [value] + [mate(value, flip) for flip in range(1, reps)]

    early = jnp.sum(early.astype(F32), axis=0).astype(BF)
    token_outs = spread_tokens(part_only, sets, over_reps(early), wide)
    summed = sum_pieces(dqkv_moved, head_out)
    input_grad = input_back(
        meta, dqkv_moved, qkv_weights, adapters, ff_all, hidden, grad_middle, token_outs[1], shards
    )
    outs = spread_heads(sets, over_reps(summed), input_grad, wide) + token_outs
    return (layer_out, input_grad, *outs)


def solution(mesh):
    rows = P("shard", None)
    enter = P(None, "shard", None)
    leave = P(None, None, "shard")
    tokens = P(("rep", "shard"), None)
    return jax.shard_map(
        body,
        mesh=mesh,
        in_specs=(tokens, tokens, P("rep"), P("rep")) + (rows,) * 6 + (enter, leave) * 6,
        out_specs=(tokens, tokens) + (enter, leave) * 6,
        check_vma=False,
    )
```

```python
import jax
import jax.numpy as jnp
from jax import lax
from jax.experimental import pallas as pl
from jax.experimental.pallas import tpu as pltpu
from jax.sharding import PartitionSpec as P

D = 1280
FF = 5120
HEADS = 16
HEAD = 80
LANES = 128
RANK = 16
SETS = 8
GROUP = 4
FOLD = 4
CHUNK = 256
BLOCK_Q = 384
TAIL = D + LANES
RATE = 1.15e9

EPSILON = 1e-05
NEGATIVE = -1e30
LOG2E = 1.4426950408889634
SCALE = HEAD ** (-0.5)
ONE_LANE = HEAD
MASK_LANE = HEAD + 1

BF = jnp.bfloat16
F32 = jnp.float32

QUARTER = D // GROUP
ENTER_QKV = 0
ENTER_O = 48
ENTER_U = 64
LEAVE_O = 80
LEAVE_D = 96
FIRST = 128
BESIDE = 512
BUNDLE = D + BESIDE

ENTER_D = 0
LEAVE_U = 64
LEAVE_QKV = 128
LATE = 256

SHARD, PART, LENGTH, CORE, RING = range(5)

VMEM = pl.BlockSpec(memory_space=pltpu.VMEM)
SMEM = pl.BlockSpec(memory_space=pltpu.SMEM)
ANY = pl.BlockSpec(memory_space=pl.ANY)


def dot(left, right):
    return jnp.dot(left, right, preferred_element_type=F32)


def dot_nt(left, right):
    return lax.dot_general(left, right, (((1,), (1,)), ((), ())), preferred_element_type=F32)


def dot_tn(left, right):
    return lax.dot_general(left, right, (((0,), (0,)), ((), ())), preferred_element_type=F32)


def norm_parts(values):
    center = values - jnp.mean(values, axis=-1, keepdims=True)
    spread = jnp.mean(center * center, axis=-1, keepdims=True)
    inverse = lax.rsqrt(spread + EPSILON)
    return center * inverse, inverse


def norm_back(grad, normal, inverse):
    average = jnp.mean(grad, axis=-1, keepdims=True)
    along = jnp.mean(grad * normal, axis=-1, keepdims=True)
    return inverse * (grad - average - normal * along)


def cost(micros):
    return pl.CostEstimate(flops=int(micros * RATE), transcendentals=0, bytes_accessed=0)


def call(kernel, name, outs, ins, specs, out_specs=None, scratch=(), micros=1.0, **rest):
    return pl.pallas_call(
        kernel,
        out_shape=outs,
        in_specs=specs,
        out_specs=[VMEM] * len(outs) if out_specs is None else out_specs,
        scratch_shapes=list(scratch),
        compiler_params=pltpu.CompilerParams(vmem_limit_bytes=56 << 20),
        cost_estimate=cost(micros),
        name=name,
        **rest,
    )(*ins)


def shape(*dims, dtype=BF):
    return jax.ShapeDtypeStruct(dims, dtype)


def padded(size):
    return -(-size // LANES) * LANES


def column_blocks(wq, wk, wv, shards):
    wide = D // shards
    pad = jnp.zeros((wide, padded(3 * wide) - 3 * wide), BF)
    for s in range(shards):
        at = slice(s * wide, (s + 1) * wide)
        yield s, jnp.concatenate([wq[:, at], wk[:, at], wv[:, at], pad], axis=1)


def pack_columns(meta, weights, after, shards):
    wide = D // shards
    slot = padded(3 * wide)
    count = shards // GROUP

    def kernel(meta, wq, wk, wv, after, cols, quarter):
        for s, block in column_blocks(wq, wk, wv, shards):
            cols[s] = jnp.where(meta[CORE] == 0, block[:, : slot // 2], block[:, slot // 2 :])

            @pl.when(meta[PART] == s // count)
            def _():
                quarter[:, s % count * slot : (s % count + 1) * slot] = block

    outs = [shape(shards, wide, slot // 2), shape(wide, count * slot)]
    return call(kernel, "pack_columns", outs, (meta, *weights, after), [SMEM] + [VMEM] * 3 + [ANY], micros=3)


def unit(size):
    row = lax.broadcasted_iota(jnp.int32, (size, size), 0)
    col = lax.broadcasted_iota(jnp.int32, (size, size), 1)
    return (row == col).astype(BF)


def pack_first(chosen, meta, hidden, w_output, narrow):
    rows = hidden.shape[0]
    wide = narrow[0].shape[2]

    def kernel(chosen, meta, hidden, w_output, *refs):
        out = refs[-1]
        eye = unit(wide)
        out[:, :D] = hidden[...]
        out[:, D:] = jnp.zeros((rows, BESIDE), BF)
        for i, ref in enumerate(refs[:-1]):
            out[:wide, D + i * RANK : D + (i + 1) * RANK] = dot_nt(eye, ref[...]).astype(BF)
        for p in range(GROUP):

            @pl.when(meta[PART] == p)
            def _():
                out[:wide, D + FIRST : D + FIRST + QUARTER] = w_output[:, p * QUARTER : (p + 1) * QUARTER]

    return pl.pallas_call(
        kernel,
        out_shape=shape(rows, BUNDLE),
        grid_spec=pltpu.PrefetchScalarGridSpec(
            num_scalar_prefetch=1,
            grid=(1,),
            in_specs=[SMEM, pl.BlockSpec((rows, D), lambda i, m: (0, 0)), pl.BlockSpec((wide, D), lambda i, m: (0, 0))]
            + [pl.BlockSpec((None, RANK, wide), lambda i, m: (m[0], 0, 0))] * len(narrow),
            out_specs=pl.BlockSpec((rows, BUNDLE), lambda i, m: (0, 0)),
        ),
        cost_estimate=cost(3),
        name="pack_first",
    )(chosen, meta, hidden, w_output, *narrow)


def feed_kernel(*refs, wide, shards):
    part = refs[GROUP][0]
    (w_up, w_down), maps, (out, sem) = refs[GROUP + 1 : GROUP + 3], refs[GROUP + 3 : -3], refs[-2:]
    narrow, downs, ups = maps[:3], maps[3:7], maps[7:11]
    copy = pltpu.make_async_copy(w_down.at[part], out.at[:, pl.ds(D, D)], sem)
    copy.start()
    eye = unit(wide)
    beside = 2 * D
    for i, ref in enumerate(narrow):
        start = beside + LEAVE_QKV + i * RANK
        out[:, start : start + RANK] = dot_nt(eye, ref[...]).astype(BF)
    end = beside + LEAVE_QKV + 3 * RANK
    out[:, end:] = jnp.zeros((wide, 2 * D + LATE - end), BF)
    for p in range(GROUP):

        @pl.when(part == p)
        def _():
            at = slice(p * wide, (p + 1) * wide)
            for i, ref in enumerate(downs):
                start = beside + ENTER_D + i * RANK
                out[:, start : start + RANK] = dot_nt(eye, ref[:, at]).astype(BF)
            for i, ref in enumerate(ups):
                start = beside + LEAVE_U + i * RANK
                out[:, start : start + RANK] = dot_nt(eye, ref[:, at]).astype(BF)
            for s in range(shards):
                start = (s * GROUP + p) * wide
                out[:, s * wide : (s + 1) * wide] = w_up[:, start : start + wide]

    copy.wait()


def pack_feed(sets, part, w_up, w_down, narrow, a_down, b_up, after, shards):
    wide = D // shards
    ff_wide = GROUP * wide
    width = 2 * D + LATE

    def at(k):
        return lambda i, *m: (m[k][0], 0, 0)

    specs = (
        [pl.BlockSpec((wide, FF), lambda i, *m: (0, 0)), ANY]
        + [pl.BlockSpec((None, RANK, wide), at(0))] * 3
        + [pl.BlockSpec((None, RANK, ff_wide), at(k)) for k in range(GROUP)] * 2
        + [ANY]
    )

    def kernel(*refs):
        feed_kernel(*refs, wide=wide, shards=shards)

    return pl.pallas_call(
        kernel,
        out_shape=shape(wide, width),
        grid_spec=pltpu.PrefetchScalarGridSpec(
            num_scalar_prefetch=GROUP + 1,
            grid=(1,),
            in_specs=specs,
            out_specs=pl.BlockSpec((wide, width), lambda i, *m: (0, 0)),
            scratch_shapes=[pltpu.SemaphoreType.DMA],
        ),
        cost_estimate=cost(5),
        name="pack_feed",
    )(*sets, part, w_up, w_down.reshape(GROUP, wide, D), *narrow, *[a_down] * GROUP, *[b_up] * GROUP, after)


def ring_shard(place, shards):
    return jnp.where(place < shards // 2, 2 * place, 2 * (shards - 1 - place) + 1)


def ring_pieces(value, shards, between):
    places = [2 * i if i < shards // 2 else 2 * (shards - 1 - i) + 1 for i in range(shards)]
    onward = [(places[i], places[(i + 1) % shards]) for i in range(shards)]
    back = [(b, a) for a, b in onward]
    half = value.shape[0] // 2
    pieces = [(value, 0, 0)]
    below, above = value, value
    for k in range(1, shards // 2):
        below = lax.ppermute(below, "shard", onward)
        above = lax.ppermute(above, "shard", back)
        below, above = between(k, (below, above))
        pieces += [(below, -k, 0), (above, k, 0)]
    far = shards // 2
    pieces.append((lax.ppermute(below[:half], "shard", onward), far, 0))
    pieces.append((lax.ppermute(above[half:], "shard", back), far, half))
    return pieces


def piece_shard(meta, step, shards):
    return ring_shard((meta[RING] + step + shards) % shards, shards)


def place_pieces(meta, pieces, steps, target, sems, column=None):
    shards = target.shape[0]
    copies = []
    for i, (ref, (step, start)) in enumerate(zip(pieces, steps)):
        if column is not None:
            ref = ref.at[:, pl.ds(column, target.shape[2])]
        block = target.at[piece_shard(meta, step, shards), pl.ds(start, ref.shape[0])]
        copies.append(pltpu.make_async_copy(ref, block, sems.at[i]))
    for copy in copies:
        copy.start()
    for copy in copies:
        copy.wait()


def qkv_kernel(meta, w_mine, w_mate, *refs, shards, steps):
    count = len(steps)
    pieces, leaves = refs[:count], refs[count : count + 3]
    first_ref, qkv_ref, inner_ref, enter, quarter, hid, sems = refs[-7:]
    wide = D // shards
    heads_here = HEADS // shards
    slot = padded(3 * wide)
    side = meta[CORE]
    rows = hid.shape[1]
    place_pieces(meta, pieces, steps, hid, sems)
    for s in range(shards):
        enter[s * wide : (s + 1) * wide, :] = hid[s, :wide, D : D + FIRST]
        quarter[s * wide : (s + 1) * wide, :] = hid[s, :wide, D + FIRST : D + FIRST + QUARTER]
    lane = lax.broadcasted_iota(jnp.int32, (rows, LANES - HEAD), 1)
    spot = lax.broadcasted_iota(jnp.int32, (rows, LANES - HEAD), 0)

    def step(s, carry):
        at = pl.ds(pl.multiple_of(s * rows, 64), rows)
        first = norm_parts(hid[s, :, :D].astype(F32))[0].astype(BF)
        first_ref[at, :] = first
        inner = dot(first, enter[:, : 3 * RANK]).astype(BF)
        inner_ref[at, :] = inner
        y_mine = dot(first, w_mine[...].reshape(D, slot // 2))
        y_mate = dot(first, w_mate[...].reshape(D, slot // 2))
        lo = jnp.where(side == 0, y_mine, y_mate)
        hi = jnp.where(side == 0, y_mate, y_mine)
        y = jnp.concatenate([lo, hi], axis=1)
        hidden_key = jnp.where((spot + s * rows < meta[LENGTH]) | (lane != MASK_LANE - HEAD), 0.0, NEGATIVE)
        for kind in range(3):
            lanes = slice(kind * RANK, (kind + 1) * RANK)
            out = y[:, kind * wide : (kind + 1) * wide] + dot(inner[:, lanes], leaves[kind][...])
            if kind == 0:
                tail = jnp.where(lane == MASK_LANE - HEAD, 1.0, 0.0)
            elif kind == 1:
                tail = hidden_key
            else:
                tail = jnp.where(lane == ONE_LANE - HEAD, 1.0, 0.0)
            for h in range(heads_here):
                base = (kind * heads_here + h) * LANES
                head = jnp.concatenate([out[:, h * HEAD : (h + 1) * HEAD], tail], axis=1)
                qkv_ref[at, base : base + LANES] = head.astype(BF)
        return carry

    lax.fori_loop(0, shards, step, 0, unroll=True)


def project_qkv(meta, chosen, w_mine, w_mate, pieces, leaves):
    shards = len(pieces) - 1
    steps = [p[1:] for p in pieces]
    rows = pieces[0][0].shape[0]
    seq_len = rows * shards
    lanes = HEADS // shards * LANES
    wide = D // shards
    weight = pl.BlockSpec(w_mine.shape, lambda i, c: (0, 0, 0))
    outs = [
        shape(seq_len, D),
        shape(seq_len, 3 * lanes),
        shape(seq_len, 3 * RANK),
        shape(D, FIRST),
        shape(D, QUARTER),
    ]

    def kernel(chosen, *refs):
        qkv_kernel(*refs, shards=shards, steps=steps)

    return pl.pallas_call(
        kernel,
        out_shape=outs,
        grid_spec=pltpu.PrefetchScalarGridSpec(
            num_scalar_prefetch=1,
            grid=(1,),
            in_specs=[SMEM, weight, weight]
            + [ANY] * len(pieces)
            + [pl.BlockSpec((None, RANK, wide), lambda i, c: (c[0], 0, 0))] * 3,
            out_specs=[pl.BlockSpec(o.shape, lambda i, c: (0, 0)) for o in outs],
            scratch_shapes=[
                pltpu.VMEM((shards, rows, BUNDLE), BF),
                pltpu.SemaphoreType.DMA((len(pieces),)),
            ],
        ),
        compiler_params=pltpu.CompilerParams(vmem_limit_bytes=56 << 20),
        cost_estimate=cost(14),
        name="project_qkv",
    )(chosen, meta, w_mine, w_mate, *[p[0] for p in pieces], *leaves)


def forward_kernel(qkv_ref, packed_ref, ctx_ref, lse_ref, *, heads_here, wide, block):
    shards, part, _ = packed_ref.shape
    seq_len = ctx_ref.shape[0]
    factor = SCALE * LOG2E

    def step(i, carry):
        at = pl.ds(pl.multiple_of(i * block, 64), block)
        for h in range(heads_here):
            queries = qkv_ref[at, h * LANES : (h + 1) * LANES]
            keys = qkv_ref[:, (heads_here + h) * LANES : (heads_here + h + 1) * LANES]
            values = qkv_ref[:, (2 * heads_here + h) * LANES : (2 * heads_here + h + 1) * LANES]
            scores = dot_nt(queries, keys)
            highest = jnp.max(scores, axis=1, keepdims=True)
            weights = jnp.exp2((scores - highest) * factor).astype(BF)
            portion = dot(weights, values)
            total = portion[:, ONE_LANE : ONE_LANE + 1]
            ctx_ref[at, h * LANES : (h + 1) * LANES] = (portion / total).astype(BF)
            lse_ref[h, at, :] = highest * factor + jnp.log2(total)
        return carry

    lax.fori_loop(0, seq_len // block, step, 0, unroll=True)
    for h in range(heads_here):
        for d in range(shards):
            for g in range(FOLD):
                start = g * wide + h * HEAD
                row = (d * FOLD + g) * part
                packed_ref[d, :, start : start + HEAD] = ctx_ref[row : row + part, h * LANES : h * LANES + HEAD]


def attend(qkv, shards):
    seq_len = qkv.shape[0]
    rows = seq_len // shards
    heads_here = HEADS // shards
    lanes = heads_here * LANES
    wide = D // shards

    def kernel(*refs):
        forward_kernel(*refs, heads_here=heads_here, wide=wide, block=BLOCK_Q)

    return call(
        kernel,
        "attention_forward",
        [
            shape(shards, rows // FOLD, FOLD * wide),
            shape(seq_len, lanes),
            shape(heads_here, seq_len, 1, dtype=F32),
        ],
        (qkv,),
        [VMEM],
        micros=12,
    )


def backward_kernel(
    qkv_ref, moved_ref, ctx_ref, lse_ref, first, inner, leave_q, leave_k, leave_v, out_ref, heads_ref, douts, delta, acc, turned,
    *, heads_here, wide, block
):
    shards = moved_ref.shape[0]
    seq_len = qkv_ref.shape[0]
    rows = seq_len // shards
    part = rows // FOLD
    slot = out_ref.shape[2]
    for d in range(shards):
        for g in range(FOLD):
            base = d * rows + g * part
            for h in range(heads_here):
                start = g * wide + h * HEAD
                piece = moved_ref[d, :, start : start + HEAD]
                douts[base : base + part, h * LANES : h * LANES + HEAD] = piece
    for h in range(heads_here):
        douts[:, h * LANES + HEAD : (h + 1) * LANES] = jnp.zeros((seq_len, LANES - HEAD), BF)
    ones = jnp.ones((8, LANES), F32)
    if slot > 3 * wide:
        out_ref[:, :, 3 * wide :] = jnp.zeros((shards, rows + RANK, slot - 3 * wide), BF)
    for h in range(heads_here):
        lanes = slice(h * LANES, (h + 1) * LANES)
        product = douts[:, lanes].astype(F32) * ctx_ref[:, lanes].astype(F32)
        delta[...] = lax.dot_general(
            ones, product, (((1,), (1,)), ((), ())), precision=lax.Precision.HIGHEST, preferred_element_type=F32
        )
        queries = qkv_ref[:, lanes]
        grads = douts[:, lanes]

        def step(i, carry):
            at = pl.ds(pl.multiple_of(i * block, block), block)
            keys = qkv_ref[at, (heads_here + h) * LANES : (heads_here + h + 1) * LANES]
            values = qkv_ref[at, (2 * heads_here + h) * LANES : (2 * heads_here + h + 1) * LANES]
            scores = dot_nt(keys, queries)
            weights = jnp.exp2(scores * (SCALE * LOG2E) - lse_ref[h])
            grad_weights = dot_nt(values, grads)
            grad_scores = (weights * (grad_weights - delta[0:1, :])).astype(BF)
            acc[2, at, :] = dot(weights.astype(BF), grads)
            acc[1, at, :] = dot(grad_scores, queries) * SCALE
            moved = dot_tn(keys, grad_scores)

            @pl.when(i == 0)
            def _():
                turned[...] = moved

            @pl.when(i > 0)
            def _():
                turned[...] += moved

            return carry

        lax.fori_loop(0, seq_len // block, step, 0, unroll=True)
        acc[0] = jnp.transpose(turned[...])
        for kind in range(3):
            start = kind * wide + h * HEAD
            for d in range(shards):
                piece = acc[kind, d * rows : (d + 1) * rows, :HEAD]
                if kind == 0:
                    piece = piece * SCALE
                out_ref[d, :rows, start : start + HEAD] = piece.astype(BF)
    heads_ref[...] = jnp.zeros_like(heads_ref)
    parts = []
    for kind, leave in enumerate((leave_q, leave_k, leave_v)):
        grad = out_ref[:, :rows, kind * wide : (kind + 1) * wide].reshape(seq_len, wide)
        lanes = slice(kind * RANK, (kind + 1) * RANK)
        parts.append(dot_nt(grad, leave[...]))
        heads_ref[:, kind * wide : (kind + 1) * wide] = dot_tn(inner[:, lanes], grad).astype(BF)
    entered = dot_tn(jnp.concatenate(parts, axis=1).astype(BF), first[...]).astype(BF)
    for kind in range(3):
        for d in range(shards):
            piece = entered[kind * RANK : (kind + 1) * RANK, d * wide : (d + 1) * wide]
            out_ref[d, rows:, kind * wide : (kind + 1) * wide] = piece


def attend_back(chosen, qkv, moved, ctx, lse, first, inner, leaves, after, shards):
    seq_len = qkv.shape[0]
    rows = seq_len // shards
    heads_here = HEADS // shards
    lanes = heads_here * LANES
    wide = D // shards
    outs = [shape(shards, rows + RANK, padded(3 * wide)), shape(RANK, padded(3 * wide))]

    def kernel(chosen, *refs):
        backward_kernel(*refs[:9], *refs[10:], heads_here=heads_here, wide=wide, block=512)

    def whole(array):
        return pl.BlockSpec(array.shape, lambda i, c: (0,) * len(array.shape))

    return pl.pallas_call(
        kernel,
        out_shape=outs,
        grid_spec=pltpu.PrefetchScalarGridSpec(
            num_scalar_prefetch=1,
            grid=(1,),
            in_specs=[whole(x) for x in (qkv, moved, ctx, lse, first, inner)]
            + [pl.BlockSpec((None, RANK, wide), lambda i, c: (c[0], 0, 0))] * 3
            + [ANY],
            out_specs=[whole(o) for o in outs],
            scratch_shapes=[
                pltpu.VMEM((seq_len, lanes), BF),
                pltpu.VMEM((8, seq_len), F32),
                pltpu.VMEM((3, seq_len, LANES), F32),
                pltpu.VMEM((LANES, seq_len), F32),
            ],
        ),
        compiler_params=pltpu.CompilerParams(vmem_limit_bytes=56 << 20),
        cost_estimate=cost(24),
        name="attention_backward",
    )(chosen, qkv, moved, ctx, lse, first, inner, *leaves, after)


def by_part(part, values):
    ordered = []
    for b in range(GROUP):
        total = values[0]
        for k in range(1, GROUP):
            total = jnp.where((part ^ k) == b, values[k], total)
        ordered.append(total)
    return ordered


def assemble_output(meta, weights):
    def kernel(meta, *refs):
        out = refs[-1]
        for k in range(GROUP):
            for b in range(GROUP):

                @pl.when((meta[PART] ^ k) == b)
                def _():
                    out[:, b * QUARTER : (b + 1) * QUARTER] = refs[k][...]

    return call(kernel, "assemble_output", [shape(D, D)], (meta, *weights), [SMEM] + [VMEM] * GROUP, micros=3)[0]


def output_kernel(moved, weight, adapters, hidden, out_grad, *refs):
    ctx_ref, middle_ref, cat_ref, inner_ref = refs[-4:]
    shards, part, lanes = moved.shape
    wide = lanes // FOLD
    for s in range(shards):
        for g in range(FOLD):
            ctx_ref[g * part : (g + 1) * part, s * wide : (s + 1) * wide] = moved[s, :, g * wide : (g + 1) * wide]
    context = ctx_ref[...]
    inner = dot(context, adapters[:, ENTER_O : ENTER_O + RANK]).astype(BF)
    inner_ref[...] = inner
    branch = dot(context, weight[...]) + dot_nt(inner, adapters[:, LEAVE_O : LEAVE_O + RANK])
    middle = hidden[...].astype(F32) + branch
    middle_ref[...] = middle
    second = norm_parts(middle)[0].astype(BF)
    cat_ref[:, :D] = second
    inner_u = dot(second, adapters[:, ENTER_U : ENTER_U + RANK])
    gi_down = dot(out_grad[...], adapters[:, LEAVE_D : LEAVE_D + RANK])
    empty = jnp.zeros((second.shape[0], LANES - 2 * RANK), F32)
    cat_ref[:, D:] = jnp.concatenate([inner_u, gi_down, empty], axis=1).astype(BF)


def project_output(moved, weight, adapters, hidden, out_grad):
    rows = hidden.shape[0]
    return call(
        output_kernel,
        "project_output",
        [shape(rows, D), shape(rows, D, dtype=F32), shape(rows, TAIL), shape(rows, RANK)],
        (moved, weight, adapters, hidden, out_grad),
        [VMEM] * 5,
        micros=6,
    )


def feed_spec(index, width=D):
    return pl.BlockSpec((D, width), lambda i: (0, index))


def down_back(meta, pieces, grads):
    arrays = [p[0] for p in pieces]
    steps = [p[1:] for p in pieces]
    count = len(arrays)
    shards, wide = count - 1, arrays[0].shape[0]
    rows = grads[0].shape[0]

    def kernel(meta, *refs):
        given, (out, weight, joined, sems) = refs[count : count + GROUP], refs[count + GROUP :]
        for k in range(GROUP):
            joined[k * rows : (k + 1) * rows] = given[k][...]
        place_pieces(meta, refs[:count], steps, weight, sems, D)
        for n in range(D // CHUNK):
            at = slice(n * CHUNK, (n + 1) * CHUNK)
            out[:, at] = dot_nt(joined[...], weight[...].reshape(D, D)[at, :]).astype(BF)

    return call(
        kernel,
        "down_backward",
        [shape(GROUP * rows, D), shape(shards, wide, D)],
        (meta, *arrays, *grads),
        [SMEM] + [ANY] * count + [VMEM] * GROUP,
        scratch=[pltpu.VMEM((GROUP * rows, D), BF), pltpu.SemaphoreType.DMA((count,))],
        micros=7,
    )


def up_kernel(meta, *refs, steps):
    count = len(steps)
    pieces, grad_ref, cats = refs[:count], refs[count], refs[count + 1 : count + 1 + GROUP]
    act_ref, pre_ref, keep, send, late, joined, w_ref, late_ref, sems, late_sems = refs[count + 1 + GROUP :]
    rows = cats[0].shape[0]
    place_pieces(meta, pieces, steps, w_ref, sems, 0)
    place_pieces(meta, pieces, steps, late_ref, late_sems, 2 * D)
    late[...] = late_ref[...].reshape(D, LATE)
    adapters = late
    for k in range(GROUP):
        joined[k * rows : (k + 1) * rows] = cats[k][:, :D]

    def step(n, carry):
        lanes = pl.ds(pl.multiple_of(n * CHUNK, CHUNK), CHUNK)
        weight = w_ref[:, :, lanes].reshape(D, CHUNK)
        pre = dot(joined[...], weight)
        extra, extra_grad = [], []
        for k in range(GROUP):
            leave = adapters[lanes, LEAVE_U + k * RANK : LEAVE_U + (k + 1) * RANK]
            enter = adapters[lanes, ENTER_D + k * RANK : ENTER_D + (k + 1) * RANK]
            extra.append(dot_nt(cats[k][:, D : D + RANK], leave))
            extra_grad.append(dot_nt(cats[k][:, D + RANK : D + 2 * RANK], enter))
        pre = pre + jnp.concatenate(extra, axis=0)
        grad = grad_ref[:, lanes].astype(F32) + jnp.concatenate(extra_grad, axis=0)
        cumulative = 0.5 * (1.0 + lax.erf(pre * (0.5**0.5)))
        density = jnp.exp2(pre * pre * (-0.5 * LOG2E)) * 0.3989422804014327
        act_ref[:, lanes] = (pre * cumulative).astype(BF)
        pre_ref[:, lanes] = (grad * (cumulative + pre * density)).astype(BF)
        return carry

    lax.fori_loop(0, D // CHUNK, step, 0, unroll=True)
    for n in range(D // CHUNK):
        lanes = slice(n * CHUNK, (n + 1) * CHUNK)
        total = dot_nt(pre_ref[...], w_ref[...].reshape(D, D)[lanes, :]).astype(BF)
        for k in range(GROUP):
            target = send if k % 2 else keep
            target[k // 2, :, lanes] = total[k * rows : (k + 1) * rows]
    for k in range(GROUP):
        target = send if k % 2 else keep
        at = slice(k * rows, (k + 1) * rows)
        gi = dot(pre_ref[at], adapters[:, LEAVE_U + k * RANK : LEAVE_U + (k + 1) * RANK])
        empty = jnp.zeros((rows, LANES - RANK), F32)
        target[k // 2, :, D:] = jnp.concatenate([gi, empty], axis=1).astype(BF)


def up_both(meta, pieces, grad, cats):
    arrays = [p[0] for p in pieces]
    steps = [p[1:] for p in pieces]
    count = len(arrays)
    shards, wide = count - 1, arrays[0].shape[0]
    rows = cats[0].shape[0]
    total = GROUP * rows
    bundle = shape(2, rows, TAIL)

    def kernel(*refs):
        up_kernel(*refs, steps=steps)

    return call(
        kernel,
        "up_forward_backward",
        [shape(total, D), shape(total, D), bundle, bundle, shape(D, LATE)],
        (meta, *arrays, grad, *cats),
        [SMEM] + [ANY] * count + [VMEM] * (1 + GROUP),
        scratch=[
            pltpu.VMEM((total, D), BF),
            pltpu.VMEM((shards, wide, D), BF),
            pltpu.VMEM((shards, wide, LATE), BF),
            pltpu.SemaphoreType.DMA((count,)),
            pltpu.SemaphoreType.DMA((count,)),
        ],
        micros=12,
    )


def down_kernel(w_ref, act_ref, pre_ref, adapters, *refs):
    tails, (keep, send, pieces) = refs[:GROUP], refs[GROUP:]
    rows = tails[0].shape[0]
    for n in range(D // CHUNK):
        lanes = slice(n * CHUNK, (n + 1) * CHUNK)
        total = dot(act_ref[...], w_ref[:, :, lanes].reshape(D, CHUNK)).astype(BF)
        for k in range(GROUP):
            target = send if k % 2 else keep
            target[k // 2, :, lanes] = total[k * rows : (k + 1) * rows]
    for k in range(GROUP):
        target = send if k % 2 else keep
        at = slice(k * rows, (k + 1) * rows)
        act = act_ref[at]
        inner = dot(act, adapters[:, ENTER_D + k * RANK : ENTER_D + (k + 1) * RANK])
        empty = jnp.zeros((rows, LANES - RANK), F32)
        target[k // 2, :, D:] = jnp.concatenate([inner, empty], axis=1).astype(BF)
        pieces[k * RANK : (k + 1) * RANK] = dot_tn(tails[k][:, RANK : 2 * RANK], act).astype(BF)
        start = (GROUP + k) * RANK
        pieces[start : start + RANK] = dot_tn(tails[k][:, :RANK], pre_ref[at]).astype(BF)


def down_forward(weight, ff, act, pre, cats):
    rows = cats[0].shape[0]
    total = GROUP * rows
    bundle = shape(2, rows, TAIL)
    return call(
        down_kernel,
        "down_forward",
        [bundle, bundle, shape(2 * GROUP * RANK, D)],
        (weight, act, pre, ff, *cats),
        [
            pl.BlockSpec(weight.shape, lambda i: (0, 0, 0)),
            pl.BlockSpec((total, D), lambda i: (0, 0)),
            pl.BlockSpec((total, D), lambda i: (0, 0)),
            feed_spec(0, LATE),
        ]
        + [pl.BlockSpec((rows, LANES), lambda i: (0, D // LANES))] * GROUP,
        out_specs=[pl.BlockSpec((2, rows, TAIL), lambda i: (0, 0, 0))] * 2
        + [pl.BlockSpec((2 * GROUP * RANK, D), lambda i: (0, 0))],
        micros=9,
        grid=(1,),
    )


def middle_kernel(
    keep, near, far, middle, out_grad, weight, adapters, grad_ref, packed, attn_ref, gi_up_ref, gi_o_ref
):
    shards, part, lanes = packed.shape
    wide = lanes // FOLD
    total = keep[0].astype(F32) + near[0].astype(F32) + far[...].astype(F32)
    gi_up = total[:, D : D + RANK].astype(BF)
    gi_up_ref[...] = gi_up
    grad = total[:, :D] + dot_nt(gi_up, adapters[:, ENTER_U : ENTER_U + RANK])
    second, inverse = norm_parts(middle[...])
    grad_middle = out_grad[...].astype(F32) + norm_back(grad, second, inverse)
    grad_ref[...] = grad_middle
    attn = grad_middle.astype(BF)
    attn_ref[...] = attn
    gi_o = dot(attn, adapters[:, LEAVE_O : LEAVE_O + RANK]).astype(BF)
    gi_o_ref[...] = gi_o
    context = dot_nt(attn, weight[...])
    context = (context + dot_nt(gi_o, adapters[:, ENTER_O : ENTER_O + RANK])).astype(BF)
    for s in range(shards):
        for g in range(FOLD):
            packed[s, :, g * wide : (g + 1) * wide] = context[g * part : (g + 1) * part, s * wide : (s + 1) * wide]


def middle_back(keep, near, far, middle, out_grad, weight, adapters, shards):
    rows = middle.shape[0]
    wide = D // shards
    return call(
        middle_kernel,
        "middle_backward",
        [
            shape(rows, D, dtype=F32),
            shape(shards, rows // FOLD, FOLD * wide),
            shape(rows, D),
            shape(rows, RANK),
            shape(rows, RANK),
        ],
        (keep, near, far, middle, out_grad, weight, adapters),
        [VMEM] * 7,
        micros=7,
    )


def scatter_stack(stack, natural):
    shards, height, _ = natural.shape
    wide = D // shards
    if natural.shape[2] > 3 * wide:
        natural[:, :, 3 * wide :] = jnp.zeros((shards, height, natural.shape[2] - 3 * wide), BF)
    for d in range(shards):
        for m in range(3 * height // RANK):
            piece = stack[m * RANK : (m + 1) * RANK, d * wide : (d + 1) * wide]
            natural[d, m // 3 * RANK : (m // 3 + 1) * RANK, m % 3 * wide : (m % 3 + 1) * wide] = piece


def token_kernel(meta, keep, near, far, middle, out_grad, adapters, cat, gi_up, context, gi_o, attn, inner_o, *refs):
    pieces, layer_ref, natural, stack = refs
    total = keep[0].astype(F32) + near[0].astype(F32) + far[...].astype(F32)
    inner_d = total[:, D : D + RANK].astype(BF)
    mlp = total[:, :D] + dot_nt(inner_d, adapters[:, LEAVE_D : LEAVE_D + RANK])
    layer_ref[...] = (middle[...] + mlp).astype(BF)
    width = pieces.shape[0]
    stack[:width] = pieces[...]
    pairs = ((gi_o[...], context[...]), (gi_up[...], cat[:, :D]), (inner_o[...], attn[...]), (inner_d, out_grad[...]))
    for i, (left, right) in enumerate(pairs):
        stack[width + i * RANK : width + (i + 1) * RANK] = dot_tn(left, right).astype(BF)
    scatter_stack(stack, natural)


def token_grads(meta, *args, shards):
    block = (4 * RANK, padded(3 * D // shards))
    rows = args[3].shape[0]
    return call(
        token_kernel,
        "token_adapter_grads",
        [shape(rows, D), shape(shards, *block)],
        (meta, *args),
        [SMEM] + [VMEM] * len(args),
        scratch=[pltpu.VMEM((12 * RANK, D), BF)],
        micros=4,
    )


def sum_pieces(moved, heads):
    rows = moved.shape[1] - RANK

    def kernel(moved, heads, out):
        out[:RANK] = jnp.sum(moved[:, rows:, :].astype(F32), axis=0).astype(BF)
        out[RANK:] = heads[...]

    return call(kernel, "sum_adapter_grads", [shape(2 * RANK, heads.shape[1])], (moved, heads), [VMEM] * 2)[0]


def input_kernel(meta, moved, w0, w1, w2, w3, adapters, late, hidden, grad_ref, after, out_ref, joined, kinds, *, wide):
    shards, slot = moved.shape[0], moved.shape[2]
    rows = hidden.shape[0]
    count = shards // GROUP
    for s in range(shards):
        for kind in range(3):
            kinds[kind, :, s * wide : (s + 1) * wide] = moved[s, :rows, kind * wide : (kind + 1) * wide]
    for k in range(GROUP):
        for j in range(count):
            start = (k * count + j) * slot
            joined[:, start : start + slot] = moved[(meta[PART] ^ k) * count + j, :rows]
    gis = []
    for kind in range(3):
        lanes = slice(LEAVE_QKV + kind * RANK, LEAVE_QKV + (kind + 1) * RANK)
        gis.append(dot(kinds[kind], late[:, lanes]))
    gi = jnp.concatenate(gis, axis=1).astype(BF)
    grad = dot_nt(gi, adapters[:, ENTER_QKV : ENTER_QKV + 3 * RANK])
    span = count * slot
    for k, w in enumerate((w0, w1, w2, w3)):
        grad = grad + dot_nt(joined[:, k * span : (k + 1) * span], w[...])
    first, inverse = norm_parts(hidden[...].astype(F32))
    out_ref[...] = (grad_ref[...] + norm_back(grad, first, inverse)).astype(BF)


def input_back(meta, moved, weights, adapters, ff, hidden, grad_middle, after, shards):
    rows = hidden.shape[0]
    wide = D // shards

    def kernel(*refs):
        input_kernel(*refs, wide=wide)

    return call(
        kernel,
        "input_backward",
        [shape(rows, D)],
        (meta, moved, *weights, adapters, ff, hidden, grad_middle, after),
        [SMEM]
        + [pl.BlockSpec(x.shape, lambda i, n=x.ndim: (0,) * n) for x in (moved, *weights, adapters)]
        + [feed_spec(0, LATE)]
        + [pl.BlockSpec(x.shape, lambda i: (0, 0)) for x in (hidden, grad_middle)]
        + [ANY],
        out_specs=[pl.BlockSpec((rows, D), lambda i: (0, 0))],
        scratch=[pltpu.VMEM((rows, shards * moved.shape[2]), BF), pltpu.VMEM((3, rows, D), BF)],
        micros=9,
        grid=(1,),
    )[0]


def spread_tokens_kernel(part, *refs, reps, wide):
    sets, blocks, (ao, bo, au, bu, ad, bd) = refs[:reps], refs[reps : 2 * reps], refs[2 * reps :]
    this = pl.program_id(0)
    flags = [jnp.where(sets[k][0] == this, 1.0, 0.0) for k in range(reps)]

    def one(value, m):
        row, lane = m // 3 * RANK, m % 3 * wide
        return value[row : row + RANK, lane : lane + wide]

    own = 0.0
    quarters = [0.0] * GROUP
    for k in range(reps):
        block = blocks[k][...].astype(F32)
        own = own + flags[k] * block[2 * RANK :]
        for j in range(GROUP):
            pair = jnp.concatenate([one(block, j), one(block, GROUP + j)], axis=0)
            quarters[k % GROUP] = quarters[k % GROUP] + flags[k ^ j] * pair
    ordered = by_part(part[0], quarters)
    ad[0] = jnp.concatenate([q[:RANK] for q in ordered], axis=1)
    bu[0] = jnp.concatenate([q[RANK:] for q in ordered], axis=1)
    for i, ref in enumerate((ao, au, bo, bd)):
        ref[0] = one(own, 2 + i)


def spread_heads_kernel(*refs, reps, wide):
    sets, blocks, outs = refs[:reps], refs[reps : 2 * reps], refs[2 * reps + 1 :]
    this = pl.program_id(0)
    own = 0.0
    for k in range(reps):
        own = own + jnp.where(sets[k][0] == this, 1.0, 0.0) * blocks[k][...].astype(F32)
    for kind in range(3):
        lanes = slice(kind * wide, (kind + 1) * wide)
        outs[2 * kind][0] = own[:RANK, lanes]
        outs[2 * kind + 1][0] = own[RANK:, lanes]


def spread(kernel, name, ins, scalars, blocks, kinds, micros, rest=0):
    outs = call(
        kernel,
        name,
        [shape(SETS, *k, dtype=F32) for k in kinds],
        ins,
        [SMEM] * scalars + [pl.BlockSpec(b.shape, lambda e: (0, 0)) for b in blocks] + [ANY] * rest,
        out_specs=[pl.BlockSpec((1, *k), lambda e: (e, 0, 0)) for k in kinds],
        micros=micros,
        grid=(SETS,),
    )
    return [jnp.transpose(o, (0, 2, 1)) if i % 2 == 0 else o for i, o in enumerate(outs)]


def spread_tokens(part, sets, blocks, wide):
    reps = len(blocks)
    narrow, broad = (RANK, wide), (RANK, GROUP * wide)

    def kernel(*refs):
        spread_tokens_kernel(*refs, reps=reps, wide=wide)

    kinds = [narrow] * 3 + [broad, broad, narrow]
    return spread(kernel, "spread_token_grads", (part, *sets, *blocks), 1 + reps, blocks, kinds, 5)


def spread_heads(sets, blocks, after, wide):
    reps = len(blocks)

    def kernel(*refs):
        spread_heads_kernel(*refs, reps=reps, wide=wide)

    return spread(kernel, "spread_head_grads", (*sets, *blocks, after), reps, blocks, [(RANK, wide)] * 6, 4, rest=1)


def body(
    hidden,
    out_grad,
    clip_lengths,
    adapter_index,
    w_query,
    w_key,
    w_value,
    w_output,
    w_up,
    w_down,
    a_query,
    b_query,
    a_key,
    b_key,
    a_value,
    b_value,
    a_output,
    b_output,
    a_up,
    b_up,
    a_down,
    b_down,
):
    shards = lax.axis_size("shard")
    reps = lax.axis_size("rep")
    wide = D // shards
    shard = lax.axis_index("shard")
    rep = lax.axis_index("rep")
    part = rep % GROUP

    def mate(value, flip):
        return lax.ppermute(value, "rep", [(i, i ^ flip) for i in range(reps)])

    def across(value):
        return lax.all_to_all(value, "shard", split_axis=0, concat_axis=0, tiled=True)

    def turned(table):
        return jnp.transpose(table, (0, 2, 1))

    def group_gather(value):
        other = mate(value, 2)
        return [value, mate(value, 1), other, mate(other, 1)]

    place = jnp.where(shard % 2 == 0, shard // 2, shards - 1 - shard // 2)
    meta = jnp.stack([shard, part, clip_lengths[0], rep & 1, place]).astype(jnp.int32)
    part_only = part[None].astype(jnp.int32)
    sets = [adapter_index] + [mate(adapter_index, flip) for flip in range(1, reps)]
    enters = [turned(t) for t in (a_query, a_key, a_value)]
    leaves = [b_query, b_key, b_value]

    narrow = enters + [turned(a_output), turned(a_up), b_output, b_down]
    bundle = pack_first(adapter_index, meta, hidden, w_output, narrow)
    cols, halves = pack_columns(meta, (w_query, w_key, w_value), bundle, shards)
    feed = pack_feed(sets[:GROUP], part_only, w_up, w_down, leaves, turned(a_down), b_up, bundle, shards)
    cols = across(cols)
    held = {}

    def between(k, arrivals):
        if k == 1:
            return lax.optimization_barrier((*arrivals, halves, feed))[:2]
        if k == 2:
            below, above, held["cols"] = lax.optimization_barrier((*arrivals, cols))
            return below, above
        if k == shards // 2 - 1:
            below, above, held["feed"] = lax.optimization_barrier((*arrivals, feed))
            return below, above
        return lax.optimization_barrier(arrivals)

    pieces = ring_pieces(bundle, shards, between)
    cols = held["cols"]
    cols_mate = mate(cols, 1)
    grads_out = group_gather(out_grad)

    first, qkv, inner_qkv, adapters, out_quarter = project_qkv(meta, adapter_index, cols, cols_mate, pieces, leaves)
    stage = {}

    def down_between(k, arrivals):
        if k == 1:
            below, above, stage["qkv"] = lax.optimization_barrier((*arrivals, qkv))
            stage["out_weight"] = assemble_output(meta, group_gather(out_quarter))
            packed, stage["ctx"], stage["lse"] = attend(stage["qkv"], shards)
            stage["packed"] = packed
            return below, above
        if k == 2:
            below, above, stage["moved"] = lax.optimization_barrier((*arrivals, across(stage["packed"])))
            return below, above
        return lax.optimization_barrier(arrivals)

    feed_pieces = ring_pieces(held["feed"], shards, down_between)
    qkv, ctx, lse, out_weight = stage["qkv"], stage["ctx"], stage["lse"], stage["out_weight"]
    context, middle, cat, inner_o = project_output(stage["moved"], out_weight, adapters, hidden, out_grad)
    halves, last = lax.optimization_barrier((halves, feed_pieces[-1][0]))
    feed_pieces[-1] = (last, *feed_pieces[-1][1:])
    qkv_quarter = lax.all_gather(halves, "shard", axis=0, tiled=True)

    grad_act, down_weight = down_back(meta, feed_pieces, grads_out)
    other = mate(cat, 2)
    other, grad_act = lax.optimization_barrier((other, grad_act))
    cats = [cat, mate(cat, 1), other, mate(other, 1)]
    act, pre, keep, give, late = up_both(meta, feed_pieces, grad_act, cats)

    def near_sum(keep, give):
        near = mate(give, 1)
        return near, (keep[1].astype(F32) + near[1].astype(F32)).astype(BF)

    near, far = near_sum(keep, give)
    far = mate(far, 2)
    keep_d, give_d, pieces_d = down_forward(down_weight, late, act, pre, cats)
    give_d, far = lax.optimization_barrier((give_d, far))
    near_d, far_d = near_sum(keep_d, give_d)
    far_d = mate(far_d, 2)
    grad_middle, dctx, attn, gi_up, gi_o = middle_back(
        keep, near, far, middle, out_grad, out_weight, adapters, shards
    )
    dctx_moved = across(dctx)
    layer_out, token_pieces = token_grads(
        meta, keep_d, near_d, far_d, middle, out_grad, adapters, cat, gi_up, context, gi_o, attn, inner_o, pieces_d,
        shards=shards,
    )
    early = across(token_pieces)
    qkv_quarter, token_pieces = lax.optimization_barrier((qkv_quarter, token_pieces))
    qkv_weights = group_gather(qkv_quarter)
    lse_rows = lse.reshape(lse.shape[0], 1, lse.shape[1])
    dqkv, head_out = attend_back(
        adapter_index, qkv, dctx_moved, ctx, lse_rows, first, inner_qkv, leaves, token_pieces, shards
    )
    dqkv, early = lax.optimization_barrier((dqkv, early))
    dqkv_moved = across(dqkv)

    def over_reps(value):
        return [value] + [mate(value, flip) for flip in range(1, reps)]

    early = jnp.sum(early.astype(F32), axis=0).astype(BF)
    token_outs = spread_tokens(part_only, sets, over_reps(early), wide)
    summed = sum_pieces(dqkv_moved, head_out)
    input_grad = input_back(
        meta, dqkv_moved, qkv_weights, adapters, late, hidden, grad_middle, token_outs[1], shards
    )
    outs = spread_heads(sets, over_reps(summed), input_grad, wide) + token_outs
    return (layer_out, input_grad, *outs)


def solution(mesh):
    rows = P("shard", None)
    enter = P(None, "shard", None)
    leave = P(None, None, "shard")
    tokens = P(("rep", "shard"), None)
    return jax.shard_map(
        body,
        mesh=mesh,
        in_specs=(tokens, tokens, P("rep"), P("rep")) + (rows,) * 6 + (enter, leave) * 6,
        out_specs=(tokens, tokens) + (enter, leave) * 6,
        check_vma=False,
    )
```

```python
import jax
import jax.numpy as jnp
from jax import lax
from jax.experimental import pallas as pl
from jax.experimental.pallas import tpu as pltpu
from jax.sharding import PartitionSpec as P

D = 1280
FF = 5120
HEADS = 16
HEAD = 80
LANES = 128
RANK = 16
SETS = 8
GROUP = 4
FOLD = 4
CHUNK = 256
BLOCK_Q = 384
TAIL = D + LANES
RATE = 1.15e9

EPSILON = 1e-05
NEGATIVE = -1e30
LOG2E = 1.4426950408889634
SCALE = HEAD ** (-0.5)
ONE_LANE = HEAD
MASK_LANE = HEAD + 1

BF = jnp.bfloat16
F32 = jnp.float32

QUARTER = D // GROUP
ENTER_QKV = 0
ENTER_O = 48
ENTER_U = 64
LEAVE_O = 80
LEAVE_D = 96
FIRST = 128
BESIDE = 512
BUNDLE = D + BESIDE

ENTER_D = 0
LEAVE_U = 64
LEAVE_QKV = 128
LATE = 256

SHARD, PART, LENGTH, CORE, RING = range(5)

VMEM = pl.BlockSpec(memory_space=pltpu.VMEM)
SMEM = pl.BlockSpec(memory_space=pltpu.SMEM)
ANY = pl.BlockSpec(memory_space=pl.ANY)


def dot(left, right):
    return jnp.dot(left, right, preferred_element_type=F32)


def dot_nt(left, right):
    return lax.dot_general(left, right, (((1,), (1,)), ((), ())), preferred_element_type=F32)


def dot_tn(left, right):
    return lax.dot_general(left, right, (((0,), (0,)), ((), ())), preferred_element_type=F32)


def norm_parts(values):
    center = values - jnp.mean(values, axis=-1, keepdims=True)
    spread = jnp.mean(center * center, axis=-1, keepdims=True)
    inverse = lax.rsqrt(spread + EPSILON)
    return center * inverse, inverse


def norm_back(grad, normal, inverse):
    average = jnp.mean(grad, axis=-1, keepdims=True)
    along = jnp.mean(grad * normal, axis=-1, keepdims=True)
    return inverse * (grad - average - normal * along)


def cost(micros):
    return pl.CostEstimate(flops=int(micros * RATE), transcendentals=0, bytes_accessed=0)


def call(kernel, name, outs, ins, specs, out_specs=None, scratch=(), micros=1.0, **rest):
    return pl.pallas_call(
        kernel,
        out_shape=outs,
        in_specs=specs,
        out_specs=[VMEM] * len(outs) if out_specs is None else out_specs,
        scratch_shapes=list(scratch),
        compiler_params=pltpu.CompilerParams(vmem_limit_bytes=56 << 20),
        cost_estimate=cost(micros),
        name=name,
        **rest,
    )(*ins)


def shape(*dims, dtype=BF):
    return jax.ShapeDtypeStruct(dims, dtype)


def padded(size):
    return -(-size // LANES) * LANES


def column_blocks(wq, wk, wv, shards):
    wide = D // shards
    pad = jnp.zeros((wide, padded(3 * wide) - 3 * wide), BF)
    for s in range(shards):
        at = slice(s * wide, (s + 1) * wide)
        yield s, jnp.concatenate([wq[:, at], wk[:, at], wv[:, at], pad], axis=1)


def pack_columns(meta, weights, after, shards):
    wide = D // shards
    slot = padded(3 * wide)
    count = shards // GROUP

    def kernel(meta, wq, wk, wv, after, cols, quarter):
        for s, block in column_blocks(wq, wk, wv, shards):
            cols[s] = jnp.where(meta[CORE] == 0, block[:, : slot // 2], block[:, slot // 2 :])

            @pl.when(meta[PART] == s // count)
            def _():
                quarter[:, s % count * slot : (s % count + 1) * slot] = block

    outs = [shape(shards, wide, slot // 2), shape(wide, count * slot)]
    return call(kernel, "pack_columns", outs, (meta, *weights, after), [SMEM] + [VMEM] * 3 + [ANY], micros=3)


def unit(size):
    row = lax.broadcasted_iota(jnp.int32, (size, size), 0)
    col = lax.broadcasted_iota(jnp.int32, (size, size), 1)
    return (row == col).astype(BF)


def pack_first(chosen, meta, hidden, w_output, narrow):
    rows = hidden.shape[0]
    wide = narrow[0].shape[2]

    def kernel(chosen, meta, hidden, w_output, *refs):
        out = refs[-1]
        eye = unit(wide)
        out[:, :D] = hidden[...]
        out[:, D:] = jnp.zeros((rows, BESIDE), BF)
        for i, ref in enumerate(refs[:-1]):
            out[:wide, D + i * RANK : D + (i + 1) * RANK] = dot_nt(eye, ref[...]).astype(BF)
        for p in range(GROUP):

            @pl.when(meta[PART] == p)
            def _():
                out[:wide, D + FIRST : D + FIRST + QUARTER] = w_output[:, p * QUARTER : (p + 1) * QUARTER]

    return pl.pallas_call(
        kernel,
        out_shape=shape(rows, BUNDLE),
        grid_spec=pltpu.PrefetchScalarGridSpec(
            num_scalar_prefetch=1,
            grid=(1,),
            in_specs=[SMEM, pl.BlockSpec((rows, D), lambda i, m: (0, 0)), pl.BlockSpec((wide, D), lambda i, m: (0, 0))]
            + [pl.BlockSpec((None, RANK, wide), lambda i, m: (m[0], 0, 0))] * len(narrow),
            out_specs=pl.BlockSpec((rows, BUNDLE), lambda i, m: (0, 0)),
        ),
        cost_estimate=cost(3),
        name="pack_first",
    )(chosen, meta, hidden, w_output, *narrow)


def feed_kernel(*refs, wide, shards):
    part = refs[GROUP][0]
    (w_up, w_down), maps, (out, sem) = refs[GROUP + 1 : GROUP + 3], refs[GROUP + 3 : -3], refs[-2:]
    narrow, downs, ups = maps[:3], maps[3:7], maps[7:11]
    copy = pltpu.make_async_copy(w_down.at[part], out.at[:, pl.ds(D, D)], sem)
    copy.start()
    eye = unit(wide)
    beside = 2 * D
    for i, ref in enumerate(narrow):
        start = beside + LEAVE_QKV + i * RANK
        out[:, start : start + RANK] = dot_nt(eye, ref[...]).astype(BF)
    end = beside + LEAVE_QKV + 3 * RANK
    out[:, end:] = jnp.zeros((wide, 2 * D + LATE - end), BF)
    for p in range(GROUP):

        @pl.when(part == p)
        def _():
            at = slice(p * wide, (p + 1) * wide)
            for i, ref in enumerate(downs):
                start = beside + ENTER_D + i * RANK
                out[:, start : start + RANK] = dot_nt(eye, ref[:, at]).astype(BF)
            for i, ref in enumerate(ups):
                start = beside + LEAVE_U + i * RANK
                out[:, start : start + RANK] = dot_nt(eye, ref[:, at]).astype(BF)
            for s in range(shards):
                start = (s * GROUP + p) * wide
                out[:, s * wide : (s + 1) * wide] = w_up[:, start : start + wide]

    copy.wait()


def pack_feed(sets, part, w_up, w_down, narrow, a_down, b_up, after, shards):
    wide = D // shards
    ff_wide = GROUP * wide
    width = 2 * D + LATE

    def at(k):
        return lambda i, *m: (m[k][0], 0, 0)

    specs = (
        [pl.BlockSpec((wide, FF), lambda i, *m: (0, 0)), ANY]
        + [pl.BlockSpec((None, RANK, wide), at(0))] * 3
        + [pl.BlockSpec((None, RANK, ff_wide), at(k)) for k in range(GROUP)] * 2
        + [ANY]
    )

    def kernel(*refs):
        feed_kernel(*refs, wide=wide, shards=shards)

    return pl.pallas_call(
        kernel,
        out_shape=shape(wide, width),
        grid_spec=pltpu.PrefetchScalarGridSpec(
            num_scalar_prefetch=GROUP + 1,
            grid=(1,),
            in_specs=specs,
            out_specs=pl.BlockSpec((wide, width), lambda i, *m: (0, 0)),
            scratch_shapes=[pltpu.SemaphoreType.DMA],
        ),
        cost_estimate=cost(5),
        name="pack_feed",
    )(*sets, part, w_up, w_down.reshape(GROUP, wide, D), *narrow, *[a_down] * GROUP, *[b_up] * GROUP, after)


def ring_shard(place, shards):
    return jnp.where(place < shards // 2, 2 * place, 2 * (shards - 1 - place) + 1)


def ring_pieces(value, shards, between):
    places = [2 * i if i < shards // 2 else 2 * (shards - 1 - i) + 1 for i in range(shards)]
    onward = [(places[i], places[(i + 1) % shards]) for i in range(shards)]
    back = [(b, a) for a, b in onward]
    half = value.shape[0] // 2
    pieces = [(value, 0, 0)]
    below, above = value, value
    for k in range(1, shards // 2):
        below = lax.ppermute(below, "shard", onward)
        above = lax.ppermute(above, "shard", back)
        below, above = between(k, (below, above))
        pieces += [(below, -k, 0), (above, k, 0)]
    far = shards // 2
    pieces.append((lax.ppermute(below[:half], "shard", onward), far, 0))
    pieces.append((lax.ppermute(above[half:], "shard", back), far, half))
    return pieces


def piece_shard(meta, step, shards):
    return ring_shard((meta[RING] + step + shards) % shards, shards)


def place_pieces(meta, pieces, steps, target, sems, column=None):
    shards = target.shape[0]
    copies = []
    for i, (ref, (step, start)) in enumerate(zip(pieces, steps)):
        if column is not None:
            ref = ref.at[:, pl.ds(column, target.shape[2])]
        block = target.at[piece_shard(meta, step, shards), pl.ds(start, ref.shape[0])]
        copies.append(pltpu.make_async_copy(ref, block, sems.at[i]))
    for copy in copies:
        copy.start()
    for copy in copies:
        copy.wait()


def qkv_kernel(meta, w_mine, w_mate, *refs, shards, steps):
    count = len(steps)
    pieces, leaves = refs[:count], refs[count : count + 3]
    first_ref, qkv_ref, inner_ref, enter, quarter, hid, sems = refs[-7:]
    wide = D // shards
    heads_here = HEADS // shards
    slot = padded(3 * wide)
    side = meta[CORE]
    rows = hid.shape[1]
    place_pieces(meta, pieces, steps, hid, sems)
    for s in range(shards):
        enter[s * wide : (s + 1) * wide, :] = hid[s, :wide, D : D + FIRST]
        quarter[s * wide : (s + 1) * wide, :] = hid[s, :wide, D + FIRST : D + FIRST + QUARTER]
    lane = lax.broadcasted_iota(jnp.int32, (rows, LANES - HEAD), 1)
    spot = lax.broadcasted_iota(jnp.int32, (rows, LANES - HEAD), 0)

    def step(s, carry):
        at = pl.ds(pl.multiple_of(s * rows, 64), rows)
        first = norm_parts(hid[s, :, :D].astype(F32))[0].astype(BF)
        first_ref[at, :] = first
        inner = dot(first, enter[:, : 3 * RANK]).astype(BF)
        inner_ref[at, :] = inner
        y_mine = dot(first, w_mine[...].reshape(D, slot // 2))
        y_mate = dot(first, w_mate[...].reshape(D, slot // 2))
        lo = jnp.where(side == 0, y_mine, y_mate)
        hi = jnp.where(side == 0, y_mate, y_mine)
        y = jnp.concatenate([lo, hi], axis=1)
        hidden_key = jnp.where((spot + s * rows < meta[LENGTH]) | (lane != MASK_LANE - HEAD), 0.0, NEGATIVE)
        for kind in range(3):
            lanes = slice(kind * RANK, (kind + 1) * RANK)
            out = y[:, kind * wide : (kind + 1) * wide] + dot(inner[:, lanes], leaves[kind][...])
            if kind == 0:
                tail = jnp.where(lane == MASK_LANE - HEAD, 1.0, 0.0)
            elif kind == 1:
                tail = hidden_key
            else:
                tail = jnp.where(lane == ONE_LANE - HEAD, 1.0, 0.0)
            for h in range(heads_here):
                base = (kind * heads_here + h) * LANES
                head = jnp.concatenate([out[:, h * HEAD : (h + 1) * HEAD], tail], axis=1)
                qkv_ref[at, base : base + LANES] = head.astype(BF)
        return carry

    lax.fori_loop(0, shards, step, 0, unroll=True)


def project_qkv(meta, chosen, w_mine, w_mate, pieces, leaves):
    shards = len(pieces) - 1
    steps = [p[1:] for p in pieces]
    rows = pieces[0][0].shape[0]
    seq_len = rows * shards
    lanes = HEADS // shards * LANES
    wide = D // shards
    weight = pl.BlockSpec(w_mine.shape, lambda i, c: (0, 0, 0))
    outs = [
        shape(seq_len, D),
        shape(seq_len, 3 * lanes),
        shape(seq_len, 3 * RANK),
        shape(D, FIRST),
        shape(D, QUARTER),
    ]

    def kernel(chosen, *refs):
        qkv_kernel(*refs, shards=shards, steps=steps)

    return pl.pallas_call(
        kernel,
        out_shape=outs,
        grid_spec=pltpu.PrefetchScalarGridSpec(
            num_scalar_prefetch=1,
            grid=(1,),
            in_specs=[SMEM, weight, weight]
            + [ANY] * len(pieces)
            + [pl.BlockSpec((None, RANK, wide), lambda i, c: (c[0], 0, 0))] * 3,
            out_specs=[pl.BlockSpec(o.shape, lambda i, c: (0, 0)) for o in outs],
            scratch_shapes=[
                pltpu.VMEM((shards, rows, BUNDLE), BF),
                pltpu.SemaphoreType.DMA((len(pieces),)),
            ],
        ),
        compiler_params=pltpu.CompilerParams(vmem_limit_bytes=56 << 20),
        cost_estimate=cost(14),
        name="project_qkv",
    )(chosen, meta, w_mine, w_mate, *[p[0] for p in pieces], *leaves)


def forward_kernel(qkv_ref, packed_ref, ctx_ref, lse_ref, *, heads_here, wide, block):
    shards, part, _ = packed_ref.shape
    seq_len = ctx_ref.shape[0]
    factor = SCALE * LOG2E

    def step(i, carry):
        at = pl.ds(pl.multiple_of(i * block, 64), block)
        for h in range(heads_here):
            queries = qkv_ref[at, h * LANES : (h + 1) * LANES]
            keys = qkv_ref[:, (heads_here + h) * LANES : (heads_here + h + 1) * LANES]
            values = qkv_ref[:, (2 * heads_here + h) * LANES : (2 * heads_here + h + 1) * LANES]
            scores = dot_nt(queries, keys)
            highest = jnp.max(scores, axis=1, keepdims=True)
            weights = jnp.exp2((scores - highest) * factor).astype(BF)
            portion = dot(weights, values)
            total = portion[:, ONE_LANE : ONE_LANE + 1]
            ctx_ref[at, h * LANES : (h + 1) * LANES] = (portion / total).astype(BF)
            lse_ref[h, at, :] = highest * factor + jnp.log2(total)
        return carry

    lax.fori_loop(0, seq_len // block, step, 0, unroll=True)
    for h in range(heads_here):
        for d in range(shards):
            for g in range(FOLD):
                start = g * wide + h * HEAD
                row = (d * FOLD + g) * part
                packed_ref[d, :, start : start + HEAD] = ctx_ref[row : row + part, h * LANES : h * LANES + HEAD]


def attend(qkv, shards):
    seq_len = qkv.shape[0]
    rows = seq_len // shards
    heads_here = HEADS // shards
    lanes = heads_here * LANES
    wide = D // shards

    def kernel(*refs):
        forward_kernel(*refs, heads_here=heads_here, wide=wide, block=BLOCK_Q)

    return call(
        kernel,
        "attention_forward",
        [
            shape(shards, rows // FOLD, FOLD * wide),
            shape(seq_len, lanes),
            shape(heads_here, seq_len, 1, dtype=F32),
        ],
        (qkv,),
        [VMEM],
        micros=12,
    )


def backward_kernel(
    qkv_ref, moved_ref, ctx_ref, lse_ref, first, inner, leave_q, leave_k, leave_v, out_ref, heads_ref, douts, delta, acc, turned,
    *, heads_here, wide, block
):
    shards = moved_ref.shape[0]
    seq_len = qkv_ref.shape[0]
    rows = seq_len // shards
    part = rows // FOLD
    slot = out_ref.shape[2]
    for d in range(shards):
        for g in range(FOLD):
            base = d * rows + g * part
            for h in range(heads_here):
                start = g * wide + h * HEAD
                piece = moved_ref[d, :, start : start + HEAD]
                douts[base : base + part, h * LANES : h * LANES + HEAD] = piece
    for h in range(heads_here):
        douts[:, h * LANES + HEAD : (h + 1) * LANES] = jnp.zeros((seq_len, LANES - HEAD), BF)
    ones = jnp.ones((8, LANES), F32)
    if slot > 3 * wide:
        out_ref[:, :, 3 * wide :] = jnp.zeros((shards, rows + RANK, slot - 3 * wide), BF)
    for h in range(heads_here):
        lanes = slice(h * LANES, (h + 1) * LANES)
        product = douts[:, lanes].astype(F32) * ctx_ref[:, lanes].astype(F32)
        delta[...] = lax.dot_general(
            ones, product, (((1,), (1,)), ((), ())), precision=lax.Precision.HIGHEST, preferred_element_type=F32
        )
        queries = qkv_ref[:, lanes]
        grads = douts[:, lanes]

        def step(i, carry):
            at = pl.ds(pl.multiple_of(i * block, block), block)
            keys = qkv_ref[at, (heads_here + h) * LANES : (heads_here + h + 1) * LANES]
            values = qkv_ref[at, (2 * heads_here + h) * LANES : (2 * heads_here + h + 1) * LANES]
            scores = dot_nt(keys, queries)
            weights = jnp.exp2(scores * (SCALE * LOG2E) - lse_ref[h])
            grad_weights = dot_nt(values, grads)
            grad_scores = (weights * (grad_weights - delta[0:1, :])).astype(BF)
            acc[2, at, :] = dot(weights.astype(BF), grads)
            acc[1, at, :] = dot(grad_scores, queries) * SCALE
            moved = dot_tn(keys, grad_scores)

            @pl.when(i == 0)
            def _():
                turned[...] = moved

            @pl.when(i > 0)
            def _():
                turned[...] += moved

            return carry

        lax.fori_loop(0, seq_len // block, step, 0, unroll=True)
        acc[0] = jnp.transpose(turned[...])
        for kind in range(3):
            start = kind * wide + h * HEAD
            for d in range(shards):
                piece = acc[kind, d * rows : (d + 1) * rows, :HEAD]
                if kind == 0:
                    piece = piece * SCALE
                out_ref[d, :rows, start : start + HEAD] = piece.astype(BF)
    heads_ref[...] = jnp.zeros_like(heads_ref)
    parts = []
    for kind, leave in enumerate((leave_q, leave_k, leave_v)):
        grad = out_ref[:, :rows, kind * wide : (kind + 1) * wide].reshape(seq_len, wide)
        lanes = slice(kind * RANK, (kind + 1) * RANK)
        parts.append(dot_nt(grad, leave[...]))
        heads_ref[:, kind * wide : (kind + 1) * wide] = dot_tn(inner[:, lanes], grad).astype(BF)
    entered = dot_tn(jnp.concatenate(parts, axis=1).astype(BF), first[...]).astype(BF)
    for kind in range(3):
        for d in range(shards):
            piece = entered[kind * RANK : (kind + 1) * RANK, d * wide : (d + 1) * wide]
            out_ref[d, rows:, kind * wide : (kind + 1) * wide] = piece


def attend_back(chosen, qkv, moved, ctx, lse, first, inner, leaves, after, shards):
    seq_len = qkv.shape[0]
    rows = seq_len // shards
    heads_here = HEADS // shards
    lanes = heads_here * LANES
    wide = D // shards
    outs = [shape(shards, rows + RANK, padded(3 * wide)), shape(RANK, padded(3 * wide))]

    def kernel(chosen, *refs):
        backward_kernel(*refs[:9], *refs[10:], heads_here=heads_here, wide=wide, block=512)

    def whole(array):
        return pl.BlockSpec(array.shape, lambda i, c: (0,) * len(array.shape))

    return pl.pallas_call(
        kernel,
        out_shape=outs,
        grid_spec=pltpu.PrefetchScalarGridSpec(
            num_scalar_prefetch=1,
            grid=(1,),
            in_specs=[whole(x) for x in (qkv, moved, ctx, lse, first, inner)]
            + [pl.BlockSpec((None, RANK, wide), lambda i, c: (c[0], 0, 0))] * 3
            + [ANY],
            out_specs=[whole(o) for o in outs],
            scratch_shapes=[
                pltpu.VMEM((seq_len, lanes), BF),
                pltpu.VMEM((8, seq_len), F32),
                pltpu.VMEM((3, seq_len, LANES), F32),
                pltpu.VMEM((LANES, seq_len), F32),
            ],
        ),
        compiler_params=pltpu.CompilerParams(vmem_limit_bytes=56 << 20),
        cost_estimate=cost(24),
        name="attention_backward",
    )(chosen, qkv, moved, ctx, lse, first, inner, *leaves, after)


def by_part(part, values):
    ordered = []
    for b in range(GROUP):
        total = values[0]
        for k in range(1, GROUP):
            total = jnp.where((part ^ k) == b, values[k], total)
        ordered.append(total)
    return ordered


def assemble_output(meta, weights):
    def kernel(meta, *refs):
        out = refs[-1]
        for k in range(GROUP):
            for b in range(GROUP):

                @pl.when((meta[PART] ^ k) == b)
                def _():
                    out[:, b * QUARTER : (b + 1) * QUARTER] = refs[k][...]

    return call(kernel, "assemble_output", [shape(D, D)], (meta, *weights), [SMEM] + [VMEM] * GROUP, micros=3)[0]


def output_kernel(moved, weight, adapters, hidden, out_grad, *refs):
    ctx_ref, middle_ref, cat_ref, inner_ref = refs[-4:]
    shards, part, lanes = moved.shape
    wide = lanes // FOLD
    for s in range(shards):
        for g in range(FOLD):
            ctx_ref[g * part : (g + 1) * part, s * wide : (s + 1) * wide] = moved[s, :, g * wide : (g + 1) * wide]
    context = ctx_ref[...]
    inner = dot(context, adapters[:, ENTER_O : ENTER_O + RANK]).astype(BF)
    inner_ref[...] = inner
    branch = dot(context, weight[...]) + dot_nt(inner, adapters[:, LEAVE_O : LEAVE_O + RANK])
    middle = hidden[...].astype(F32) + branch
    middle_ref[...] = middle
    second = norm_parts(middle)[0].astype(BF)
    cat_ref[:, :D] = second
    inner_u = dot(second, adapters[:, ENTER_U : ENTER_U + RANK])
    gi_down = dot(out_grad[...], adapters[:, LEAVE_D : LEAVE_D + RANK])
    empty = jnp.zeros((second.shape[0], LANES - 2 * RANK), F32)
    cat_ref[:, D:] = jnp.concatenate([inner_u, gi_down, empty], axis=1).astype(BF)


def project_output(moved, weight, adapters, hidden, out_grad):
    rows = hidden.shape[0]
    return call(
        output_kernel,
        "project_output",
        [shape(rows, D), shape(rows, D, dtype=F32), shape(rows, TAIL), shape(rows, RANK)],
        (moved, weight, adapters, hidden, out_grad),
        [VMEM] * 5,
        micros=6,
    )


def feed_spec(index, width=D):
    return pl.BlockSpec((D, width), lambda i: (0, index))


def down_back(meta, pieces, grads):
    arrays = [p[0] for p in pieces]
    steps = [p[1:] for p in pieces]
    count = len(arrays)
    shards, wide = count - 1, arrays[0].shape[0]
    rows = grads[0].shape[0]

    def kernel(meta, *refs):
        given, (out, weight, joined, sems) = refs[count : count + GROUP], refs[count + GROUP :]
        for k in range(GROUP):
            joined[k * rows : (k + 1) * rows] = given[k][...]
        place_pieces(meta, refs[:count], steps, weight, sems, D)
        for n in range(D // CHUNK):
            at = slice(n * CHUNK, (n + 1) * CHUNK)
            out[:, at] = dot_nt(joined[...], weight[...].reshape(D, D)[at, :]).astype(BF)

    return call(
        kernel,
        "down_backward",
        [shape(GROUP * rows, D), shape(shards, wide, D)],
        (meta, *arrays, *grads),
        [SMEM] + [ANY] * count + [VMEM] * GROUP,
        scratch=[pltpu.VMEM((GROUP * rows, D), BF), pltpu.SemaphoreType.DMA((count,))],
        micros=7,
    )


def up_kernel(meta, *refs, steps):
    count = len(steps)
    pieces, grad_ref, cats = refs[:count], refs[count], refs[count + 1 : count + 1 + GROUP]
    act_ref, pre_ref, keep, send, late, joined, w_ref, late_ref, sems, late_sems = refs[count + 1 + GROUP :]
    rows = cats[0].shape[0]
    place_pieces(meta, pieces, steps, w_ref, sems, 0)
    place_pieces(meta, pieces, steps, late_ref, late_sems, 2 * D)
    late[...] = late_ref[...].reshape(D, LATE)
    adapters = late
    for k in range(GROUP):
        joined[k * rows : (k + 1) * rows] = cats[k][:, :D]

    def step(n, carry):
        lanes = pl.ds(pl.multiple_of(n * CHUNK, CHUNK), CHUNK)
        weight = w_ref[:, :, lanes].reshape(D, CHUNK)
        pre = dot(joined[...], weight)
        extra, extra_grad = [], []
        for k in range(GROUP):
            leave = adapters[lanes, LEAVE_U + k * RANK : LEAVE_U + (k + 1) * RANK]
            enter = adapters[lanes, ENTER_D + k * RANK : ENTER_D + (k + 1) * RANK]
            extra.append(dot_nt(cats[k][:, D : D + RANK], leave))
            extra_grad.append(dot_nt(cats[k][:, D + RANK : D + 2 * RANK], enter))
        pre = pre + jnp.concatenate(extra, axis=0)
        grad = grad_ref[:, lanes].astype(F32) + jnp.concatenate(extra_grad, axis=0)
        cumulative = 0.5 * (1.0 + lax.erf(pre * (0.5**0.5)))
        density = jnp.exp2(pre * pre * (-0.5 * LOG2E)) * 0.3989422804014327
        act_ref[:, lanes] = (pre * cumulative).astype(BF)
        pre_ref[:, lanes] = (grad * (cumulative + pre * density)).astype(BF)
        return carry

    lax.fori_loop(0, D // CHUNK, step, 0, unroll=True)
    for n in range(D // CHUNK):
        lanes = slice(n * CHUNK, (n + 1) * CHUNK)
        total = dot_nt(pre_ref[...], w_ref[...].reshape(D, D)[lanes, :]).astype(BF)
        for k in range(GROUP):
            target = send if k % 2 else keep
            target[k // 2, :, lanes] = total[k * rows : (k + 1) * rows]
    for k in range(GROUP):
        target = send if k % 2 else keep
        at = slice(k * rows, (k + 1) * rows)
        gi = dot(pre_ref[at], adapters[:, LEAVE_U + k * RANK : LEAVE_U + (k + 1) * RANK])
        empty = jnp.zeros((rows, LANES - RANK), F32)
        target[k // 2, :, D:] = jnp.concatenate([gi, empty], axis=1).astype(BF)


def up_both(meta, pieces, grad, cats):
    arrays = [p[0] for p in pieces]
    steps = [p[1:] for p in pieces]
    count = len(arrays)
    shards, wide = count - 1, arrays[0].shape[0]
    rows = cats[0].shape[0]
    total = GROUP * rows
    bundle = shape(2, rows, TAIL)

    def kernel(*refs):
        up_kernel(*refs, steps=steps)

    return call(
        kernel,
        "up_forward_backward",
        [shape(total, D), shape(total, D), bundle, bundle, shape(D, LATE)],
        (meta, *arrays, grad, *cats),
        [SMEM] + [ANY] * count + [VMEM] * (1 + GROUP),
        scratch=[
            pltpu.VMEM((total, D), BF),
            pltpu.VMEM((shards, wide, D), BF),
            pltpu.VMEM((shards, wide, LATE), BF),
            pltpu.SemaphoreType.DMA((count,)),
            pltpu.SemaphoreType.DMA((count,)),
        ],
        micros=12,
    )


def down_kernel(w_ref, act_ref, pre_ref, adapters, *refs):
    tails, (keep, send, pieces) = refs[:GROUP], refs[GROUP:]
    rows = tails[0].shape[0]
    for n in range(D // CHUNK):
        lanes = slice(n * CHUNK, (n + 1) * CHUNK)
        total = dot(act_ref[...], w_ref[:, :, lanes].reshape(D, CHUNK)).astype(BF)
        for k in range(GROUP):
            target = send if k % 2 else keep
            target[k // 2, :, lanes] = total[k * rows : (k + 1) * rows]
    for k in range(GROUP):
        target = send if k % 2 else keep
        at = slice(k * rows, (k + 1) * rows)
        act = act_ref[at]
        inner = dot(act, adapters[:, ENTER_D + k * RANK : ENTER_D + (k + 1) * RANK])
        empty = jnp.zeros((rows, LANES - RANK), F32)
        target[k // 2, :, D:] = jnp.concatenate([inner, empty], axis=1).astype(BF)
        pieces[k * RANK : (k + 1) * RANK] = dot_tn(tails[k][:, RANK : 2 * RANK], act).astype(BF)
        start = (GROUP + k) * RANK
        pieces[start : start + RANK] = dot_tn(tails[k][:, :RANK], pre_ref[at]).astype(BF)


def down_forward(weight, ff, act, pre, cats):
    rows = cats[0].shape[0]
    total = GROUP * rows
    bundle = shape(2, rows, TAIL)
    return call(
        down_kernel,
        "down_forward",
        [bundle, bundle, shape(2 * GROUP * RANK, D)],
        (weight, act, pre, ff, *cats),
        [
            pl.BlockSpec(weight.shape, lambda i: (0, 0, 0)),
            pl.BlockSpec((total, D), lambda i: (0, 0)),
            pl.BlockSpec((total, D), lambda i: (0, 0)),
            feed_spec(0, LATE),
        ]
        + [pl.BlockSpec((rows, LANES), lambda i: (0, D // LANES))] * GROUP,
        out_specs=[pl.BlockSpec((2, rows, TAIL), lambda i: (0, 0, 0))] * 2
        + [pl.BlockSpec((2 * GROUP * RANK, D), lambda i: (0, 0))],
        micros=9,
        grid=(1,),
    )


def middle_kernel(
    keep, near, far, middle, out_grad, weight, adapters, grad_ref, packed, attn_ref, gi_up_ref, gi_o_ref
):
    shards, part, lanes = packed.shape
    wide = lanes // FOLD
    total = keep[0].astype(F32) + near[0].astype(F32) + far[...].astype(F32)
    gi_up = total[:, D : D + RANK].astype(BF)
    gi_up_ref[...] = gi_up
    grad = total[:, :D] + dot_nt(gi_up, adapters[:, ENTER_U : ENTER_U + RANK])
    second, inverse = norm_parts(middle[...])
    grad_middle = out_grad[...].astype(F32) + norm_back(grad, second, inverse)
    grad_ref[...] = grad_middle
    attn = grad_middle.astype(BF)
    attn_ref[...] = attn
    gi_o = dot(attn, adapters[:, LEAVE_O : LEAVE_O + RANK]).astype(BF)
    gi_o_ref[...] = gi_o
    context = dot_nt(attn, weight[...])
    context = (context + dot_nt(gi_o, adapters[:, ENTER_O : ENTER_O + RANK])).astype(BF)
    for s in range(shards):
        for g in range(FOLD):
            packed[s, :, g * wide : (g + 1) * wide] = context[g * part : (g + 1) * part, s * wide : (s + 1) * wide]


def middle_back(keep, near, far, middle, out_grad, weight, adapters, shards):
    rows = middle.shape[0]
    wide = D // shards
    return call(
        middle_kernel,
        "middle_backward",
        [
            shape(rows, D, dtype=F32),
            shape(shards, rows // FOLD, FOLD * wide),
            shape(rows, D),
            shape(rows, RANK),
            shape(rows, RANK),
        ],
        (keep, near, far, middle, out_grad, weight, adapters),
        [VMEM] * 7,
        micros=7,
    )


def scatter_stack(stack, natural):
    shards, height, _ = natural.shape
    wide = D // shards
    if natural.shape[2] > 3 * wide:
        natural[:, :, 3 * wide :] = jnp.zeros((shards, height, natural.shape[2] - 3 * wide), BF)
    for d in range(shards):
        for m in range(3 * height // RANK):
            piece = stack[m * RANK : (m + 1) * RANK, d * wide : (d + 1) * wide]
            natural[d, m // 3 * RANK : (m // 3 + 1) * RANK, m % 3 * wide : (m % 3 + 1) * wide] = piece


def token_kernel(meta, keep, near, far, middle, out_grad, adapters, cat, gi_up, context, gi_o, attn, inner_o, *refs):
    pieces, layer_ref, natural, stack = refs
    total = keep[0].astype(F32) + near[0].astype(F32) + far[...].astype(F32)
    inner_d = total[:, D : D + RANK].astype(BF)
    mlp = total[:, :D] + dot_nt(inner_d, adapters[:, LEAVE_D : LEAVE_D + RANK])
    layer_ref[...] = (middle[...] + mlp).astype(BF)
    width = pieces.shape[0]
    stack[:width] = pieces[...]
    pairs = ((gi_o[...], context[...]), (gi_up[...], cat[:, :D]), (inner_o[...], attn[...]), (inner_d, out_grad[...]))
    for i, (left, right) in enumerate(pairs):
        stack[width + i * RANK : width + (i + 1) * RANK] = dot_tn(left, right).astype(BF)
    scatter_stack(stack, natural)


def token_grads(meta, *args, shards):
    block = (4 * RANK, padded(3 * D // shards))
    rows = args[3].shape[0]
    return call(
        token_kernel,
        "token_adapter_grads",
        [shape(rows, D), shape(shards, *block)],
        (meta, *args),
        [SMEM] + [VMEM] * len(args),
        scratch=[pltpu.VMEM((12 * RANK, D), BF)],
        micros=4,
    )


def sum_pieces(moved, heads):
    rows = moved.shape[1] - RANK

    def kernel(moved, heads, out):
        out[:RANK] = jnp.sum(moved[:, rows:, :].astype(F32), axis=0).astype(BF)
        out[RANK:] = heads[...]

    return call(kernel, "sum_adapter_grads", [shape(2 * RANK, heads.shape[1])], (moved, heads), [VMEM] * 2)[0]


def assemble_columns(meta, pieces):
    arrays = [p[0] for p in pieces]
    steps = [p[1:] for p in pieces]
    count = len(arrays)
    wide, columns = arrays[0].shape

    def kernel(meta, *refs):
        place_pieces(meta, refs[:count], steps, refs[count], refs[count + 1])

    out = call(
        kernel,
        "assemble_columns",
        [shape(count - 1, wide, columns)],
        (meta, *arrays),
        [SMEM] + [ANY] * count,
        scratch=[pltpu.SemaphoreType.DMA((count,))],
        micros=3,
    )[0]
    return out.reshape(D, columns)


def input_kernel(meta, moved, w0, w1, w2, w3, adapters, late, hidden, grad_ref, after, out_ref, joined, kinds, *, wide):
    shards, slot = moved.shape[0], moved.shape[2]
    rows = hidden.shape[0]
    count = shards // GROUP
    for s in range(shards):
        for kind in range(3):
            kinds[kind, :, s * wide : (s + 1) * wide] = moved[s, :rows, kind * wide : (kind + 1) * wide]
    for k in range(GROUP):
        for j in range(count):
            start = (k * count + j) * slot
            joined[:, start : start + slot] = moved[(meta[PART] ^ k) * count + j, :rows]
    gis = []
    for kind in range(3):
        lanes = slice(LEAVE_QKV + kind * RANK, LEAVE_QKV + (kind + 1) * RANK)
        gis.append(dot(kinds[kind], late[:, lanes]))
    gi = jnp.concatenate(gis, axis=1).astype(BF)
    grad = dot_nt(gi, adapters[:, ENTER_QKV : ENTER_QKV + 3 * RANK])
    span = count * slot
    for k, w in enumerate((w0, w1, w2, w3)):
        grad = grad + dot_nt(joined[:, k * span : (k + 1) * span], w[...])
    first, inverse = norm_parts(hidden[...].astype(F32))
    out_ref[...] = (grad_ref[...] + norm_back(grad, first, inverse)).astype(BF)


def input_back(meta, moved, weights, adapters, ff, hidden, grad_middle, after, shards):
    rows = hidden.shape[0]
    wide = D // shards

    def kernel(*refs):
        input_kernel(*refs, wide=wide)

    return call(
        kernel,
        "input_backward",
        [shape(rows, D)],
        (meta, moved, *weights, adapters, ff, hidden, grad_middle, after),
        [SMEM]
        + [pl.BlockSpec(x.shape, lambda i, n=x.ndim: (0,) * n) for x in (moved, *weights, adapters)]
        + [feed_spec(0, LATE)]
        + [pl.BlockSpec(x.shape, lambda i: (0, 0)) for x in (hidden, grad_middle)]
        + [ANY],
        out_specs=[pl.BlockSpec((rows, D), lambda i: (0, 0))],
        scratch=[pltpu.VMEM((rows, shards * moved.shape[2]), BF), pltpu.VMEM((3, rows, D), BF)],
        micros=9,
        grid=(1,),
    )[0]


def spread_tokens_kernel(part, *refs, reps, wide):
    sets, blocks, (ao, bo, au, bu, ad, bd) = refs[:reps], refs[reps : 2 * reps], refs[2 * reps :]
    this = pl.program_id(0)
    flags = [jnp.where(sets[k][0] == this, 1.0, 0.0) for k in range(reps)]

    def one(value, m):
        row, lane = m // 3 * RANK, m % 3 * wide
        return value[row : row + RANK, lane : lane + wide]

    own = 0.0
    quarters = [0.0] * GROUP
    for k in range(reps):
        block = blocks[k][...].astype(F32)
        own = own + flags[k] * block[2 * RANK :]
        for j in range(GROUP):
            pair = jnp.concatenate([one(block, j), one(block, GROUP + j)], axis=0)
            quarters[k % GROUP] = quarters[k % GROUP] + flags[k ^ j] * pair
    ordered = by_part(part[0], quarters)
    ad[0] = jnp.concatenate([q[:RANK] for q in ordered], axis=1)
    bu[0] = jnp.concatenate([q[RANK:] for q in ordered], axis=1)
    for i, ref in enumerate((ao, au, bo, bd)):
        ref[0] = one(own, 2 + i)


def spread_heads_kernel(*refs, reps, wide):
    sets, blocks, outs = refs[:reps], refs[reps : 2 * reps], refs[2 * reps + 1 :]
    this = pl.program_id(0)
    own = 0.0
    for k in range(reps):
        own = own + jnp.where(sets[k][0] == this, 1.0, 0.0) * blocks[k][...].astype(F32)
    for kind in range(3):
        lanes = slice(kind * wide, (kind + 1) * wide)
        outs[2 * kind][0] = own[:RANK, lanes]
        outs[2 * kind + 1][0] = own[RANK:, lanes]


def spread(kernel, name, ins, scalars, blocks, kinds, micros, rest=0):
    outs = call(
        kernel,
        name,
        [shape(SETS, *k, dtype=F32) for k in kinds],
        ins,
        [SMEM] * scalars + [pl.BlockSpec(b.shape, lambda e: (0, 0)) for b in blocks] + [ANY] * rest,
        out_specs=[pl.BlockSpec((1, *k), lambda e: (e, 0, 0)) for k in kinds],
        micros=micros,
        grid=(SETS,),
    )
    return [jnp.transpose(o, (0, 2, 1)) if i % 2 == 0 else o for i, o in enumerate(outs)]


def spread_tokens(part, sets, blocks, wide):
    reps = len(blocks)
    narrow, broad = (RANK, wide), (RANK, GROUP * wide)

    def kernel(*refs):
        spread_tokens_kernel(*refs, reps=reps, wide=wide)

    kinds = [narrow] * 3 + [broad, broad, narrow]
    return spread(kernel, "spread_token_grads", (part, *sets, *blocks), 1 + reps, blocks, kinds, 5)


def spread_heads(sets, blocks, after, wide):
    reps = len(blocks)

    def kernel(*refs):
        spread_heads_kernel(*refs, reps=reps, wide=wide)

    return spread(kernel, "spread_head_grads", (*sets, *blocks, after), reps, blocks, [(RANK, wide)] * 6, 4, rest=1)


def body(
    hidden,
    out_grad,
    clip_lengths,
    adapter_index,
    w_query,
    w_key,
    w_value,
    w_output,
    w_up,
    w_down,
    a_query,
    b_query,
    a_key,
    b_key,
    a_value,
    b_value,
    a_output,
    b_output,
    a_up,
    b_up,
    a_down,
    b_down,
):
    shards = lax.axis_size("shard")
    reps = lax.axis_size("rep")
    wide = D // shards
    shard = lax.axis_index("shard")
    rep = lax.axis_index("rep")
    part = rep % GROUP

    def mate(value, flip):
        return lax.ppermute(value, "rep", [(i, i ^ flip) for i in range(reps)])

    def across(value):
        return lax.all_to_all(value, "shard", split_axis=0, concat_axis=0, tiled=True)

    def turned(table):
        return jnp.transpose(table, (0, 2, 1))

    def group_gather(value):
        other = mate(value, 2)
        return [value, mate(value, 1), other, mate(other, 1)]

    place = jnp.where(shard % 2 == 0, shard // 2, shards - 1 - shard // 2)
    meta = jnp.stack([shard, part, clip_lengths[0], rep & 1, place]).astype(jnp.int32)
    part_only = part[None].astype(jnp.int32)
    sets = [adapter_index] + [mate(adapter_index, flip) for flip in range(1, reps)]
    enters = [turned(t) for t in (a_query, a_key, a_value)]
    leaves = [b_query, b_key, b_value]

    narrow = enters + [turned(a_output), turned(a_up), b_output, b_down]
    bundle = pack_first(adapter_index, meta, hidden, w_output, narrow)
    cols, halves = pack_columns(meta, (w_query, w_key, w_value), bundle, shards)
    feed = pack_feed(sets[:GROUP], part_only, w_up, w_down, leaves, turned(a_down), b_up, bundle, shards)
    cols = across(cols)
    held = {}

    def between(k, arrivals):
        if k == 1:
            return lax.optimization_barrier((*arrivals, halves, feed))[:2]
        if k == 2:
            below, above, held["cols"] = lax.optimization_barrier((*arrivals, cols))
            return below, above
        if k == shards // 2 - 1:
            below, above, held["feed"] = lax.optimization_barrier((*arrivals, feed))
            return below, above
        return lax.optimization_barrier(arrivals)

    pieces = ring_pieces(bundle, shards, between)
    cols = held["cols"]
    cols_mate = mate(cols, 1)
    grads_out = group_gather(out_grad)

    first, qkv, inner_qkv, adapters, out_quarter = project_qkv(meta, adapter_index, cols, cols_mate, pieces, leaves)
    stage = {}

    def down_between(k, arrivals):
        if k == 1:
            below, above, stage["qkv"] = lax.optimization_barrier((*arrivals, qkv))
            stage["out_weight"] = assemble_output(meta, group_gather(out_quarter))
            packed, stage["ctx"], stage["lse"] = attend(stage["qkv"], shards)
            stage["packed"] = packed
            return below, above
        if k == 2:
            below, above, stage["moved"] = lax.optimization_barrier((*arrivals, across(stage["packed"])))
            return below, above
        return lax.optimization_barrier(arrivals)

    feed_pieces = ring_pieces(held["feed"], shards, down_between)
    qkv, ctx, lse, out_weight = stage["qkv"], stage["ctx"], stage["lse"], stage["out_weight"]
    context, middle, cat, inner_o = project_output(stage["moved"], out_weight, adapters, hidden, out_grad)
    halves, last = lax.optimization_barrier((halves, feed_pieces[-1][0]))
    feed_pieces[-1] = (last, *feed_pieces[-1][1:])

    other = mate(cat, 2)
    done = {}

    def near_sum(keep, give):
        near = mate(give, 1)
        return near, (keep[1].astype(F32) + near[1].astype(F32)).astype(BF)

    def columns_between(k, arrivals):
        if k == 1:
            grad_act, done["weight"] = down_back(meta, feed_pieces, grads_out)
            below, above, grad_act, far_cat = lax.optimization_barrier((*arrivals, grad_act, other))
            done["cats"] = [cat, mate(cat, 1), far_cat, mate(far_cat, 1)]
            done["up"] = up_both(meta, feed_pieces, grad_act, done["cats"])
            return below, above
        if k == 2:
            act, pre, keep, give, late = done["up"]
            below, above, give = lax.optimization_barrier((*arrivals, give))
            near, far = near_sum(keep, give)
            far = mate(far, 2)
            keep_d, give_d, pieces_d = down_forward(done["weight"], late, act, pre, done["cats"])
            give_d, far = lax.optimization_barrier((give_d, far))
            done["second"] = keep, near, far, late, keep_d, give_d, pieces_d
            return below, above
        if k == 3:
            keep, near, far, late, keep_d, give_d, pieces_d = done["second"]
            below, above, give_d = lax.optimization_barrier((*arrivals, give_d))
            near_d, far_d = near_sum(keep_d, give_d)
            done["third"] = near_d, mate(far_d, 2)
            return below, above
        return lax.optimization_barrier(arrivals)

    column_pieces = ring_pieces(halves, shards, columns_between)
    keep, near, far, late, keep_d, give_d, pieces_d = done["second"]
    near_d, far_d = done["third"]
    grad_middle, dctx, attn, gi_up, gi_o = middle_back(
        keep, near, far, middle, out_grad, out_weight, adapters, shards
    )
    arrived = [p[0] for p in column_pieces[-2:]]
    dctx, *arrived = lax.optimization_barrier((dctx, *arrived))
    column_pieces[-2:] = [(v, *p[1:]) for v, p in zip(arrived, column_pieces[-2:])]
    qkv_quarter = assemble_columns(meta, column_pieces)
    dctx_moved = across(dctx)
    layer_out, token_pieces = token_grads(
        meta, keep_d, near_d, far_d, middle, out_grad, adapters, cat, gi_up, context, gi_o, attn, inner_o, pieces_d,
        shards=shards,
    )
    early = across(token_pieces)
    qkv_quarter, token_pieces = lax.optimization_barrier((qkv_quarter, token_pieces))
    qkv_weights = group_gather(qkv_quarter)
    lse_rows = lse.reshape(lse.shape[0], 1, lse.shape[1])
    dqkv, head_out = attend_back(
        adapter_index, qkv, dctx_moved, ctx, lse_rows, first, inner_qkv, leaves, token_pieces, shards
    )
    dqkv, early = lax.optimization_barrier((dqkv, early))
    dqkv_moved = across(dqkv)

    def over_reps(value):
        return [value] + [mate(value, flip) for flip in range(1, reps)]

    early = jnp.sum(early.astype(F32), axis=0).astype(BF)
    token_outs = spread_tokens(part_only, sets, over_reps(early), wide)
    summed = sum_pieces(dqkv_moved, head_out)
    input_grad = input_back(
        meta, dqkv_moved, qkv_weights, adapters, late, hidden, grad_middle, token_outs[1], shards
    )
    outs = spread_heads(sets, over_reps(summed), input_grad, wide) + token_outs
    return (layer_out, input_grad, *outs)


def solution(mesh):
    rows = P("shard", None)
    enter = P(None, "shard", None)
    leave = P(None, None, "shard")
    tokens = P(("rep", "shard"), None)
    return jax.shard_map(
        body,
        mesh=mesh,
        in_specs=(tokens, tokens, P("rep"), P("rep")) + (rows,) * 6 + (enter, leave) * 6,
        out_specs=(tokens, tokens) + (enter, leave) * 6,
        check_vma=False,
    )
```

```python
import jax
import jax.numpy as jnp
from jax import lax
from jax.experimental import pallas as pl
from jax.experimental.pallas import tpu as pltpu
from jax.sharding import PartitionSpec as P

D = 1280
FF = 5120
HEADS = 16
HEAD = 80
LANES = 128
RANK = 16
SETS = 8
GROUP = 4
FOLD = 4
CHUNK = 256
BLOCK_Q = 384
TAIL = D + LANES
RATE = 1.15e9

EPSILON = 1e-05
NEGATIVE = -1e30
LOG2E = 1.4426950408889634
SCALE = HEAD ** (-0.5)
ONE_LANE = HEAD
MASK_LANE = HEAD + 1

BF = jnp.bfloat16
F32 = jnp.float32

QUARTER = D // GROUP
ENTER_QKV = 0
ENTER_O = 48
ENTER_U = 64
LEAVE_O = 80
LEAVE_D = 96
FIRST = 128
BESIDE = 512
BUNDLE = D + BESIDE

ENTER_D = 0
LEAVE_U = 64
LEAVE_QKV = 128
LATE = 256

SHARD, PART, LENGTH, CORE, RING = range(5)

VMEM = pl.BlockSpec(memory_space=pltpu.VMEM)
SMEM = pl.BlockSpec(memory_space=pltpu.SMEM)
ANY = pl.BlockSpec(memory_space=pl.ANY)


def dot(left, right):
    return jnp.dot(left, right, preferred_element_type=F32)


def dot_nt(left, right):
    return lax.dot_general(left, right, (((1,), (1,)), ((), ())), preferred_element_type=F32)


def dot_tn(left, right):
    return lax.dot_general(left, right, (((0,), (0,)), ((), ())), preferred_element_type=F32)


def norm_parts(values):
    center = values - jnp.mean(values, axis=-1, keepdims=True)
    spread = jnp.mean(center * center, axis=-1, keepdims=True)
    inverse = lax.rsqrt(spread + EPSILON)
    return center * inverse, inverse


def norm_back(grad, normal, inverse):
    average = jnp.mean(grad, axis=-1, keepdims=True)
    along = jnp.mean(grad * normal, axis=-1, keepdims=True)
    return inverse * (grad - average - normal * along)


def cost(micros):
    return pl.CostEstimate(flops=int(micros * RATE), transcendentals=0, bytes_accessed=0)


def call(kernel, name, outs, ins, specs, out_specs=None, scratch=(), micros=1.0, **rest):
    return pl.pallas_call(
        kernel,
        out_shape=outs,
        in_specs=specs,
        out_specs=[VMEM] * len(outs) if out_specs is None else out_specs,
        scratch_shapes=list(scratch),
        compiler_params=pltpu.CompilerParams(vmem_limit_bytes=56 << 20),
        cost_estimate=cost(micros),
        name=name,
        **rest,
    )(*ins)


def shape(*dims, dtype=BF):
    return jax.ShapeDtypeStruct(dims, dtype)


def padded(size):
    return -(-size // LANES) * LANES


def column_blocks(wq, wk, wv, shards):
    wide = D // shards
    pad = jnp.zeros((wide, padded(3 * wide) - 3 * wide), BF)
    for s in range(shards):
        at = slice(s * wide, (s + 1) * wide)
        yield s, jnp.concatenate([wq[:, at], wk[:, at], wv[:, at], pad], axis=1)


def pack_columns(meta, weights, after, shards):
    wide = D // shards
    slot = padded(3 * wide)
    count = shards // GROUP

    def kernel(meta, wq, wk, wv, after, cols, quarter):
        for s, block in column_blocks(wq, wk, wv, shards):
            cols[s] = jnp.where(meta[CORE] == 0, block[:, : slot // 2], block[:, slot // 2 :])

            @pl.when(meta[PART] == s // count)
            def _():
                quarter[:, s % count * slot : (s % count + 1) * slot] = block

    outs = [shape(shards, wide, slot // 2), shape(wide, count * slot)]
    return call(kernel, "pack_columns", outs, (meta, *weights, after), [SMEM] + [VMEM] * 3 + [ANY], micros=3)


def unit(size):
    row = lax.broadcasted_iota(jnp.int32, (size, size), 0)
    col = lax.broadcasted_iota(jnp.int32, (size, size), 1)
    return (row == col).astype(BF)


def pack_first(chosen, meta, hidden, w_output, narrow):
    rows = hidden.shape[0]
    wide = narrow[0].shape[2]

    def kernel(chosen, meta, hidden, w_output, *refs):
        out = refs[-1]
        eye = unit(wide)
        out[:, :D] = hidden[...]
        out[:, D:] = jnp.zeros((rows, BESIDE), BF)
        for i, ref in enumerate(refs[:-1]):
            out[:wide, D + i * RANK : D + (i + 1) * RANK] = dot_nt(eye, ref[...]).astype(BF)
        for p in range(GROUP):

            @pl.when(meta[PART] == p)
            def _():
                out[:wide, D + FIRST : D + FIRST + QUARTER] = w_output[:, p * QUARTER : (p + 1) * QUARTER]

    return pl.pallas_call(
        kernel,
        out_shape=shape(rows, BUNDLE),
        grid_spec=pltpu.PrefetchScalarGridSpec(
            num_scalar_prefetch=1,
            grid=(1,),
            in_specs=[SMEM, pl.BlockSpec((rows, D), lambda i, m: (0, 0)), pl.BlockSpec((wide, D), lambda i, m: (0, 0))]
            + [pl.BlockSpec((None, RANK, wide), lambda i, m: (m[0], 0, 0))] * len(narrow),
            out_specs=pl.BlockSpec((rows, BUNDLE), lambda i, m: (0, 0)),
        ),
        cost_estimate=cost(3),
        name="pack_first",
    )(chosen, meta, hidden, w_output, *narrow)


def feed_kernel(*refs, wide, shards):
    part = refs[GROUP][0]
    (w_up, w_down), maps, (out, sem) = refs[GROUP + 1 : GROUP + 3], refs[GROUP + 3 : -3], refs[-2:]
    narrow, downs, ups = maps[:3], maps[3:7], maps[7:11]
    copy = pltpu.make_async_copy(w_down.at[part], out.at[:, pl.ds(D, D)], sem)
    copy.start()
    eye = unit(wide)
    beside = 2 * D
    for i, ref in enumerate(narrow):
        start = beside + LEAVE_QKV + i * RANK
        out[:, start : start + RANK] = dot_nt(eye, ref[...]).astype(BF)
    end = beside + LEAVE_QKV + 3 * RANK
    out[:, end:] = jnp.zeros((wide, 2 * D + LATE - end), BF)
    for p in range(GROUP):

        @pl.when(part == p)
        def _():
            at = slice(p * wide, (p + 1) * wide)
            for i, ref in enumerate(downs):
                start = beside + ENTER_D + i * RANK
                out[:, start : start + RANK] = dot_nt(eye, ref[:, at]).astype(BF)
            for i, ref in enumerate(ups):
                start = beside + LEAVE_U + i * RANK
                out[:, start : start + RANK] = dot_nt(eye, ref[:, at]).astype(BF)
            for s in range(shards):
                start = (s * GROUP + p) * wide
                out[:, s * wide : (s + 1) * wide] = w_up[:, start : start + wide]

    copy.wait()


def pack_feed(sets, part, w_up, w_down, narrow, a_down, b_up, after, shards):
    wide = D // shards
    ff_wide = GROUP * wide
    width = 2 * D + LATE

    def at(k):
        return lambda i, *m: (m[k][0], 0, 0)

    specs = (
        [pl.BlockSpec((wide, FF), lambda i, *m: (0, 0)), ANY]
        + [pl.BlockSpec((None, RANK, wide), at(0))] * 3
        + [pl.BlockSpec((None, RANK, ff_wide), at(k)) for k in range(GROUP)] * 2
        + [ANY]
    )

    def kernel(*refs):
        feed_kernel(*refs, wide=wide, shards=shards)

    return pl.pallas_call(
        kernel,
        out_shape=shape(wide, width),
        grid_spec=pltpu.PrefetchScalarGridSpec(
            num_scalar_prefetch=GROUP + 1,
            grid=(1,),
            in_specs=specs,
            out_specs=pl.BlockSpec((wide, width), lambda i, *m: (0, 0)),
            scratch_shapes=[pltpu.SemaphoreType.DMA],
        ),
        cost_estimate=cost(5),
        name="pack_feed",
    )(*sets, part, w_up, w_down.reshape(GROUP, wide, D), *narrow, *[a_down] * GROUP, *[b_up] * GROUP, after)


def ring_shard(place, shards):
    return jnp.where(place < shards // 2, 2 * place, 2 * (shards - 1 - place) + 1)


def ring_pieces(value, shards, between):
    places = [2 * i if i < shards // 2 else 2 * (shards - 1 - i) + 1 for i in range(shards)]
    onward = [(places[i], places[(i + 1) % shards]) for i in range(shards)]
    back = [(b, a) for a, b in onward]
    half = value.shape[0] // 2
    pieces = [(value, 0, 0)]
    below, above = value, value
    for k in range(1, shards // 2):
        below = lax.ppermute(below, "shard", onward)
        above = lax.ppermute(above, "shard", back)
        below, above = between(k, (below, above))
        pieces += [(below, -k, 0), (above, k, 0)]
    far = shards // 2
    pieces.append((lax.ppermute(below[:half], "shard", onward), far, 0))
    pieces.append((lax.ppermute(above[half:], "shard", back), far, half))
    return pieces


def piece_shard(meta, step, shards):
    return ring_shard((meta[RING] + step + shards) % shards, shards)


def place_pieces(meta, pieces, steps, target, sems, column=None):
    shards = target.shape[0]
    copies = []
    for i, (ref, (step, start)) in enumerate(zip(pieces, steps)):
        if column is not None:
            ref = ref.at[:, pl.ds(column, target.shape[2])]
        block = target.at[piece_shard(meta, step, shards), pl.ds(start, ref.shape[0])]
        copies.append(pltpu.make_async_copy(ref, block, sems.at[i]))
    for copy in copies:
        copy.start()
    for copy in copies:
        copy.wait()


def qkv_kernel(meta, w_mine, w_mate, *refs, shards, steps):
    count = len(steps)
    pieces, leaves = refs[:count], refs[count : count + 3]
    first_ref, qkv_ref, inner_ref, enter, quarter, hid, sems = refs[-7:]
    wide = D // shards
    heads_here = HEADS // shards
    slot = padded(3 * wide)
    side = meta[CORE]
    rows = hid.shape[1]
    place_pieces(meta, pieces, steps, hid, sems)
    for s in range(shards):
        enter[s * wide : (s + 1) * wide, :] = hid[s, :wide, D : D + FIRST]
        quarter[s * wide : (s + 1) * wide, :] = hid[s, :wide, D + FIRST : D + FIRST + QUARTER]
    lane = lax.broadcasted_iota(jnp.int32, (rows, LANES - HEAD), 1)
    spot = lax.broadcasted_iota(jnp.int32, (rows, LANES - HEAD), 0)

    def step(s, carry):
        at = pl.ds(pl.multiple_of(s * rows, 64), rows)
        first = norm_parts(hid[s, :, :D].astype(F32))[0].astype(BF)
        first_ref[at, :] = first
        inner = dot(first, enter[:, : 3 * RANK]).astype(BF)
        inner_ref[at, :] = inner
        y_mine = dot(first, w_mine[...].reshape(D, slot // 2))
        y_mate = dot(first, w_mate[...].reshape(D, slot // 2))
        lo = jnp.where(side == 0, y_mine, y_mate)
        hi = jnp.where(side == 0, y_mate, y_mine)
        y = jnp.concatenate([lo, hi], axis=1)
        hidden_key = jnp.where((spot + s * rows < meta[LENGTH]) | (lane != MASK_LANE - HEAD), 0.0, NEGATIVE)
        for kind in range(3):
            lanes = slice(kind * RANK, (kind + 1) * RANK)
            out = y[:, kind * wide : (kind + 1) * wide] + dot(inner[:, lanes], leaves[kind][...])
            if kind == 0:
                tail = jnp.where(lane == MASK_LANE - HEAD, 1.0, 0.0)
            elif kind == 1:
                tail = hidden_key
            else:
                tail = jnp.where(lane == ONE_LANE - HEAD, 1.0, 0.0)
            for h in range(heads_here):
                base = (kind * heads_here + h) * LANES
                head = jnp.concatenate([out[:, h * HEAD : (h + 1) * HEAD], tail], axis=1)
                qkv_ref[at, base : base + LANES] = head.astype(BF)
        return carry

    lax.fori_loop(0, shards, step, 0, unroll=True)


def project_qkv(meta, chosen, w_mine, w_mate, pieces, leaves):
    shards = len(pieces) - 1
    steps = [p[1:] for p in pieces]
    rows = pieces[0][0].shape[0]
    seq_len = rows * shards
    lanes = HEADS // shards * LANES
    wide = D // shards
    weight = pl.BlockSpec(w_mine.shape, lambda i, c: (0, 0, 0))
    outs = [
        shape(seq_len, D),
        shape(seq_len, 3 * lanes),
        shape(seq_len, 3 * RANK),
        shape(D, FIRST),
        shape(D, QUARTER),
    ]

    def kernel(chosen, *refs):
        qkv_kernel(*refs, shards=shards, steps=steps)

    return pl.pallas_call(
        kernel,
        out_shape=outs,
        grid_spec=pltpu.PrefetchScalarGridSpec(
            num_scalar_prefetch=1,
            grid=(1,),
            in_specs=[SMEM, weight, weight]
            + [ANY] * len(pieces)
            + [pl.BlockSpec((None, RANK, wide), lambda i, c: (c[0], 0, 0))] * 3,
            out_specs=[pl.BlockSpec(o.shape, lambda i, c: (0, 0)) for o in outs],
            scratch_shapes=[
                pltpu.VMEM((shards, rows, BUNDLE), BF),
                pltpu.SemaphoreType.DMA((len(pieces),)),
            ],
        ),
        compiler_params=pltpu.CompilerParams(vmem_limit_bytes=56 << 20),
        cost_estimate=cost(14),
        name="project_qkv",
    )(chosen, meta, w_mine, w_mate, *[p[0] for p in pieces], *leaves)


def forward_kernel(qkv_ref, packed_ref, ctx_ref, lse_ref, *, heads_here, wide, block):
    shards, part, _ = packed_ref.shape
    seq_len = ctx_ref.shape[0]
    factor = SCALE * LOG2E

    def step(i, carry):
        at = pl.ds(pl.multiple_of(i * block, 64), block)
        for h in range(heads_here):
            queries = qkv_ref[at, h * LANES : (h + 1) * LANES]
            keys = qkv_ref[:, (heads_here + h) * LANES : (heads_here + h + 1) * LANES]
            values = qkv_ref[:, (2 * heads_here + h) * LANES : (2 * heads_here + h + 1) * LANES]
            scores = dot_nt(queries, keys)
            highest = jnp.max(scores, axis=1, keepdims=True)
            weights = jnp.exp2((scores - highest) * factor).astype(BF)
            portion = dot(weights, values)
            total = portion[:, ONE_LANE : ONE_LANE + 1]
            ctx_ref[at, h * LANES : (h + 1) * LANES] = (portion / total).astype(BF)
            lse_ref[h, at, :] = highest * factor + jnp.log2(total)
        return carry

    lax.fori_loop(0, seq_len // block, step, 0, unroll=True)
    for h in range(heads_here):
        for d in range(shards):
            for g in range(FOLD):
                start = g * wide + h * HEAD
                row = (d * FOLD + g) * part
                packed_ref[d, :, start : start + HEAD] = ctx_ref[row : row + part, h * LANES : h * LANES + HEAD]


def attend(qkv, shards):
    seq_len = qkv.shape[0]
    rows = seq_len // shards
    heads_here = HEADS // shards
    lanes = heads_here * LANES
    wide = D // shards

    def kernel(*refs):
        forward_kernel(*refs, heads_here=heads_here, wide=wide, block=BLOCK_Q)

    return call(
        kernel,
        "attention_forward",
        [
            shape(shards, rows // FOLD, FOLD * wide),
            shape(seq_len, lanes),
            shape(heads_here, seq_len, 1, dtype=F32),
        ],
        (qkv,),
        [VMEM],
        micros=12,
    )


def backward_kernel(
    qkv_ref, moved_ref, ctx_ref, lse_ref, first, inner, leave_q, leave_k, leave_v, out_ref, heads_ref, douts, delta, acc, turned,
    *, heads_here, wide, block
):
    shards = moved_ref.shape[0]
    seq_len = qkv_ref.shape[0]
    rows = seq_len // shards
    part = rows // FOLD
    slot = out_ref.shape[2]
    for d in range(shards):
        for g in range(FOLD):
            base = d * rows + g * part
            for h in range(heads_here):
                start = g * wide + h * HEAD
                piece = moved_ref[d, :, start : start + HEAD]
                douts[base : base + part, h * LANES : h * LANES + HEAD] = piece
    for h in range(heads_here):
        douts[:, h * LANES + HEAD : (h + 1) * LANES] = jnp.zeros((seq_len, LANES - HEAD), BF)
    ones = jnp.ones((8, LANES), F32)
    if slot > 3 * wide:
        out_ref[:, :, 3 * wide :] = jnp.zeros((shards, rows + RANK, slot - 3 * wide), BF)
    for h in range(heads_here):
        lanes = slice(h * LANES, (h + 1) * LANES)
        product = douts[:, lanes].astype(F32) * ctx_ref[:, lanes].astype(F32)
        delta[...] = lax.dot_general(
            ones, product, (((1,), (1,)), ((), ())), precision=lax.Precision.HIGHEST, preferred_element_type=F32
        )
        queries = qkv_ref[:, lanes]
        grads = douts[:, lanes]

        def step(i, carry):
            at = pl.ds(pl.multiple_of(i * block, block), block)
            keys = qkv_ref[at, (heads_here + h) * LANES : (heads_here + h + 1) * LANES]
            values = qkv_ref[at, (2 * heads_here + h) * LANES : (2 * heads_here + h + 1) * LANES]
            scores = dot_nt(keys, queries)
            weights = jnp.exp2(scores * (SCALE * LOG2E) - lse_ref[h])
            grad_weights = dot_nt(values, grads)
            grad_scores = (weights * (grad_weights - delta[0:1, :])).astype(BF)
            acc[2, at, :] = dot(weights.astype(BF), grads)
            acc[1, at, :] = dot(grad_scores, queries) * SCALE
            moved = dot_tn(keys, grad_scores)

            @pl.when(i == 0)
            def _():
                turned[...] = moved

            @pl.when(i > 0)
            def _():
                turned[...] += moved

            return carry

        lax.fori_loop(0, seq_len // block, step, 0, unroll=True)
        acc[0] = jnp.transpose(turned[...])
        for kind in range(3):
            start = kind * wide + h * HEAD
            for d in range(shards):
                piece = acc[kind, d * rows : (d + 1) * rows, :HEAD]
                if kind == 0:
                    piece = piece * SCALE
                out_ref[d, :rows, start : start + HEAD] = piece.astype(BF)
    heads_ref[...] = jnp.zeros_like(heads_ref)
    parts = []
    for kind, leave in enumerate((leave_q, leave_k, leave_v)):
        grad = out_ref[:, :rows, kind * wide : (kind + 1) * wide].reshape(seq_len, wide)
        lanes = slice(kind * RANK, (kind + 1) * RANK)
        parts.append(dot_nt(grad, leave[...]))
        heads_ref[:, kind * wide : (kind + 1) * wide] = dot_tn(inner[:, lanes], grad).astype(BF)
    entered = dot_tn(jnp.concatenate(parts, axis=1).astype(BF), first[...]).astype(BF)
    for kind in range(3):
        for d in range(shards):
            piece = entered[kind * RANK : (kind + 1) * RANK, d * wide : (d + 1) * wide]
            out_ref[d, rows:, kind * wide : (kind + 1) * wide] = piece


def attend_back(chosen, qkv, moved, ctx, lse, first, inner, leaves, after, shards):
    seq_len = qkv.shape[0]
    rows = seq_len // shards
    heads_here = HEADS // shards
    lanes = heads_here * LANES
    wide = D // shards
    outs = [shape(shards, rows + RANK, padded(3 * wide)), shape(RANK, padded(3 * wide))]

    def kernel(chosen, *refs):
        backward_kernel(*refs[:9], *refs[10:], heads_here=heads_here, wide=wide, block=512)

    def whole(array):
        return pl.BlockSpec(array.shape, lambda i, c: (0,) * len(array.shape))

    return pl.pallas_call(
        kernel,
        out_shape=outs,
        grid_spec=pltpu.PrefetchScalarGridSpec(
            num_scalar_prefetch=1,
            grid=(1,),
            in_specs=[whole(x) for x in (qkv, moved, ctx, lse, first, inner)]
            + [pl.BlockSpec((None, RANK, wide), lambda i, c: (c[0], 0, 0))] * 3
            + [ANY],
            out_specs=[whole(o) for o in outs],
            scratch_shapes=[
                pltpu.VMEM((seq_len, lanes), BF),
                pltpu.VMEM((8, seq_len), F32),
                pltpu.VMEM((3, seq_len, LANES), F32),
                pltpu.VMEM((LANES, seq_len), F32),
            ],
        ),
        compiler_params=pltpu.CompilerParams(vmem_limit_bytes=56 << 20),
        cost_estimate=cost(24),
        name="attention_backward",
    )(chosen, qkv, moved, ctx, lse, first, inner, *leaves, after)


def by_part(part, values):
    ordered = []
    for b in range(GROUP):
        total = values[0]
        for k in range(1, GROUP):
            total = jnp.where((part ^ k) == b, values[k], total)
        ordered.append(total)
    return ordered


def assemble_output(meta, weights):
    def kernel(meta, *refs):
        out = refs[-1]
        for k in range(GROUP):
            for b in range(GROUP):

                @pl.when((meta[PART] ^ k) == b)
                def _():
                    out[:, b * QUARTER : (b + 1) * QUARTER] = refs[k][...]

    return call(kernel, "assemble_output", [shape(D, D)], (meta, *weights), [SMEM] + [VMEM] * GROUP, micros=3)[0]


def output_kernel(moved, weight, adapters, hidden, out_grad, *refs):
    ctx_ref, middle_ref, cat_ref, inner_ref = refs[-4:]
    shards, part, lanes = moved.shape
    wide = lanes // FOLD
    for s in range(shards):
        for g in range(FOLD):
            ctx_ref[g * part : (g + 1) * part, s * wide : (s + 1) * wide] = moved[s, :, g * wide : (g + 1) * wide]
    context = ctx_ref[...]
    inner = dot(context, adapters[:, ENTER_O : ENTER_O + RANK]).astype(BF)
    inner_ref[...] = inner
    branch = dot(context, weight[...]) + dot_nt(inner, adapters[:, LEAVE_O : LEAVE_O + RANK])
    middle = hidden[...].astype(F32) + branch
    middle_ref[...] = middle
    second = norm_parts(middle)[0].astype(BF)
    cat_ref[:, :D] = second
    inner_u = dot(second, adapters[:, ENTER_U : ENTER_U + RANK])
    gi_down = dot(out_grad[...], adapters[:, LEAVE_D : LEAVE_D + RANK])
    empty = jnp.zeros((second.shape[0], LANES - 2 * RANK), F32)
    cat_ref[:, D:] = jnp.concatenate([inner_u, gi_down, empty], axis=1).astype(BF)


def project_output(moved, weight, adapters, hidden, out_grad):
    rows = hidden.shape[0]
    return call(
        output_kernel,
        "project_output",
        [shape(rows, D), shape(rows, D, dtype=F32), shape(rows, TAIL), shape(rows, RANK)],
        (moved, weight, adapters, hidden, out_grad),
        [VMEM] * 5,
        micros=6,
    )


def feed_spec(index, width=D):
    return pl.BlockSpec((D, width), lambda i: (0, index))


def down_back(meta, pieces, grads):
    arrays = [p[0] for p in pieces]
    steps = [p[1:] for p in pieces]
    count = len(arrays)
    shards, wide = count - 1, arrays[0].shape[0]
    rows = grads[0].shape[0]

    def kernel(meta, *refs):
        given, (out, weight, joined, sems) = refs[count : count + GROUP], refs[count + GROUP :]
        for k in range(GROUP):
            joined[k * rows : (k + 1) * rows] = given[k][...]
        place_pieces(meta, refs[:count], steps, weight, sems, D)
        for n in range(D // CHUNK):
            at = slice(n * CHUNK, (n + 1) * CHUNK)
            out[:, at] = dot_nt(joined[...], weight[...].reshape(D, D)[at, :]).astype(BF)

    return call(
        kernel,
        "down_backward",
        [shape(GROUP * rows, D), shape(shards, wide, D)],
        (meta, *arrays, *grads),
        [SMEM] + [ANY] * count + [VMEM] * GROUP,
        scratch=[pltpu.VMEM((GROUP * rows, D), BF), pltpu.SemaphoreType.DMA((count,))],
        micros=7,
    )


def up_kernel(meta, *refs, steps):
    count = len(steps)
    pieces, grad_ref, cats = refs[:count], refs[count], refs[count + 1 : count + 1 + GROUP]
    act_ref, pre_ref, keep, send, late, joined, w_ref, late_ref, sems, late_sems = refs[count + 1 + GROUP :]
    rows = cats[0].shape[0]
    place_pieces(meta, pieces, steps, w_ref, sems, 0)
    place_pieces(meta, pieces, steps, late_ref, late_sems, 2 * D)
    late[...] = late_ref[...].reshape(D, LATE)
    adapters = late
    for k in range(GROUP):
        joined[k * rows : (k + 1) * rows] = cats[k][:, :D]

    def step(n, carry):
        lanes = pl.ds(pl.multiple_of(n * CHUNK, CHUNK), CHUNK)
        weight = w_ref[:, :, lanes].reshape(D, CHUNK)
        pre = dot(joined[...], weight)
        extra, extra_grad = [], []
        for k in range(GROUP):
            leave = adapters[lanes, LEAVE_U + k * RANK : LEAVE_U + (k + 1) * RANK]
            enter = adapters[lanes, ENTER_D + k * RANK : ENTER_D + (k + 1) * RANK]
            extra.append(dot_nt(cats[k][:, D : D + RANK], leave))
            extra_grad.append(dot_nt(cats[k][:, D + RANK : D + 2 * RANK], enter))
        pre = pre + jnp.concatenate(extra, axis=0)
        grad = grad_ref[:, lanes].astype(F32) + jnp.concatenate(extra_grad, axis=0)
        cumulative = 0.5 * (1.0 + lax.erf(pre * (0.5**0.5)))
        density = jnp.exp2(pre * pre * (-0.5 * LOG2E)) * 0.3989422804014327
        act_ref[:, lanes] = (pre * cumulative).astype(BF)
        pre_ref[:, lanes] = (grad * (cumulative + pre * density)).astype(BF)
        return carry

    lax.fori_loop(0, D // CHUNK, step, 0, unroll=True)
    for n in range(D // CHUNK):
        lanes = slice(n * CHUNK, (n + 1) * CHUNK)
        total = dot_nt(pre_ref[...], w_ref[...].reshape(D, D)[lanes, :]).astype(BF)
        for k in range(GROUP):
            target = send if k % 2 else keep
            target[k // 2, :, lanes] = total[k * rows : (k + 1) * rows]
    for k in range(GROUP):
        target = send if k % 2 else keep
        at = slice(k * rows, (k + 1) * rows)
        gi = dot(pre_ref[at], adapters[:, LEAVE_U + k * RANK : LEAVE_U + (k + 1) * RANK])
        empty = jnp.zeros((rows, LANES - RANK), F32)
        target[k // 2, :, D:] = jnp.concatenate([gi, empty], axis=1).astype(BF)


def up_both(meta, pieces, grad, cats):
    arrays = [p[0] for p in pieces]
    steps = [p[1:] for p in pieces]
    count = len(arrays)
    shards, wide = count - 1, arrays[0].shape[0]
    rows = cats[0].shape[0]
    total = GROUP * rows
    bundle = shape(2, rows, TAIL)

    def kernel(*refs):
        up_kernel(*refs, steps=steps)

    return call(
        kernel,
        "up_forward_backward",
        [shape(total, D), shape(total, D), bundle, bundle, shape(D, LATE)],
        (meta, *arrays, grad, *cats),
        [SMEM] + [ANY] * count + [VMEM] * (1 + GROUP),
        scratch=[
            pltpu.VMEM((total, D), BF),
            pltpu.VMEM((shards, wide, D), BF),
            pltpu.VMEM((shards, wide, LATE), BF),
            pltpu.SemaphoreType.DMA((count,)),
            pltpu.SemaphoreType.DMA((count,)),
        ],
        micros=12,
    )


def down_kernel(w_ref, act_ref, pre_ref, adapters, *refs):
    tails, (keep, send, pieces) = refs[:GROUP], refs[GROUP:]
    rows = tails[0].shape[0]
    for n in range(D // CHUNK):
        lanes = slice(n * CHUNK, (n + 1) * CHUNK)
        total = dot(act_ref[...], w_ref[:, :, lanes].reshape(D, CHUNK)).astype(BF)
        for k in range(GROUP):
            target = send if k % 2 else keep
            target[k // 2, :, lanes] = total[k * rows : (k + 1) * rows]
    for k in range(GROUP):
        target = send if k % 2 else keep
        at = slice(k * rows, (k + 1) * rows)
        act = act_ref[at]
        inner = dot(act, adapters[:, ENTER_D + k * RANK : ENTER_D + (k + 1) * RANK])
        empty = jnp.zeros((rows, LANES - RANK), F32)
        target[k // 2, :, D:] = jnp.concatenate([inner, empty], axis=1).astype(BF)
        pieces[k * RANK : (k + 1) * RANK] = dot_tn(tails[k][:, RANK : 2 * RANK], act).astype(BF)
        start = (GROUP + k) * RANK
        pieces[start : start + RANK] = dot_tn(tails[k][:, :RANK], pre_ref[at]).astype(BF)


def down_forward(weight, ff, act, pre, cats):
    rows = cats[0].shape[0]
    total = GROUP * rows
    bundle = shape(2, rows, TAIL)
    return call(
        down_kernel,
        "down_forward",
        [bundle, bundle, shape(2 * GROUP * RANK, D)],
        (weight, act, pre, ff, *cats),
        [
            pl.BlockSpec(weight.shape, lambda i: (0, 0, 0)),
            pl.BlockSpec((total, D), lambda i: (0, 0)),
            pl.BlockSpec((total, D), lambda i: (0, 0)),
            feed_spec(0, LATE),
        ]
        + [pl.BlockSpec((rows, LANES), lambda i: (0, D // LANES))] * GROUP,
        out_specs=[pl.BlockSpec((2, rows, TAIL), lambda i: (0, 0, 0))] * 2
        + [pl.BlockSpec((2 * GROUP * RANK, D), lambda i: (0, 0))],
        micros=9,
        grid=(1,),
    )


def middle_kernel(
    keep, near, far, middle, out_grad, weight, adapters, grad_ref, packed, attn_ref, gi_up_ref, gi_o_ref
):
    shards, part, lanes = packed.shape
    wide = lanes // FOLD
    total = keep[0].astype(F32) + near[0].astype(F32) + far[...].astype(F32)
    gi_up = total[:, D : D + RANK].astype(BF)
    gi_up_ref[...] = gi_up
    grad = total[:, :D] + dot_nt(gi_up, adapters[:, ENTER_U : ENTER_U + RANK])
    second, inverse = norm_parts(middle[...])
    grad_middle = out_grad[...].astype(F32) + norm_back(grad, second, inverse)
    grad_ref[...] = grad_middle
    attn = grad_middle.astype(BF)
    attn_ref[...] = attn
    gi_o = dot(attn, adapters[:, LEAVE_O : LEAVE_O + RANK]).astype(BF)
    gi_o_ref[...] = gi_o
    context = dot_nt(attn, weight[...])
    context = (context + dot_nt(gi_o, adapters[:, ENTER_O : ENTER_O + RANK])).astype(BF)
    for s in range(shards):
        for g in range(FOLD):
            packed[s, :, g * wide : (g + 1) * wide] = context[g * part : (g + 1) * part, s * wide : (s + 1) * wide]


def middle_back(keep, near, far, middle, out_grad, weight, adapters, shards):
    rows = middle.shape[0]
    wide = D // shards
    return call(
        middle_kernel,
        "middle_backward",
        [
            shape(rows, D, dtype=F32),
            shape(shards, rows // FOLD, FOLD * wide),
            shape(rows, D),
            shape(rows, RANK),
            shape(rows, RANK),
        ],
        (keep, near, far, middle, out_grad, weight, adapters),
        [VMEM] * 7,
        micros=7,
    )


def scatter_stack(stack, natural):
    shards, height, _ = natural.shape
    wide = D // shards
    if natural.shape[2] > 3 * wide:
        natural[:, :, 3 * wide :] = jnp.zeros((shards, height, natural.shape[2] - 3 * wide), BF)
    for d in range(shards):
        for m in range(3 * height // RANK):
            piece = stack[m * RANK : (m + 1) * RANK, d * wide : (d + 1) * wide]
            natural[d, m // 3 * RANK : (m // 3 + 1) * RANK, m % 3 * wide : (m % 3 + 1) * wide] = piece


def token_kernel(meta, keep, near, far, middle, out_grad, adapters, cat, gi_up, context, gi_o, attn, inner_o, *refs):
    pieces, layer_ref, natural, stack = refs
    total = keep[0].astype(F32) + near[0].astype(F32) + far[...].astype(F32)
    inner_d = total[:, D : D + RANK].astype(BF)
    mlp = total[:, :D] + dot_nt(inner_d, adapters[:, LEAVE_D : LEAVE_D + RANK])
    layer_ref[...] = (middle[...] + mlp).astype(BF)
    width = pieces.shape[0]
    stack[:width] = pieces[...]
    pairs = ((gi_o[...], context[...]), (gi_up[...], cat[:, :D]), (inner_o[...], attn[...]), (inner_d, out_grad[...]))
    for i, (left, right) in enumerate(pairs):
        stack[width + i * RANK : width + (i + 1) * RANK] = dot_tn(left, right).astype(BF)
    scatter_stack(stack, natural)


def token_grads(meta, *args, shards):
    block = (4 * RANK, padded(3 * D // shards))
    rows = args[3].shape[0]
    return call(
        token_kernel,
        "token_adapter_grads",
        [shape(rows, D), shape(shards, *block)],
        (meta, *args),
        [SMEM] + [VMEM] * len(args),
        scratch=[pltpu.VMEM((12 * RANK, D), BF)],
        micros=4,
    )


def sum_pieces(moved, heads):
    rows = moved.shape[1] - RANK

    def kernel(moved, heads, out):
        out[:RANK] = jnp.sum(moved[:, rows:, :].astype(F32), axis=0).astype(BF)
        out[RANK:] = heads[...]

    return call(kernel, "sum_adapter_grads", [shape(2 * RANK, heads.shape[1])], (moved, heads), [VMEM] * 2)[0]


def assemble_columns(meta, pieces):
    arrays = [p[0] for p in pieces]
    steps = [p[1:] for p in pieces]
    count = len(arrays)
    wide, columns = arrays[0].shape

    def kernel(meta, *refs):
        place_pieces(meta, refs[:count], steps, refs[count], refs[count + 1])

    out = call(
        kernel,
        "assemble_columns",
        [shape(count - 1, wide, columns)],
        (meta, *arrays),
        [SMEM] + [ANY] * count,
        scratch=[pltpu.SemaphoreType.DMA((count,))],
        micros=3,
    )[0]
    return out.reshape(D, columns)


def input_kernel(meta, moved, w0, w1, w2, w3, adapters, late, hidden, grad_ref, after, out_ref, joined, kinds, *, wide):
    shards, slot = moved.shape[0], moved.shape[2]
    rows = hidden.shape[0]
    count = shards // GROUP
    for s in range(shards):
        for kind in range(3):
            kinds[kind, :, s * wide : (s + 1) * wide] = moved[s, :rows, kind * wide : (kind + 1) * wide]
    for k in range(GROUP):
        for j in range(count):
            start = (k * count + j) * slot
            joined[:, start : start + slot] = moved[(meta[PART] ^ k) * count + j, :rows]
    gis = []
    for kind in range(3):
        lanes = slice(LEAVE_QKV + kind * RANK, LEAVE_QKV + (kind + 1) * RANK)
        gis.append(dot(kinds[kind], late[:, lanes]))
    gi = jnp.concatenate(gis, axis=1).astype(BF)
    grad = dot_nt(gi, adapters[:, ENTER_QKV : ENTER_QKV + 3 * RANK])
    span = count * slot
    for k, w in enumerate((w0, w1, w2, w3)):
        grad = grad + dot_nt(joined[:, k * span : (k + 1) * span], w[...])
    first, inverse = norm_parts(hidden[...].astype(F32))
    out_ref[...] = (grad_ref[...] + norm_back(grad, first, inverse)).astype(BF)


def input_back(meta, moved, weights, adapters, ff, hidden, grad_middle, after, shards):
    rows = hidden.shape[0]
    wide = D // shards

    def kernel(*refs):
        input_kernel(*refs, wide=wide)

    return call(
        kernel,
        "input_backward",
        [shape(rows, D)],
        (meta, moved, *weights, adapters, ff, hidden, grad_middle, after),
        [SMEM]
        + [pl.BlockSpec(x.shape, lambda i, n=x.ndim: (0,) * n) for x in (moved, *weights, adapters)]
        + [feed_spec(0, LATE)]
        + [pl.BlockSpec(x.shape, lambda i: (0, 0)) for x in (hidden, grad_middle)]
        + [ANY],
        out_specs=[pl.BlockSpec((rows, D), lambda i: (0, 0))],
        scratch=[pltpu.VMEM((rows, shards * moved.shape[2]), BF), pltpu.VMEM((3, rows, D), BF)],
        micros=9,
        grid=(1,),
    )[0]


def spread_tokens_kernel(part, *refs, reps, wide):
    sets, blocks, (ao, bo, au, bu, ad, bd) = refs[:reps], refs[reps : 2 * reps], refs[2 * reps :]
    this = pl.program_id(0)
    flags = [jnp.where(sets[k][0] == this, 1.0, 0.0) for k in range(reps)]

    def one(value, m):
        row, lane = m // 3 * RANK, m % 3 * wide
        return value[row : row + RANK, lane : lane + wide]

    own = 0.0
    quarters = [0.0] * GROUP
    for k in range(reps):
        block = blocks[k][...].astype(F32)
        own = own + flags[k] * block[2 * RANK :]
        for j in range(GROUP):
            pair = jnp.concatenate([one(block, j), one(block, GROUP + j)], axis=0)
            quarters[k % GROUP] = quarters[k % GROUP] + flags[k ^ j] * pair
    ordered = by_part(part[0], quarters)
    ad[0] = jnp.concatenate([q[:RANK] for q in ordered], axis=1)
    bu[0] = jnp.concatenate([q[RANK:] for q in ordered], axis=1)
    for i, ref in enumerate((ao, au, bo, bd)):
        ref[0] = one(own, 2 + i)


def spread_heads_kernel(*refs, reps, wide):
    sets, blocks, outs = refs[:reps], refs[reps : 2 * reps], refs[2 * reps + 1 :]
    values = [block[...].astype(F32) for block in blocks]
    for this in range(SETS):
        own = 0.0
        for k in range(reps):
            own = own + jnp.where(sets[k][0] == this, 1.0, 0.0) * values[k]
        for kind in range(3):
            lanes = slice(kind * wide, (kind + 1) * wide)
            outs[2 * kind][this] = own[:RANK, lanes]
            outs[2 * kind + 1][this] = own[RANK:, lanes]


def spread(kernel, name, ins, scalars, blocks, kinds, micros, rest=0):
    outs = call(
        kernel,
        name,
        [shape(SETS, *k, dtype=F32) for k in kinds],
        ins,
        [SMEM] * scalars + [pl.BlockSpec(b.shape, lambda e: (0, 0)) for b in blocks] + [ANY] * rest,
        out_specs=[pl.BlockSpec((1, *k), lambda e: (e, 0, 0)) for k in kinds],
        micros=micros,
        grid=(SETS,),
    )
    return [jnp.transpose(o, (0, 2, 1)) if i % 2 == 0 else o for i, o in enumerate(outs)]


def spread_tokens(part, sets, blocks, wide):
    reps = len(blocks)
    narrow, broad = (RANK, wide), (RANK, GROUP * wide)

    def kernel(*refs):
        spread_tokens_kernel(*refs, reps=reps, wide=wide)

    kinds = [narrow] * 3 + [broad, broad, narrow]
    return spread(kernel, "spread_token_grads", (part, *sets, *blocks), 1 + reps, blocks, kinds, 5)


def spread_heads(sets, blocks, after, wide):
    reps = len(blocks)

    def kernel(*refs):
        spread_heads_kernel(*refs, reps=reps, wide=wide)

    outs = call(
        kernel,
        "spread_head_grads",
        [shape(SETS, RANK, wide, dtype=F32)] * 6,
        (*sets, *blocks, after),
        [SMEM] * reps + [VMEM] * reps + [ANY],
        micros=2,
    )
    return [jnp.transpose(o, (0, 2, 1)) if i % 2 == 0 else o for i, o in enumerate(outs)]


def body(
    hidden,
    out_grad,
    clip_lengths,
    adapter_index,
    w_query,
    w_key,
    w_value,
    w_output,
    w_up,
    w_down,
    a_query,
    b_query,
    a_key,
    b_key,
    a_value,
    b_value,
    a_output,
    b_output,
    a_up,
    b_up,
    a_down,
    b_down,
):
    shards = lax.axis_size("shard")
    reps = lax.axis_size("rep")
    wide = D // shards
    shard = lax.axis_index("shard")
    rep = lax.axis_index("rep")
    part = rep % GROUP

    def mate(value, flip):
        return lax.ppermute(value, "rep", [(i, i ^ flip) for i in range(reps)])

    def across(value):
        return lax.all_to_all(value, "shard", split_axis=0, concat_axis=0, tiled=True)

    def turned(table):
        return jnp.transpose(table, (0, 2, 1))

    def group_gather(value):
        other = mate(value, 2)
        return [value, mate(value, 1), other, mate(other, 1)]

    place = jnp.where(shard % 2 == 0, shard // 2, shards - 1 - shard // 2)
    meta = jnp.stack([shard, part, clip_lengths[0], rep & 1, place]).astype(jnp.int32)
    part_only = part[None].astype(jnp.int32)
    sets = [adapter_index] + [mate(adapter_index, flip) for flip in range(1, reps)]
    enters = [turned(t) for t in (a_query, a_key, a_value)]
    leaves = [b_query, b_key, b_value]

    narrow = enters + [turned(a_output), turned(a_up), b_output, b_down]
    bundle = pack_first(adapter_index, meta, hidden, w_output, narrow)
    cols, halves = pack_columns(meta, (w_query, w_key, w_value), bundle, shards)
    feed = pack_feed(sets[:GROUP], part_only, w_up, w_down, leaves, turned(a_down), b_up, bundle, shards)
    cols = across(cols)
    held = {}

    def between(k, arrivals):
        if k == 1:
            return lax.optimization_barrier((*arrivals, halves, feed))[:2]
        if k == 2:
            below, above, held["cols"] = lax.optimization_barrier((*arrivals, cols))
            return below, above
        if k == shards // 2 - 1:
            below, above, held["feed"] = lax.optimization_barrier((*arrivals, feed))
            return below, above
        return lax.optimization_barrier(arrivals)

    pieces = ring_pieces(bundle, shards, between)
    cols = held["cols"]
    cols_mate = mate(cols, 1)
    grads_out = group_gather(out_grad)

    first, qkv, inner_qkv, adapters, out_quarter = project_qkv(meta, adapter_index, cols, cols_mate, pieces, leaves)
    stage = {}

    def down_between(k, arrivals):
        if k == 1:
            below, above, stage["qkv"] = lax.optimization_barrier((*arrivals, qkv))
            stage["out_weight"] = assemble_output(meta, group_gather(out_quarter))
            packed, stage["ctx"], stage["lse"] = attend(stage["qkv"], shards)
            stage["packed"] = packed
            return below, above
        if k == 2:
            below, above, stage["moved"] = lax.optimization_barrier((*arrivals, across(stage["packed"])))
            return below, above
        return lax.optimization_barrier(arrivals)

    feed_pieces = ring_pieces(held["feed"], shards, down_between)
    qkv, ctx, lse, out_weight = stage["qkv"], stage["ctx"], stage["lse"], stage["out_weight"]
    context, middle, cat, inner_o = project_output(stage["moved"], out_weight, adapters, hidden, out_grad)
    halves, last = lax.optimization_barrier((halves, feed_pieces[-1][0]))
    feed_pieces[-1] = (last, *feed_pieces[-1][1:])

    other = mate(cat, 2)
    done = {}

    def near_sum(keep, give):
        near = mate(give, 1)
        return near, (keep[1].astype(F32) + near[1].astype(F32)).astype(BF)

    def columns_between(k, arrivals):
        if k == 1:
            grad_act, done["weight"] = down_back(meta, feed_pieces, grads_out)
            below, above, grad_act, far_cat = lax.optimization_barrier((*arrivals, grad_act, other))
            done["cats"] = [cat, mate(cat, 1), far_cat, mate(far_cat, 1)]
            done["up"] = up_both(meta, feed_pieces, grad_act, done["cats"])
            return below, above
        if k == 2:
            act, pre, keep, give, late = done["up"]
            below, above, give = lax.optimization_barrier((*arrivals, give))
            near, far = near_sum(keep, give)
            far = mate(far, 2)
            keep_d, give_d, pieces_d = down_forward(done["weight"], late, act, pre, done["cats"])
            give_d, far = lax.optimization_barrier((give_d, far))
            done["second"] = keep, near, far, late, keep_d, give_d, pieces_d
            return below, above
        if k == 3:
            keep, near, far, late, keep_d, give_d, pieces_d = done["second"]
            below, above, give_d = lax.optimization_barrier((*arrivals, give_d))
            near_d, far_d = near_sum(keep_d, give_d)
            done["third"] = near_d, mate(far_d, 2)
            return below, above
        return lax.optimization_barrier(arrivals)

    column_pieces = ring_pieces(halves, shards, columns_between)
    keep, near, far, late, keep_d, give_d, pieces_d = done["second"]
    near_d, far_d = done["third"]
    grad_middle, dctx, attn, gi_up, gi_o = middle_back(
        keep, near, far, middle, out_grad, out_weight, adapters, shards
    )
    arrived = [p[0] for p in column_pieces[-2:]]
    dctx, *arrived = lax.optimization_barrier((dctx, *arrived))
    column_pieces[-2:] = [(v, *p[1:]) for v, p in zip(arrived, column_pieces[-2:])]
    qkv_quarter = assemble_columns(meta, column_pieces)
    dctx_moved = across(dctx)
    layer_out, token_pieces = token_grads(
        meta, keep_d, near_d, far_d, middle, out_grad, adapters, cat, gi_up, context, gi_o, attn, inner_o, pieces_d,
        shards=shards,
    )
    early = across(token_pieces)
    qkv_quarter, token_pieces = lax.optimization_barrier((qkv_quarter, token_pieces))
    qkv_weights = group_gather(qkv_quarter)
    lse_rows = lse.reshape(lse.shape[0], 1, lse.shape[1])
    dqkv, head_out = attend_back(
        adapter_index, qkv, dctx_moved, ctx, lse_rows, first, inner_qkv, leaves, token_pieces, shards
    )
    dqkv, early = lax.optimization_barrier((dqkv, early))
    dqkv_moved = across(dqkv)

    def over_reps(value):
        return [value] + [mate(value, flip) for flip in range(1, reps)]

    early = jnp.sum(early.astype(F32), axis=0).astype(BF)
    token_outs = spread_tokens(part_only, sets, over_reps(early), wide)
    summed = sum_pieces(dqkv_moved, head_out)
    input_grad = input_back(
        meta, dqkv_moved, qkv_weights, adapters, late, hidden, grad_middle, token_outs[1], shards
    )
    outs = spread_heads(sets, over_reps(summed), input_grad, wide) + token_outs
    return (layer_out, input_grad, *outs)


def solution(mesh):
    rows = P("shard", None)
    enter = P(None, "shard", None)
    leave = P(None, None, "shard")
    tokens = P(("rep", "shard"), None)
    return jax.shard_map(
        body,
        mesh=mesh,
        in_specs=(tokens, tokens, P("rep"), P("rep")) + (rows,) * 6 + (enter, leave) * 6,
        out_specs=(tokens, tokens) + (enter, leave) * 6,
        check_vma=False,
    )
```
